32 devices in a mesh: seq: 8 (over z, x), tensor: 4 (over y, core).
Axes of the slice: x: 2, y: 2, z: 4, core: 2. Of those that a mesh axis runs over, the one named last changes fastest.
Arguments:
- latents: bfloat16 [4096, 1024], P('seq')
- sources: bfloat16 [8192, 1024], P('seq'), may hold values from -6 to 6
- source_index: int32 [32, 256], P('seq'), may hold values from 0 to 8191, as said below
- block_clip: int32 [32], replicated, may hold values from 0 to 2, as said below
- clip_frames: int32 [3], replicated, may hold values from 1 to 2, as said below
- norm_src: float32 [1024], replicated, may hold values from 0.5 to 1.5
- norm_cross: float32 [1024], replicated, may hold values from 0.5 to 1.5
- norm_self: float32 [1024], replicated, may hold values from 0.5 to 1.5
- norm_mlp: float32 [1024], replicated, may hold values from 0.5 to 1.5
- cross_q: bfloat16 [1024, 1024], P(None, 'tensor'), may hold values from -0.1875 to 0.1875
- cross_k: bfloat16 [1024, 1024], P(None, 'tensor'), may hold values from -0.1875 to 0.1875
- cross_v: bfloat16 [1024, 1024], P(None, 'tensor'), may hold values from -0.1875 to 0.1875
- cross_o: bfloat16 [1024, 1024], P('tensor'), may hold values from -0.5 to 0.5
- self_q: bfloat16 [1024, 1024], P(None, 'tensor'), may hold values from -0.1875 to 0.1875
- self_k: bfloat16 [1024, 1024], P(None, 'tensor'), may hold values from -0.1875 to 0.1875
- self_v: bfloat16 [1024, 1024], P(None, 'tensor'), may hold values from -0.1875 to 0.1875
- self_o: bfloat16 [1024, 1024], P('tensor'), may hold values from -0.75 to 0.75
- mlp_in: bfloat16 [1024, 4096], P(None, 'tensor'), may hold values from -0.1875 to 0.1875
- mlp_out: bfloat16 [4096, 1024], P('tensor'), may hold values from -0.09375 to 0.09375
- out_grad: bfloat16 [4096, 1024], P('seq'), may hold values from -6 to 6
Outputs:
- output: bfloat16 [4096, 1024], P('seq')
- latents_grad: bfloat16 [4096, 1024], P('seq')
- sources_grad: bfloat16 [8192, 1024], P('seq')
- norm_src_grad: float32 [1024], replicated
- norm_cross_grad: float32 [1024], replicated
- norm_self_grad: float32 [1024], replicated
- norm_mlp_grad: float32 [1024], replicated
- cross_q_grad: float32 [1024, 1024], P('seq', 'tensor')
- cross_k_grad: float32 [1024, 1024], P('seq', 'tensor')
- cross_v_grad: float32 [1024, 1024], P('seq', 'tensor')
- cross_o_grad: float32 [1024, 1024], P('tensor', 'seq')
- self_q_grad: float32 [1024, 1024], P('seq', 'tensor')
- self_k_grad: float32 [1024, 1024], P('seq', 'tensor')
- self_v_grad: float32 [1024, 1024], P('seq', 'tensor')
- self_o_grad: float32 [1024, 1024], P('tensor', 'seq')
- mlp_in_grad: float32 [1024, 4096], P('seq', 'tensor')
- mlp_out_grad: float32 [4096, 1024], P('tensor', 'seq')
- penalty: float32 [], replicated
The draws below stay inside these ranges and needn't reach their ends.
Inputs may be any that keep to these rules, and one draw needn't show every extreme that they name: `clip_frames`: the entries sum to 4 and the largest is exactly 2. block_clip[b] depends only on b % 4, and clip c is named by exactly clip_frames[c] of the 4 residues. `source_index`: over the groups b with b // 4 == j the entries are a permutation of the rows j * 4 * 256 to (j + 1) * 4 * 256 - 1.
All inputs are finite; a program needn't handle non-finite values.
Results may differ from the reference program's by a relative error of at most 0.03.
Values may be sent and summed in bfloat16 or wider, within the bound.
No kernel may reach another device: no remote copies, remote signals or barrier semaphores. Data moves between devices by JAX's collectives and lax.ppermute only.
A program may use at most 128 MiB of HBM per device.

```python
import jax
import jax.numpy as jnp
from jax import lax

D = 1024
HEADS = 8
HEAD = 128
FF = 4096
GROUP = 128
SRC = 256
GROUPS_FRAME = 8
BLK_DEV = 4
BLOCKS = 32
TOKENS = 4096
SOURCES = 8192
FRAMES = 4
CLIPS = 3
MOST = 2


def draw_latents(key, part):
    row_ids = jnp.arange(TOKENS, dtype=jnp.float32)
    row_scale = 0.3 + 2.7 * row_ids / TOKENS
    base_values = jax.random.normal(key, (TOKENS, D), jnp.float32)
    return (base_values * row_scale[:, None]).astype(jnp.bfloat16)


def clip_layout(key):
    base_key = jax.random.fold_in(key, 7)
    first_key, second_key, third_key = jax.random.split(base_key, 3)
    longest = jax.random.randint(first_key, (), 0, CLIPS)
    spare_frames = FRAMES - MOST - (CLIPS - 1)
    targets = jax.random.randint(second_key, (spare_frames,), 1, CLIPS)
    ordinals = jnp.arange(CLIPS, dtype=jnp.int32)
    ordered = 1 + jnp.sum((targets[:, None] == ordinals[None, :]).astype(jnp.int32), axis=0)
    ordered = jnp.where(ordinals == 0, MOST, ordered)
    frames = ordered[(ordinals - longest) % CLIPS]
    bounds = jnp.cumsum(ordered)
    positions = jnp.arange(FRAMES, dtype=jnp.int32)
    frame_ranks = jnp.sum((bounds[None, :] <= positions[:, None]).astype(jnp.int32), axis=1)
    labels = (longest + frame_ranks) % CLIPS
    shuffled = labels[2:][jax.random.permutation(third_key, FRAMES - 2)]
    placed = jnp.concatenate([labels[:1], shuffled, labels[1:2]])
    blocks = placed[jnp.arange(BLOCKS, dtype=jnp.int32) % FRAMES]
    return (frames.astype(jnp.int32), blocks.astype(jnp.int32))


def draw_clip_frames(key, part):
    return clip_layout(key)[0]


def draw_block_clip(key, part):
    return clip_layout(key)[1]


def draw_source_index(key, part):
    pool_rows = BLK_DEV * SRC
    seq_count = BLOCKS // BLK_DEV
    seq_keys = jax.random.split(jax.random.fold_in(key, 11), seq_count)
    shuffles = jax.vmap(lambda one_key: jax.random.permutation(one_key, pool_rows))(seq_keys)
    offsets = jnp.arange(seq_count, dtype=jnp.int32)[:, None] * pool_rows
    return (shuffles + offsets).reshape(BLOCKS, SRC).astype(jnp.int32)


def steps_of(stream_key, shape, cuts, low, largest):
    def one(axis_at, parts):
        draws = jax.random.uniform(jax.random.fold_in(jax.random.fold_in(stream_key, 6), axis_at), (parts,), jnp.float32, low / len(cuts), largest / len(cuts))
        return jnp.repeat(jnp.exp(draws), shape[axis_at] // parts).reshape((-1,) + (1,) * (len(shape) - axis_at - 1))

    gain = one(*cuts[0])
    for cut in cuts[1:]:
        gain = gain * one(*cut)
    return gain


def gaussian(stream_key, shape, width, bound, pieces=(), held_as=jnp.bfloat16):
    array = jax.random.normal(stream_key, shape, jnp.float32) * width
    if len(pieces) > 0:
        array = steps_of(stream_key, shape, pieces, -0.22, 0.18) * array
    return jnp.clip(array, min=-bound, max=bound).astype(held_as)


def setup_inputs(seed: int = 0) -> dict:
    arg_keys = jax.random.split(jax.random.key(seed), 21)
    latents = draw_latents(jax.random.fold_in(arg_keys[20], 71), 0)
    sources = gaussian(arg_keys[1], (SOURCES, D), 1.0, 6.0, ((0, 8),))
    source_index = draw_source_index(jax.random.fold_in(arg_keys[20], 71), 0)
    block_clip = draw_block_clip(jax.random.fold_in(arg_keys[20], 71), 0)
    clip_frames = draw_clip_frames(jax.random.fold_in(arg_keys[20], 71), 0)
    norm_src = jnp.clip(1.0 + 0.1 * jax.random.normal(arg_keys[5], (D,), jnp.float32), 0.5, 1.5)
    norm_cross = jnp.clip(1.0 + 0.1 * jax.random.normal(arg_keys[6], (D,), jnp.float32), 0.5, 1.5)
    norm_self = jnp.clip(1.0 + 0.1 * jax.random.normal(arg_keys[7], (D,), jnp.float32), 0.5, 1.5)
    norm_mlp = jnp.clip(1.0 + 0.1 * jax.random.normal(arg_keys[8], (D,), jnp.float32), 0.5, 1.5)
    cross_q = gaussian(arg_keys[9], (D, D), D ** -0.5, 0.1875, ((1, 4),))
    cross_k = gaussian(arg_keys[10], (D, D), D ** -0.5, 0.1875, ((1, 4),))
    cross_v = gaussian(arg_keys[11], (D, D), D ** -0.5, 0.1875, ((1, 4),))
    cross_o = gaussian(arg_keys[12], (D, D), (D // 8) ** -0.5, 0.5, ((0, 4),))
    self_q = gaussian(arg_keys[13], (D, D), D ** -0.5, 0.1875, ((1, 4),))
    self_k = gaussian(arg_keys[14], (D, D), D ** -0.5, 0.1875, ((1, 4),))
    self_v = gaussian(arg_keys[15], (D, D), D ** -0.5, 0.1875, ((1, 4),))
    self_o = gaussian(arg_keys[16], (D, D), (D // 16) ** -0.5, 0.75, ((0, 4),))
    mlp_in = gaussian(arg_keys[17], (D, FF), D ** -0.5, 0.1875, ((1, 4),))
    mlp_out = gaussian(arg_keys[18], (FF, D), FF ** -0.5, 0.09375, ((0, 4),))
    out_grad = gaussian(arg_keys[19], (TOKENS, D), 1.0, 6.0, ((0, 8),))
    return {"latents": latents, "sources": sources, "source_index": source_index, "block_clip": block_clip, "clip_frames": clip_frames, "norm_src": norm_src, "norm_cross": norm_cross, "norm_self": norm_self, "norm_mlp": norm_mlp, "cross_q": cross_q, "cross_k": cross_k, "cross_v": cross_v, "cross_o": cross_o, "self_q": self_q, "self_k": self_k, "self_v": self_v, "self_o": self_o, "mlp_in": mlp_in, "mlp_out": mlp_out, "out_grad": out_grad}


epsilon = 1e-05
masked_value = -1e+30
highest = lax.Precision.HIGHEST

@jax.custom_vjp
def low(v):
    return lax.optimization_barrier(v.astype(jnp.bfloat16)).astype(jnp.float32)

@jax.custom_vjp
def low_back(v):
    return v

def low_keep(v):
    return (low(v), None)

def low_pass(kept, grad):
    return (grad,)

def back_keep(v):
    return (v, None)

def back_low(kept, grad):
    return (low(grad),)
low.defvjp(low_keep, low_pass)
low_back.defvjp(back_keep, back_low)

def layer_norm(values):
    centred = values - lax.optimization_barrier(jnp.mean(values, axis=-1, keepdims=True))
    variance = lax.optimization_barrier(jnp.mean(centred * centred, axis=-1, keepdims=True))
    return centred * lax.rsqrt(variance + epsilon)

def product(left, right):
    return jnp.dot(left, right, precision=highest)

def forward(inputs, source_rows, norm_src, norm_cross, norm_self, norm_mlp, cross_q, cross_k, cross_v, cross_o, self_q, self_k, self_v, self_o, mlp_in, mlp_out, source_index, block_clip):
    scaling = HEAD ** (-0.5)
    normed_src = low(layer_norm(source_rows) * norm_src)
    normed_one = low(layer_norm(inputs) * norm_cross)
    cross_query = low_back(low(product(normed_one, cross_q)))
    cross_key = low_back(low(product(normed_src, cross_k)))
    cross_value = low_back(low(product(normed_src, cross_v)))
    block_query = cross_query.reshape(BLOCKS, GROUP, HEADS, HEAD)
    block_key = cross_key[source_index].reshape(BLOCKS, SRC, HEADS, HEAD)
    block_value = cross_value[source_index].reshape(BLOCKS, SRC, HEADS, HEAD)
    raw_scores = jnp.einsum('bqhd,bkhd->bhqk', block_query, block_key, precision=highest)
    cross_probs = jax.nn.softmax(low_back(raw_scores) * scaling, axis=-1)
    cross_mixed = jnp.einsum('bhqk,bkhd->bqhd', low(cross_probs), block_value, precision=highest)
    cross_mixed = low_back(low(cross_mixed.reshape(TOKENS, D)))
    after_cross = inputs + low_back(product(cross_mixed, cross_o))
    normed_two = low(layer_norm(after_cross) * norm_self)
    self_query = low_back(low(product(normed_two, self_q))).reshape(TOKENS, HEADS, HEAD)
    self_key = low_back(low(product(normed_two, self_k))).reshape(TOKENS, HEADS, HEAD)
    self_value = low_back(low(product(normed_two, self_v))).reshape(TOKENS, HEADS, HEAD)
    row_clip = block_clip[jnp.arange(TOKENS, dtype=jnp.int32) // GROUP]
    query_rows = 4 * GROUP
    query_count = TOKENS // query_rows

    def attend(block_in):
        queries, query_clip = block_in
        raw_block = jnp.einsum('qhd,khd->hqk', queries, self_key, precision=highest)
        key_mask = (query_clip[:, None] == row_clip[None, :])[None]
        scaled = jnp.where(key_mask, low_back(raw_block) * scaling, masked_value)
        attn_probs = jax.nn.softmax(scaled, axis=-1)
        return jnp.einsum('hqk,khd->qhd', low(attn_probs), self_value, precision=highest)
    self_mixed = lax.map(jax.checkpoint(attend), (self_query.reshape(query_count, query_rows, HEADS, HEAD), row_clip.reshape(query_count, query_rows)))
    self_mixed = low_back(low(self_mixed.reshape(TOKENS, D)))
    after_self = after_cross + low_back(product(self_mixed, self_o))
    normed_three = low(layer_norm(after_self) * norm_mlp)
    hidden = low_back(product(normed_three, mlp_in))
    activated = low(jax.nn.gelu(hidden, approximate=False))
    return after_self + low_back(product(activated, mlp_out))

def reference(latents, sources, source_index, block_clip, clip_frames, norm_src, norm_cross, norm_self, norm_mlp, cross_q, cross_k, cross_v, cross_o, self_q, self_k, self_v, self_o, mlp_in, mlp_out, out_grad):
    floats = (latents.astype(jnp.float32), sources.astype(jnp.float32), norm_src.astype(jnp.float32), norm_cross.astype(jnp.float32), norm_self.astype(jnp.float32), norm_mlp.astype(jnp.float32), cross_q.astype(jnp.float32), cross_k.astype(jnp.float32), cross_v.astype(jnp.float32), cross_o.astype(jnp.float32), self_q.astype(jnp.float32), self_k.astype(jnp.float32), self_v.astype(jnp.float32), self_o.astype(jnp.float32), mlp_in.astype(jnp.float32), mlp_out.astype(jnp.float32))

    def run(*values):
        return forward(*values, source_index, block_clip)
    result, pullback = jax.vjp(run, *floats)
    grads = pullback(out_grad.astype(jnp.float32))
    squares = lax.optimization_barrier(jnp.mean(jnp.square(result).reshape(BLOCKS, GROUP * D), axis=1))
    block_norms = jnp.sqrt(squares + 1e-06)
    clip_ids = jnp.arange(CLIPS, dtype=jnp.int32)
    member = block_clip[None, :] == clip_ids[:, None]
    per_clip = lax.optimization_barrier(jnp.sum(jnp.where(member, block_norms[None, :], 0.0), axis=1))
    penalty = jnp.mean(per_clip / (GROUPS_FRAME * clip_frames.astype(jnp.float32)))
    return (result.astype(jnp.bfloat16), grads[0].astype(jnp.bfloat16), grads[1].astype(jnp.bfloat16), grads[2], grads[3], grads[4], grads[5], grads[6], grads[7], grads[8], grads[9], grads[10], grads[11], grads[12], grads[13], grads[14], grads[15], penalty)
```

```python
import functools

import jax
import jax.numpy as jnp
from jax import lax
from jax.experimental import pallas as pl
from jax.experimental.pallas import tpu as pltpu
from jax.sharding import PartitionSpec as P

HEAD = 128
GROUP = 128
SRC = 256
GROUPS_FRAME = 8
LOG2E = 1.4426950408889634
epsilon = 1e-05
masked_value = -1e30
bf16 = jnp.bfloat16
f32 = jnp.float32
EXTRA = 16

VMEM = pl.BlockSpec(memory_space=pltpu.VMEM)
SMEM = pl.BlockSpec(memory_space=pltpu.SMEM)


def sds(shape, dtype):
    return jax.ShapeDtypeStruct(shape, dtype)


def dot(a, b):
    return lax.dot_general(a, b, (((1,), (0,)), ((), ())), preferred_element_type=f32)


def dot_t(a, b):
    return lax.dot_general(a, b, (((1,), (1,)), ((), ())), preferred_element_type=f32)


def dot_ta(a, b):
    return lax.dot_general(a, b, (((0,), (0,)), ((), ())), preferred_element_type=f32)


def centre(values):
    centred = values - jnp.mean(values, axis=-1, keepdims=True)
    variance = jnp.mean(centred * centred, axis=-1, keepdims=True)
    inverse = lax.rsqrt(variance + epsilon)
    return centred * inverse, inverse


def call(body, outs, ins, args, name, scratch=(), grid=None, prefetch=0, flops=0, nbytes=0, trans=0):
    out_specs = [spec for ignored, spec in outs]
    out_shape = [shape for shape, ignored in outs]
    return pl.pallas_call(
        body,
        out_shape=out_shape,
        grid_spec=pltpu.PrefetchScalarGridSpec(
            num_scalar_prefetch=prefetch,
            grid=() if grid is None else grid,
            in_specs=ins,
            out_specs=out_specs,
            scratch_shapes=list(scratch),
        ),
        compiler_params=pltpu.CompilerParams(vmem_limit_bytes=56 * 2**20),
        cost_estimate=pl.CostEstimate(
            flops=int(flops), bytes_accessed=int(nbytes), transcendentals=int(trans)
        ),
        name=name,
    )(*args)


def cross_forward_body(
    core_ref, idx_ref, lat_ref, src_ref, gain_one_ref, gain_src_ref, wq_ref, wk_ref, wv_ref,
    n1_ref, ns_ref, q_ref, kvp_ref, keep_ref, send_ref, kv_s, *, steps,
):
    i = pl.program_id(0)
    width = wq_ref.shape[1]
    heads = width // HEAD
    rows_src = src_ref.shape[0]
    normed_src = (centre(src_ref[...].astype(f32))[0] * gain_src_ref[...]).astype(bf16)
    ns_ref[...] = normed_src
    row0 = pl.multiple_of(i * rows_src, rows_src)
    kv_s[pl.ds(row0, rows_src), 0:width] = dot(normed_src, wk_ref[...]).astype(bf16)
    kv_s[pl.ds(row0, rows_src), width:] = dot(normed_src, wv_ref[...]).astype(bf16)
    normed_one = (centre(lat_ref[...].astype(f32))[0] * gain_one_ref[...]).astype(bf16)
    n1_ref[...] = normed_one
    grp0 = pl.multiple_of(i * GROUP, GROUP)
    q_ref[pl.ds(grp0, GROUP), :] = dot(normed_one, wq_ref[...]).astype(bf16)

    @pl.when(i == steps - 1)
    def _():
        count = kv_s.shape[0]
        lanes = lax.broadcasted_iota(jnp.int32, (128, count), 1).astype(f32)
        for b in range(steps):
            for part in range(SRC // 128):
                row = idx_ref[b : b + 1, part * 128 : (part + 1) * 128]
                column = jnp.transpose(jnp.broadcast_to(row, (128, 128)))
                picks = jnp.where(jnp.tile(column, (1, count // 128)) == lanes, 1.0, 0.0).astype(bf16)
                r0 = b * SRC + part * 128
                kvp_ref[r0 : r0 + 128, :] = dot(picks, kv_s[...]).astype(bf16)
        for b in range(steps):
            for h in range(heads):
                cols = slice(h * HEAD, (h + 1) * HEAD)
                q = q_ref[b * GROUP : (b + 1) * GROUP, cols]
                k = kvp_ref[b * SRC : (b + 1) * SRC, cols]
                v = kvp_ref[b * SRC : (b + 1) * SRC, width + h * HEAD : width + (h + 1) * HEAD]
                s = dot_t(q, k) * (HEAD ** (-0.5) * LOG2E)
                p = jnp.exp2(s - jnp.max(s, axis=-1, keepdims=True))
                total = jnp.sum(p, axis=-1, keepdims=True)
                mixed = (dot(p.astype(bf16), v) / total).astype(bf16)
                if b < steps // 2:
                    keep_ref[b * GROUP : (b + 1) * GROUP, cols] = mixed
                else:
                    r0 = (b - steps // 2) * GROUP
                    send_ref[r0 : r0 + GROUP, cols] = mixed


def cross_forward(core, idx, latents, sources, gain_one, gain_src, wq, wk, wv):
    rows, width_d = latents.shape
    steps = rows // GROUP
    count = sources.shape[0]
    blk = count // steps
    width = wq.shape[1]
    whole = lambda shape: pl.BlockSpec(shape, lambda i, c: (0,) * len(shape))
    return call(
        functools.partial(cross_forward_body, steps=steps),
        [
            (sds((rows, width_d), bf16), pl.BlockSpec((GROUP, width_d), lambda i, c: (i, 0))),
            (sds((count, width_d), bf16), pl.BlockSpec((blk, width_d), lambda i, c: (i, 0))),
            (sds((rows, width), bf16), whole((rows, width))),
            (sds((count, 2 * width), bf16), whole((count, 2 * width))),
            (sds((rows // 2, width), bf16), whole((rows // 2, width))),
            (sds((rows // 2, width), bf16), whole((rows // 2, width))),
        ],
        [
            whole(idx.shape),
            pl.BlockSpec((GROUP, width_d), lambda i, c: ((i + c[0] * (steps // 2)) % steps, 0)),
            pl.BlockSpec((blk, width_d), lambda i, c: (i, 0)),
            whole((1, width_d)),
            whole((1, width_d)),
            whole(wq.shape),
            whole(wk.shape),
            whole(wv.shape),
        ],
        (core, idx, latents, sources, gain_one, gain_src, wq, wk, wv),
        "cross_forward",
        scratch=[pltpu.VMEM((count, 2 * width), bf16)],
        grid=(steps,),
        prefetch=1,
        flops=4e9,
        nbytes=12e6,
    )


def project_body(core_ref, *refs, parts):
    pieces, weights = refs[:parts], refs[parts : 2 * parts]
    base_ref, gain_ref, after_ref, normed_ref = refs[2 * parts :]
    sums = [dot(pieces[k][...], weights[k][...]) for k in range(parts)]
    even, odd = sums[0::2], sums[1::2]
    while len(even) > 1:
        even = [even[k] + even[k + 1] for k in range(0, len(even), 2)]
        odd = [odd[k] + odd[k + 1] for k in range(0, len(odd), 2)]
    after = base_ref[...].astype(f32) + (even[0] + odd[0])
    after_ref[...] = after
    normed_ref[...] = (centre(after)[0] * gain_ref[...]).astype(bf16)


def project(core, pieces, weights, base, gain, own_half):
    parts = len(pieces)
    half, width = pieces[0].shape
    width_d = weights[0].shape[1]
    whole = lambda shape: pl.BlockSpec(shape, lambda i, c: (0,) * len(shape))
    base_spec = (
        pl.BlockSpec((half, width_d), lambda i, c: (c[0], 0)) if own_half else whole((half, width_d))
    )
    return call(
        functools.partial(project_body, parts=parts),
        [(sds((half, width_d), f32), whole((half, width_d))), (sds((half, width_d), bf16), whole((half, width_d)))],
        [whole((half, width))] * parts
        + [whole((width, width_d))] * parts
        + [base_spec, whole((1, width_d))],
        (core, *pieces, *weights, base, gain),
        "project",
        grid=(1,),
        prefetch=1,
        flops=2 * half * width * parts * width_d,
        nbytes=5e6,
    )


def qkv_body(mine_ref, other_ref, wq_ref, wk_ref, wv_ref, q_ref, kv_ref):
    half = mine_ref.shape[0]
    width = wq_ref.shape[1]
    for part, ref in enumerate((mine_ref, other_ref)):
        rows = slice(part * half, (part + 1) * half)
        x = ref[...]
        kv_ref[rows, 0:width] = dot(x, wk_ref[...]).astype(bf16)
        kv_ref[rows, width:] = dot(x, wv_ref[...]).astype(bf16)
        q_ref[rows, :] = dot(x, wq_ref[...]).astype(bf16)


def qkv(mine, other, wq, wk, wv):
    half, width_d = mine.shape
    width = wq.shape[1]
    return call(
        qkv_body,
        [(sds((2 * half, width), bf16), VMEM), (sds((2 * half, 2 * width), bf16), VMEM)],
        [VMEM] * 5,
        (mine, other, wq, wk, wv),
        "qkv",
        flops=2 * 2 * half * width_d * 3 * width,
        nbytes=4e6,
    )


def assemble(refs, entries, dst, rows_blocks):
    for ri, base, p, k in entries:
        for j in range(rows_blocks):
            dst[p * rows_blocks + j, k * GROUP : (k + 1) * GROUP, :] = refs[ri][
                base + j * GROUP : base + (j + 1) * GROUP, :
            ]


def split_rows(rows_value):
    high = rows_value.astype(bf16)
    rest = rows_value - high.astype(f32)
    middle = rest.astype(bf16)
    low = (rest - middle.astype(f32)).astype(bf16)
    return high, middle, low


def pack_extra(row_tiles, heads, blocks, width):
    per_row = width // 128
    out = []
    for h in range(heads):
        flat = [
            jnp.concatenate(row_tiles[h][r * per_row : (r + 1) * per_row], axis=1)
            for r in range(blocks // per_row)
        ]
        rows_value = jnp.concatenate(flat, axis=0)
        out += [part.astype(f32) for part in split_rows(rows_value)]
    used = heads * 3 * (blocks // per_row)
    if used < EXTRA:
        out.append(jnp.zeros((EXTRA - used, width), f32))
    return jnp.concatenate(out, axis=0).astype(bf16)


def unpack_extra(extra, h, j, blocks, width):
    per_row = width // 128
    rows_per = blocks // per_row
    row, lane = j // per_row, (j % per_row) * 128
    parts = [
        extra[(h * 3 + t) * rows_per + row : (h * 3 + t) * rows_per + row + 1, lane : lane + 128]
        for t in range(3)
    ]
    return (parts[0] + parts[1]) + parts[2]


def attend_body(
    clip_q, clip_k, *refs, pieces, entries, heads, blocks, period,
):
    q_ref = refs[0]
    kv_refs = refs[1 : 1 + pieces]
    keep_ref, send_ref, qx_ref, lsec_ref, kv_s, m_s, l_s, acc_s, row_s, o_s = refs[1 + pieces :]
    width = heads * HEAD
    assemble(kv_refs, entries, kv_s, blocks)

    def per_block(i, carry):
        r0 = pl.multiple_of(i * GROUP, GROUP)
        m_s[...] = jnp.full(m_s.shape, masked_value, f32)
        l_s[...] = jnp.zeros(l_s.shape, f32)
        acc_s[...] = jnp.zeros(acc_s.shape, f32)

        def per_keys(g, inner):
            @pl.when(clip_q[i] == clip_k[g])
            def _():
                for h in range(heads):
                    cols = slice(h * HEAD, (h + 1) * HEAD)
                    q = q_ref[pl.ds(r0, GROUP), cols]
                    k = kv_s[g, :, cols]
                    v = kv_s[g, :, width + h * HEAD : width + (h + 1) * HEAD]
                    s = dot_t(q, k) * (HEAD ** (-0.5) * LOG2E)
                    m_old = m_s[h][:, 0:1]
                    m_new = jnp.maximum(m_old, jnp.max(s, axis=-1, keepdims=True))
                    p = jnp.exp2(s - m_new)
                    alpha = jnp.exp2(m_old - m_new)
                    l_new = l_s[h][:, 0:1] * alpha + jnp.sum(p, axis=-1, keepdims=True)
                    acc_s[h] = acc_s[h] * alpha + dot(p.astype(bf16), v)
                    m_s[h] = jnp.broadcast_to(m_new, (GROUP, 128))
                    l_s[h] = jnp.broadcast_to(l_new, (GROUP, 128))

            return inner

        lax.fori_loop(0, period, per_keys, 0)
        for h in range(heads):
            total = l_s[h]
            o_s[pl.ds(r0, GROUP), h * HEAD : (h + 1) * HEAD] = (acc_s[h] / total).astype(bf16)
            lse = m_s[h] + jnp.log2(total)
            lsec_ref[h, pl.ds(r0, GROUP), :] = lse
            row_s[h, i] = jnp.transpose(lse)[0:8]
        return carry

    lax.fori_loop(0, blocks, per_block, 0)
    half = blocks // 2 * GROUP
    keep_ref[...] = o_s[0:half, :]
    send_ref[...] = o_s[half:, :]
    rows = blocks * GROUP
    qx_ref[0:rows, :] = q_ref[...]
    tiles = [[row_s[h, j][0:1] for j in range(blocks)] for h in range(heads)]
    qx_ref[rows : rows + EXTRA, :] = pack_extra(tiles, heads, blocks, width)


def attend(clip_q, clip_k, q, kv_pieces, entries):
    rows, width = q.shape
    heads, blocks, period = width // HEAD, rows // GROUP, clip_k.shape[0]
    pieces = len(kv_pieces)
    body = functools.partial(
        attend_body, pieces=pieces, entries=entries, heads=heads, blocks=blocks, period=period
    )
    return call(
        body,
        [
            (sds((rows // 2, width), bf16), VMEM),
            (sds((rows // 2, width), bf16), VMEM),
            (sds((rows + EXTRA, width), bf16), VMEM),
            (sds((heads, rows, 128), f32), VMEM),
        ],
        [SMEM, SMEM] + [VMEM] * (1 + pieces),
        (clip_q, clip_k, q, *kv_pieces),
        "attend",
        scratch=[
            pltpu.VMEM((period, GROUPS_FRAME * GROUP, 2 * width), bf16),
            pltpu.VMEM((heads, GROUP, 128), f32),
            pltpu.VMEM((heads, GROUP, 128), f32),
            pltpu.VMEM((heads, GROUP, HEAD), f32),
            pltpu.VMEM((heads, blocks, 8, 128), f32),
            pltpu.VMEM((rows, width), bf16),
        ],
        flops=2e9,
        nbytes=7e6,
        trans=2e6,
    )


def out_back_body(mine_ref, other_ref, wo_ref, okeep_ref, osend_ref, dox_ref, dc_ref, *, heads, blocks):
    half = mine_ref.shape[0]
    rows = 2 * half
    tiles = [[] for h in range(heads)]
    for part, (ref, o_ref) in enumerate(((mine_ref, okeep_ref), (other_ref, osend_ref))):
        grad = dot_t(ref[...], wo_ref[...]).astype(bf16)
        dox_ref[part * half : (part + 1) * half, :] = grad
        product = grad.astype(f32) * o_ref[...].astype(f32)
        for h in range(heads):
            delta = jnp.sum(product[:, h * HEAD : (h + 1) * HEAD], axis=-1, keepdims=True)
            delta = jnp.broadcast_to(delta, (half, 128))
            dc_ref[h, part * half : (part + 1) * half, :] = delta
            for j in range(half // GROUP):
                tiles[h].append(jnp.transpose(delta[j * GROUP : (j + 1) * GROUP])[0:1])
    dox_ref[rows : rows + EXTRA, :] = pack_extra(tiles, heads, blocks, heads * HEAD)


def out_back(mine, other, wo, okeep, osend):
    half, width_d = mine.shape
    width = wo.shape[0]
    heads, blocks = width // HEAD, 2 * half // GROUP
    return call(
        functools.partial(out_back_body, heads=heads, blocks=blocks),
        [(sds((2 * half + EXTRA, width), bf16), VMEM), (sds((heads, 2 * half, 128), f32), VMEM)],
        [VMEM] * 5,
        (mine, other, wo, okeep, osend),
        "out_back",
        flops=2 * 2 * half * width * width_d,
        nbytes=4e6,
    )


def query_back_body(clip_q, clip_k, *refs, pieces, entries, heads, blocks, period):
    qx_ref, dox_ref, lsec_ref, dc_ref = refs[0:4]
    kv_refs = refs[4 : 4 + pieces]
    dq_ref, kv_s, acc_s = refs[4 + pieces :]
    width = heads * HEAD
    assemble(kv_refs, entries, kv_s, blocks)

    def per_block(i, carry):
        r0 = pl.multiple_of(i * GROUP, GROUP)
        acc_s[...] = jnp.zeros(acc_s.shape, f32)

        def per_keys(g, inner):
            @pl.when(clip_q[i] == clip_k[g])
            def _():
                for h in range(heads):
                    cols = slice(h * HEAD, (h + 1) * HEAD)
                    k = kv_s[g, :, cols]
                    v = kv_s[g, :, width + h * HEAD : width + (h + 1) * HEAD]
                    s = dot_t(qx_ref[pl.ds(r0, GROUP), cols], k) * (HEAD ** (-0.5) * LOG2E)
                    p = jnp.exp2(s - lsec_ref[h, pl.ds(r0, GROUP), :][:, 0:1])
                    dp = dot_t(dox_ref[pl.ds(r0, GROUP), cols], v)
                    delta = dc_ref[h, pl.ds(r0, GROUP), :][:, 0:1]
                    ds = (p * (dp - delta) * (HEAD ** (-0.5))).astype(bf16)
                    acc_s[h] = acc_s[h] + dot(ds, k)

            return inner

        lax.fori_loop(0, period, per_keys, 0)
        for h in range(heads):
            dq_ref[pl.ds(r0, GROUP), h * HEAD : (h + 1) * HEAD] = acc_s[h].astype(bf16)
        return carry

    lax.fori_loop(0, blocks, per_block, 0)


def query_back(clip_q, clip_k, qx, dox, lsec, dc, kv_pieces, entries):
    rows, width = qx.shape[0] - EXTRA, qx.shape[1]
    heads, blocks, period = width // HEAD, rows // GROUP, clip_k.shape[0]
    pieces = len(kv_pieces)
    return call(
        functools.partial(
            query_back_body, pieces=pieces, entries=entries, heads=heads, blocks=blocks, period=period
        ),
        [(sds((rows, width), bf16), VMEM)],
        [SMEM, SMEM] + [VMEM] * (4 + pieces),
        (clip_q, clip_k, qx, dox, lsec, dc, *kv_pieces),
        "query_back",
        scratch=[
            pltpu.VMEM((period, GROUPS_FRAME * GROUP, 2 * width), bf16),
            pltpu.VMEM((heads, GROUP, HEAD), f32),
        ],
        flops=2e9,
        nbytes=7e6,
        trans=2e6,
    )[0]


def key_back_body(clip_q, clip_k, *refs, pieces, entries, heads, blocks, period):
    kv_ref, dq_ref, wq_ref, wk_ref, wv_ref = refs[0:5]
    qx_refs = refs[5 : 5 + pieces]
    dox_refs = refs[5 + pieces : 5 + 2 * pieces]
    dqkv_ref, keep_ref, send_ref, q_s, do_s, lse_s, delta_s, dk_s, dv_s = refs[5 + 2 * pieces :]
    width = heads * HEAD
    rows = blocks * GROUP
    assemble(qx_refs, entries, q_s, blocks)
    assemble(dox_refs, entries, do_s, blocks)
    for ri, base, p, k in entries:
        for source, target in ((qx_refs, lse_s), (dox_refs, delta_s)):
            extra = source[ri][base + rows : base + rows + EXTRA, :].astype(f32)
            for h in range(heads):
                for j in range(blocks):
                    line = unpack_extra(extra, h, j, blocks, width)
                    target[p * blocks + j, h, :, k * GROUP : (k + 1) * GROUP] = jnp.broadcast_to(
                        line, (8, 128)
                    )
    dqkv_ref[:, 0:width] = dq_ref[...]

    def per_block(j, carry):
        r0 = pl.multiple_of(j * GROUP, GROUP)
        dk_s[...] = jnp.zeros(dk_s.shape, f32)
        dv_s[...] = jnp.zeros(dv_s.shape, f32)

        def per_queries(g, inner):
            @pl.when(clip_q[j] == clip_k[g])
            def _():
                for h in range(heads):
                    cols = slice(h * HEAD, (h + 1) * HEAD)
                    k = kv_ref[pl.ds(r0, GROUP), cols]
                    v = kv_ref[pl.ds(r0, GROUP), width + h * HEAD : width + (h + 1) * HEAD]
                    q = q_s[g, :, cols]
                    do = do_s[g, :, cols]
                    st = dot_t(k, q) * (HEAD ** (-0.5) * LOG2E)
                    pt = jnp.exp2(st - lse_s[g, h, 0:1, :])
                    dv_s[h] = dv_s[h] + dot(pt.astype(bf16), do)
                    dpt = dot_t(v, do)
                    dst = (pt * (dpt - delta_s[g, h, 0:1, :]) * (HEAD ** (-0.5))).astype(bf16)
                    dk_s[h] = dk_s[h] + dot(dst, q)

            return inner

        lax.fori_loop(0, period, per_queries, 0)
        for h in range(heads):
            dqkv_ref[pl.ds(r0, GROUP), width + h * HEAD : width + (h + 1) * HEAD] = dk_s[h].astype(bf16)
            dqkv_ref[pl.ds(r0, GROUP), 2 * width + h * HEAD : 2 * width + (h + 1) * HEAD] = dv_s[
                h
            ].astype(bf16)
        return carry

    lax.fori_loop(0, blocks, per_block, 0)
    half = rows // 2
    for part, ref in enumerate((keep_ref, send_ref)):
        r = slice(part * half, (part + 1) * half)
        total = dot_t(dqkv_ref[r, 0:width], wq_ref[...])
        total = total + dot_t(dqkv_ref[r, width : 2 * width], wk_ref[...])
        total = total + dot_t(dqkv_ref[r, 2 * width :], wv_ref[...])
        ref[...] = total.astype(bf16)


def key_back(clip_q, clip_k, kv, dq, wq, wk, wv, qx_pieces, dox_pieces, entries):
    rows, width = dq.shape
    width_d = wq.shape[0]
    heads, blocks, period = width // HEAD, rows // GROUP, clip_k.shape[0]
    pieces = len(qx_pieces)
    tall = GROUPS_FRAME * GROUP
    return call(
        functools.partial(
            key_back_body, pieces=pieces, entries=entries, heads=heads, blocks=blocks, period=period
        ),
        [
            (sds((rows, 3 * width), bf16), VMEM),
            (sds((rows // 2, width_d), bf16), VMEM),
            (sds((rows // 2, width_d), bf16), VMEM),
        ],
        [SMEM, SMEM] + [VMEM] * (5 + 2 * pieces),
        (clip_q, clip_k, kv, dq, wq, wk, wv, *qx_pieces, *dox_pieces),
        "key_back",
        scratch=[
            pltpu.VMEM((period, tall, width), bf16),
            pltpu.VMEM((period, tall, width), bf16),
            pltpu.VMEM((period, heads, 8, tall), f32),
            pltpu.VMEM((period, heads, 8, tall), f32),
            pltpu.VMEM((heads, GROUP, HEAD), f32),
            pltpu.VMEM((heads, GROUP, HEAD), f32),
        ],
        flops=4e9,
        nbytes=9e6,
        trans=2e6,
    )


def mlp_body(mine_ref, other_ref, win_ref, ag_ref, act_ref, hg_ref, keep_ref, send_ref, *, steps):
    i = pl.program_id(0)
    x = jnp.where(i < steps // 2, mine_ref[...], other_ref[...])
    units = win_ref.shape[1]
    chunk = 256
    total = None
    for n in range(units // chunk):
        cols = slice(n * chunk, (n + 1) * chunk)
        w = win_ref[:, cols]
        hidden = dot(x, w)
        cdf = 0.5 * (1.0 + lax.erf(hidden * 0.7071067811865476))
        act_ref[:, cols] = (hidden * cdf).astype(bf16)
        density = jnp.exp2(hidden * hidden * (-0.5 * LOG2E)) * 0.3989422804014327
        grad = (ag_ref[:, cols] * (cdf + hidden * density)).astype(bf16)
        hg_ref[:, cols] = grad
        term = dot_t(grad, w)
        total = term if total is None else total + term
    total = total.astype(bf16)

    @pl.when(i < steps // 2)
    def _():
        keep_ref[...] = total

    @pl.when(i >= steps // 2)
    def _():
        send_ref[...] = total


def mlp(mine, other, w_in, act_grad):
    half, width_d = mine.shape
    units = w_in.shape[1]
    steps = 2 * half // GROUP
    rows = 2 * half
    low = lambda i: (jnp.minimum(i, steps // 2 - 1), 0)
    high = lambda i: (jnp.maximum(i - steps // 2, 0), 0)
    return call(
        functools.partial(mlp_body, steps=steps),
        [
            (sds((rows, units), bf16), pl.BlockSpec((GROUP, units), lambda i: (i, 0))),
            (sds((rows, units), bf16), pl.BlockSpec((GROUP, units), lambda i: (i, 0))),
            (sds((half, width_d), bf16), pl.BlockSpec((GROUP, width_d), low)),
            (sds((half, width_d), bf16), pl.BlockSpec((GROUP, width_d), high)),
        ],
        [
            pl.BlockSpec((GROUP, width_d), low),
            pl.BlockSpec((GROUP, width_d), high),
            pl.BlockSpec((width_d, units), lambda i: (0, 0)),
            pl.BlockSpec((GROUP, units), lambda i: (i, 0)),
        ],
        (mine, other, w_in, act_grad),
        "mlp",
        grid=(steps,),
        flops=4 * rows * width_d * units,
        nbytes=9e6,
        trans=2 * rows * units,
    )


def norm_back_body(core_ref, s_ref, r_ref, v_ref, gain_ref, base_ref, after_ref, branch_ref, gg_ref):
    n = s_ref[...].astype(f32) + r_ref[...].astype(f32)
    unit, inverse = centre(v_ref[...].astype(f32))
    t = n * gain_ref[...]
    back = inverse * (
        t - jnp.mean(t, axis=-1, keepdims=True) - unit * jnp.mean(t * unit, axis=-1, keepdims=True)
    )
    after = base_ref[...].astype(f32) + back
    after_ref[...] = after
    branch_ref[...] = after.astype(bf16)
    gg_ref[...] = jnp.sum(n * unit, axis=0, keepdims=True)


def norm_back(core, s, r, v, gain, base, own_half):
    half, width_d = s.shape
    whole = lambda shape: pl.BlockSpec(shape, lambda i, c: (0,) * len(shape))
    own = pl.BlockSpec((half, width_d), lambda i, c: (c[0], 0))
    full = whole((half, width_d))
    return call(
        norm_back_body,
        [
            (sds((half, width_d), f32), full),
            (sds((half, width_d), bf16), full),
            (sds((1, width_d), f32), whole((1, width_d))),
        ],
        [full, full, full, whole((1, width_d)), own if own_half else full],
        (core, s, r, v, gain, base),
        "norm_back",
        grid=(1,),
        prefetch=1,
        flops=20 * half * width_d,
        nbytes=5e6,
    )


def final_body(core_ref, s_ref, r_ref, v_ref, gain_ref, base_ref, out_ref, *, with_base):
    n = s_ref[...].astype(f32) + r_ref[...].astype(f32)
    unit, inverse = centre(v_ref[...].astype(f32))
    t = n * gain_ref[...]
    back = inverse * (
        t - jnp.mean(t, axis=-1, keepdims=True) - unit * jnp.mean(t * unit, axis=-1, keepdims=True)
    )
    if with_base:
        back = base_ref[...] + back
    out_ref[...] = back.astype(bf16)


def final_norm(core, s, r, v, gain, base):
    half, width_d = s.shape
    steps = half // 256
    with_base = base is not None
    blk = pl.BlockSpec((256, width_d), lambda i, c: (i, 0))
    own = pl.BlockSpec((256, width_d), lambda i, c: (c[0] * steps + i, 0))
    gain_spec = pl.BlockSpec((1, width_d), lambda i, c: (0, 0))
    if base is None:
        base = gain
    return call(
        functools.partial(final_body, with_base=with_base),
        [(sds((half, width_d), bf16), blk)],
        [blk, blk, own, gain_spec, blk if with_base else gain_spec],
        (core, s, r, v, gain, base),
        "final_norm",
        grid=(steps,),
        prefetch=1,
        flops=20 * half * width_d,
        nbytes=5e6,
    )[0]


def gains_body(core_ref, keep_ref, send_ref, v_ref, out_ref, *, steps):
    i = pl.program_id(0)
    n = jnp.where(i < steps // 2, keep_ref[...], send_ref[...]).astype(f32)
    unit = centre(v_ref[...].astype(f32))[0]
    part = jnp.sum(n * unit, axis=0, keepdims=True)

    @pl.when(i == 0)
    def _():
        out_ref[...] = part

    @pl.when(i > 0)
    def _():
        out_ref[...] = out_ref[...] + part


def gains(core, keep, send, v):
    half, width_d = keep.shape
    blk = 256
    steps = 2 * half // blk
    return call(
        functools.partial(gains_body, steps=steps),
        [(sds((1, width_d), f32), pl.BlockSpec((1, width_d), lambda i, c: (0, 0)))],
        [
            pl.BlockSpec((blk, width_d), lambda i, c: (jnp.minimum(i, steps // 2 - 1), 0)),
            pl.BlockSpec((blk, width_d), lambda i, c: (jnp.maximum(i - steps // 2, 0), 0)),
            pl.BlockSpec((blk, width_d), lambda i, c: ((i + c[0] * (steps // 2)) % steps, 0)),
        ],
        (core, keep, send, v),
        "gains",
        grid=(steps,),
        prefetch=1,
        flops=20 * half * width_d,
        nbytes=8 * half * width_d,
    )[0]


def result_body(s_ref, r_ref, after_ref, out_ref, squares_ref):
    result = after_ref[...] + (s_ref[...].astype(f32) + r_ref[...].astype(f32))
    out_ref[...] = result.astype(bf16)
    for b in range(result.shape[0] // GROUP):
        rows = result[b * GROUP : (b + 1) * GROUP]
        squares_ref[b : b + 1, :] = jnp.sum(rows * rows, axis=0, keepdims=True)


def result_half(s, r, after):
    half, width_d = s.shape
    return call(
        result_body,
        [(sds((half, width_d), bf16), VMEM), (sds((half // GROUP, width_d), f32), VMEM)],
        [VMEM] * 3,
        (s, r, after),
        "result",
        flops=6 * half * width_d,
        nbytes=5e6,
    )


def cross_back_body(
    core_ref, mine_ref, other_ref, wo_ref, q_ref, kvp_ref, row_ref, wq_ref, wk_ref, wv_ref,
    dq_ref, dkv_ref, one_keep_ref, one_send_ref, src_keep_ref, src_send_ref, dkvp_s, *, blocks,
):
    width = wq_ref.shape[1]
    heads = width // HEAD
    count = kvp_ref.shape[0]
    scale = HEAD ** (-0.5)
    for b in range(blocks):
        ref = mine_ref if b < blocks // 2 else other_ref
        part = (b % (blocks // 2)) * GROUP
        grad = dot_t(ref[part : part + GROUP, :], wo_ref[...]).astype(bf16)
        for h in range(heads):
            cols = slice(h * HEAD, (h + 1) * HEAD)
            vcols = slice(width + h * HEAD, width + (h + 1) * HEAD)
            q = q_ref[b * GROUP : (b + 1) * GROUP, cols]
            k = kvp_ref[b * SRC : (b + 1) * SRC, cols]
            v = kvp_ref[b * SRC : (b + 1) * SRC, vcols]
            do = grad[:, cols]
            s = dot_t(q, k) * (scale * LOG2E)
            p = jnp.exp2(s - jnp.max(s, axis=-1, keepdims=True))
            p = p / jnp.sum(p, axis=-1, keepdims=True)
            dp = dot_t(do, v)
            delta = jnp.sum(p * dp, axis=-1, keepdims=True)
            ds = (p * (dp - delta) * scale).astype(bf16)
            dq_ref[b * GROUP : (b + 1) * GROUP, cols] = dot(ds, k).astype(bf16)
            dkvp_s[b * SRC : (b + 1) * SRC, cols] = dot_ta(ds, q).astype(bf16)
            dkvp_s[b * SRC : (b + 1) * SRC, vcols] = dot_ta(p.astype(bf16), do).astype(bf16)
        one = dot_t(dq_ref[b * GROUP : (b + 1) * GROUP, :], wq_ref[...]).astype(bf16)
        if b < blocks // 2:
            one_keep_ref[part : part + GROUP, :] = one
        else:
            one_send_ref[part : part + GROUP, :] = one
    half = count // 2
    blk = 256
    for n in range(count // blk):
        r0 = pl.multiple_of(
            jnp.where(n * blk < half, core_ref[0], 1 - core_ref[0]) * half + (n * blk) % half, blk
        )
        wanted = lax.broadcasted_iota(jnp.int32, (blk, count), 0).astype(f32) + r0.astype(f32)
        picks = jnp.where(row_ref[...] == wanted, 1.0, 0.0).astype(bf16)
        dkv = dot(picks, dkvp_s[...]).astype(bf16)
        dkv_ref[pl.ds(r0, blk), :] = dkv
        total = (dot_t(dkv[:, 0:width], wk_ref[...]) + dot_t(dkv[:, width:], wv_ref[...])).astype(bf16)
        at = (n * blk) % half
        if n * blk < half:
            src_keep_ref[at : at + blk, :] = total
        else:
            src_send_ref[at : at + blk, :] = total


def cross_back(core, mine, other, wo, q, kvp, row, wq, wk, wv):
    rows, width = q.shape
    width_d = wq.shape[0]
    count = kvp.shape[0]
    blocks = rows // GROUP
    return call(
        functools.partial(cross_back_body, blocks=blocks),
        [
            (sds((rows, width), bf16), VMEM),
            (sds((count, 2 * width), bf16), VMEM),
            (sds((rows // 2, width_d), bf16), VMEM),
            (sds((rows // 2, width_d), bf16), VMEM),
            (sds((count // 2, width_d), bf16), VMEM),
            (sds((count // 2, width_d), bf16), VMEM),
        ],
        [SMEM] + [VMEM] * 9,
        (core, mine, other, wo, q, kvp, row, wq, wk, wv),
        "cross_back",
        scratch=[pltpu.VMEM((count, 2 * width), bf16)],
        flops=4e9,
        nbytes=12e6,
    )


def xor_pairs(bit, size):
    return [(i, i ^ bit) for i in range(size)]


def tensor_swap(x, bit):
    return lax.ppermute(x, "tensor", xor_pairs(bit, lax.axis_size("tensor")))


def seq_gather(x):
    size = lax.axis_size("seq")
    if size == 8:
        ring = lambda d: [(s, ((s // 2 + d) % 4) * 2 + s % 2) for s in range(8)]
        move = lambda v, pairs: lax.ppermute(v, "seq", pairs)
        flip = xor_pairs(1, 8)
        beside = move(x, flip)
        up = move(x, ring(1))
        down = move(x, ring(-1))
        far = move(up, ring(1))
        up_beside = move(up, flip)
        down_beside = move(beside, ring(-1))
        far_beside = move(far, flip)
        return [x, beside, up, down, far, up_beside, down_beside, far_beside]
    return [lax.all_gather(x, "seq", axis=0, tiled=True)]


def gather_entries(size, rows, sets):
    if size == 8:
        return tuple((k, 0, 0, k) for k in range(8))
    return tuple((0, s * rows, s % sets, s // sets) for s in range(size))


def half_sum(keep, send):
    size = lax.axis_size("tensor")
    got = tensor_swap(send, 1)
    own = (keep.astype(f32) + got.astype(f32)).astype(bf16)
    bit = 2
    while True:
        other = tensor_swap(own, bit)
        if bit * 2 >= size:
            return own, other
        own = (own.astype(f32) + other.astype(f32)).astype(bf16)
        bit *= 2


def tensor_pieces(keep, send):
    size = lax.axis_size("tensor")
    return [keep if k == 0 else tensor_swap(send if k % 2 else keep, k) for k in range(size)]


def weight_pieces(weight):
    size = lax.axis_size("tensor")
    pieces = {0: weight}
    bit = size // 2
    while bit >= 1:
        pieces.update({k + bit: tensor_swap(v, bit) for k, v in list(pieces.items())})
        bit //= 2
    return [pieces[k] for k in range(size)]


def scatter_rows(parts):
    size = lax.axis_size("seq")
    if size != 8:
        return lax.psum_scatter(parts, "seq", scatter_dimension=0, tiled=True).astype(f32)
    index = lax.axis_index("seq")
    z, x = index // 2, index % 2
    features, columns = parts.shape
    view = parts.reshape(4, 2, features // 8, columns)
    keep = lax.dynamic_index_in_dim(view, x, 1, keepdims=False)
    send = lax.dynamic_index_in_dim(view, 1 - x, 1, keepdims=False)
    both = keep.astype(f32) + lax.ppermute(send, "seq", xor_pairs(1, 8)).astype(f32)
    short = both.astype(bf16)
    total = lax.dynamic_index_in_dim(both, z, 0, keepdims=False)
    for d in (1, 2, 3):
        pairs = [(s, ((s // 2 + d) % 4) * 2 + s % 2) for s in range(8)]
        piece = lax.dynamic_index_in_dim(short, (z + d) % 4, 0, keepdims=False)
        total = total + lax.ppermute(piece, "seq", pairs).astype(f32)
    return total


def sum_everywhere(v):
    for axis in ("tensor", "seq"):
        bit = 1
        while bit < lax.axis_size(axis):
            v = v + lax.ppermute(v, axis, xor_pairs(bit, lax.axis_size(axis)))
            bit *= 2
    return v


def local(
    latents, sources, source_index, block_clip, clip_frames, norm_src, norm_cross, norm_self, norm_mlp,
    cross_q, cross_k, cross_v, cross_o, self_q, self_k, self_v, self_o, mlp_in, mlp_out, out_grad,
):
    rows, width_d = latents.shape
    half = rows // 2
    blocks = rows // GROUP
    count = sources.shape[0]
    width = cross_q.shape[1]
    tensor_size, seq_size = lax.axis_size("tensor"), lax.axis_size("seq")
    t_index, s_index = lax.axis_index("tensor"), lax.axis_index("seq")
    core_index = t_index % 2
    core = core_index.astype(jnp.int32).reshape(1)
    period = block_clip.shape[0] // GROUPS_FRAME
    sets = period // blocks

    def own_first(v):
        first, second = v[: v.shape[0] // 2], v[v.shape[0] // 2 :]
        return jnp.where(core_index == 0, v, jnp.concatenate((second, first)))

    def in_place(mine, other):
        return jnp.where(
            core_index == 0, jnp.concatenate((mine, other)), jnp.concatenate((other, mine))
        )

    gain = lambda g: g.reshape(1, width_d)
    index = own_first((source_index - s_index * count).astype(f32))
    turned = (jnp.arange(blocks, dtype=jnp.int32) + core_index * (blocks // 2)) % blocks
    clip_q = block_clip[blocks * (s_index % sets) + turned]
    clip_k = block_clip[(blocks * jnp.arange(sets, dtype=jnp.int32)[:, None] + turned[None, :]).reshape(-1)]

    cross_o_all = weight_pieces(cross_o)
    self_o_all = weight_pieces(self_o)
    normed_one, normed_src, cross_query, cross_kv, mixed_keep, mixed_send = cross_forward(
        core, index, latents, sources, gain(norm_cross), gain(norm_src), cross_q, cross_k, cross_v
    )
    after_cross, two_mine = project(
        core, tensor_pieces(mixed_keep, mixed_send), cross_o_all, latents, gain(norm_self), True
    )
    two_other = tensor_swap(two_mine, 1)
    query, key_value = qkv(two_mine, two_other, self_q, self_k, self_v)
    kv_pieces = seq_gather(key_value)
    kv_entries = gather_entries(seq_size, rows, sets)
    out_rel = own_first(out_grad)
    act_grad = dot_t(out_rel, mlp_out)
    self_keep, self_send, query_more, lse_columns = attend(clip_q, clip_k, query, kv_pieces, kv_entries)
    after_self, three_mine = project(
        core, tensor_pieces(self_keep, self_send), self_o_all, after_cross, gain(norm_mlp), False
    )
    three_other = tensor_swap(three_mine, 1)
    activated, hidden_grad, three_keep, three_send = mlp(three_mine, three_other, mlp_in, act_grad)
    query_pieces = seq_gather(query_more)
    more_entries = gather_entries(seq_size, rows + EXTRA, sets)

    three_sum, three_got = half_sum(three_keep, three_send)
    after_self_grad, self_branch, mlp_gain = norm_back(
        core, three_sum, three_got, after_self, gain(norm_mlp), out_grad, True
    )
    self_branch_other = tensor_swap(self_branch, 1)
    mlp_part = dot(activated, mlp_out).astype(bf16)
    result_sum, result_got = half_sum(mlp_part[:half], mlp_part[half:])
    output_half, squares = result_half(result_sum, result_got, after_self)
    output = in_place(output_half, tensor_swap(output_half, 1))
    normed_three = jnp.concatenate((three_mine, three_other))
    mlp_in_out = scatter_rows(dot_ta(normed_three, hidden_grad).astype(bf16))
    mlp_out_out = scatter_rows(dot_ta(out_rel, activated).astype(bf16))

    out_more, delta_columns = out_back(self_branch, self_branch_other, self_o, self_keep, self_send)
    out_pieces = seq_gather(out_more)
    self_query_grad = query_back(
        clip_q, clip_k, query_more, out_more, lse_columns, delta_columns, kv_pieces, kv_entries
    )
    self_grads, two_keep, two_send = key_back(
        clip_q, clip_k, key_value, self_query_grad, self_q, self_k, self_v, query_pieces, out_pieces, more_entries
    )
    two_sum, two_got = half_sum(two_keep, two_send)
    after_cross_grad, cross_branch, self_gain = norm_back(
        core, two_sum, two_got, after_cross, gain(norm_self), after_self_grad, False
    )
    cross_branch_other = tensor_swap(cross_branch, 1)
    normed_two = jnp.concatenate((two_mine, two_other))
    self_branch_all = jnp.concatenate((self_branch, self_branch_other))
    self_mixed = jnp.concatenate((self_keep, self_send))
    self_out = scatter_rows(
        jnp.concatenate(
            (dot_ta(normed_two, self_grads).astype(bf16), dot_ta(self_branch_all, self_mixed).astype(bf16)),
            axis=1,
        )
    )

    cross_query_grad, cross_kv_grad, one_keep, one_send, src_keep, src_send = cross_back(
        core, cross_branch, cross_branch_other, cross_o, cross_query, cross_kv,
        index.reshape(1, -1), cross_q, cross_k, cross_v,
    )
    one_sum, one_got = half_sum(one_keep, one_send)
    src_sum, src_got = half_sum(src_keep, src_send)
    cross_gain = gains(core, one_keep, one_send, latents)
    src_gain = gains(core, src_keep, src_send, sources)
    cross_branch_all = jnp.concatenate((cross_branch, cross_branch_other))
    cross_mixed = jnp.concatenate((mixed_keep, mixed_send))
    cross_out = scatter_rows(
        jnp.concatenate(
            (
                dot_ta(normed_one, cross_query_grad).astype(bf16),
                dot_ta(normed_src, cross_kv_grad).astype(bf16),
                dot_ta(cross_branch_all, cross_mixed).astype(bf16),
            ),
            axis=1,
        )
    )
    lat_half = final_norm(core, one_sum, one_got, latents, gain(norm_cross), after_cross_grad)
    src_half = final_norm(core, src_sum, src_got, sources, gain(norm_src), None)
    latents_grad = in_place(lat_half, tensor_swap(lat_half, 1))
    sources_grad = in_place(src_half, tensor_swap(src_half, 1))

    copies = 1.0 / (tensor_size // 2)
    own_blocks = blocks * s_index + turned[: blocks // 2]
    own_clips = block_clip[own_blocks]
    norms = jnp.sqrt(jnp.sum(squares, axis=1) / (GROUP * width_d) + 1e-06)
    frames = clip_frames[own_clips].astype(f32)
    share = jnp.sum(norms / (GROUPS_FRAME * frames)) / clip_frames.shape[0]
    small = jnp.concatenate(
        (
            src_gain,
            cross_gain,
            self_gain * copies,
            mlp_gain * copies,
            jnp.broadcast_to(share * copies, (1, width_d)),
            jnp.zeros((3, width_d), f32),
        )
    )
    small = sum_everywhere(small)
    units = mlp_in.shape[1]
    return (
        output,
        latents_grad,
        sources_grad,
        small[0],
        small[1],
        small[2],
        small[3],
        cross_out[:, 0:width],
        cross_out[:, width : 2 * width],
        cross_out[:, 2 * width : 3 * width],
        cross_out[:, 3 * width :].T,
        self_out[:, 0:width],
        self_out[:, width : 2 * width],
        self_out[:, 2 * width : 3 * width],
        self_out[:, 3 * width :].T,
        mlp_in_out,
        mlp_out_out.T,
        small[4, 0],
    )


def solution(mesh):
    in_specs = (
        P("seq", None), P("seq", None), P("seq", None), P(), P(), P(), P(), P(), P(),
        P(None, "tensor"), P(None, "tensor"), P(None, "tensor"), P("tensor", None),
        P(None, "tensor"), P(None, "tensor"), P(None, "tensor"), P("tensor", None),
        P(None, "tensor"), P("tensor", None), P("seq", None),
    )
    out_specs = (
        P("seq", None), P("seq", None), P("seq", None), P(), P(), P(), P(),
        P("seq", "tensor"), P("seq", "tensor"), P("seq", "tensor"), P("tensor", "seq"),
        P("seq", "tensor"), P("seq", "tensor"), P("seq", "tensor"), P("tensor", "seq"),
        P("seq", "tensor"), P("tensor", "seq"), P(),
    )
    return jax.shard_map(local, mesh=mesh, in_specs=in_specs, out_specs=out_specs, check_vma=False)
```

```python
import functools
import math

import jax
import jax.numpy as jnp
from jax import lax
from jax.experimental import pallas as pl
from jax.experimental.pallas import tpu as pltpu
from jax.sharding import PartitionSpec as P

HEAD = 128
GROUP = 128
SRC = 256
GROUPS_FRAME = 8
LOG2E = 1.4426950408889634
epsilon = 1e-05
masked_value = -1e30
bf16 = jnp.bfloat16
f32 = jnp.float32
EXTRA = 16
WEIGHT = 1

VMEM = pl.BlockSpec(memory_space=pltpu.VMEM)
SMEM = pl.BlockSpec(memory_space=pltpu.SMEM)


def sds(shape, dtype):
    return jax.ShapeDtypeStruct(shape, dtype)


def dot(a, b):
    return lax.dot_general(a, b, (((1,), (0,)), ((), ())), preferred_element_type=f32)


def dot_t(a, b):
    return lax.dot_general(a, b, (((1,), (1,)), ((), ())), preferred_element_type=f32)


def dot_ta(a, b):
    return lax.dot_general(a, b, (((0,), (0,)), ((), ())), preferred_element_type=f32)


def centre(values):
    centred = values - jnp.mean(values, axis=-1, keepdims=True)
    variance = jnp.mean(centred * centred, axis=-1, keepdims=True)
    inverse = lax.rsqrt(variance + epsilon)
    return centred * inverse, inverse


ANY = pl.BlockSpec(memory_space=pl.ANY)
CHUNK = 64


def by_chunks(rows, step, carry=0):
    for first in range(0, rows, CHUNK):
        carry = step(slice(first, first + CHUNK), carry)
    return carry


def norm_into(out_ref, in_ref, gain_ref):
    gain_vec = gain_ref[...]

    def step(r, held):
        out_ref[r, :] = (centre(in_ref[r, :].astype(f32))[0] * gain_vec).astype(bf16)
        return held

    by_chunks(in_ref.shape[0], step)


def folded(rows_value):
    parts = [rows_value[k : k + 8] for k in range(0, CHUNK, 8)]
    while len(parts) > 1:
        parts = [parts[k] + parts[k + 1] for k in range(0, len(parts), 2)]
    return parts[0]


def call(
    body, outs, ins, args, name, scratch=(), grid=None, prefetch=0, flops=0, nbytes=0, trans=0, ties=(), aliases=None,
    spare=6,
):
    given = prefetch + len(ins)
    room = 0
    for spec, v in [*zip(ins, args[prefetch:]), *[(spec, shape) for shape, spec in outs]]:
        if spec.block_shape is not None:
            room += 2 * math.prod(spec.block_shape) * v.dtype.itemsize
        elif spec is VMEM:
            room += math.prod(v.shape) * v.dtype.itemsize
    room += sum(math.prod(v.shape) * jnp.dtype(v.dtype).itemsize for v in scratch)

    def run(*refs):
        body(*refs[:given], *refs[given + len(ties) :])

    return pl.pallas_call(
        run,
        out_shape=[shape for shape, ignored in outs],
        grid_spec=pltpu.PrefetchScalarGridSpec(
            num_scalar_prefetch=prefetch,
            grid=() if grid is None else grid,
            in_specs=list(ins) + [ANY] * len(ties),
            out_specs=[spec for ignored, spec in outs],
            scratch_shapes=list(scratch),
        ),
        compiler_params=pltpu.CompilerParams(vmem_limit_bytes=room + spare * 2**20),
        cost_estimate=pl.CostEstimate(
            flops=int(flops * WEIGHT), bytes_accessed=int(nbytes * WEIGHT), transcendentals=int(trans * WEIGHT)
        ),
        input_output_aliases=aliases or {},
        name=name,
    )(*args, *ties)


def index_row(idx_ref, pos_ref, b, blocks, count):
    at = (b + pos_ref[0] * (blocks // 2)) % blocks
    return (idx_ref[pl.ds(at, 1), :] - pos_ref[1] * count).astype(f32)


def clip_of(clip_ref, pos_ref, b, blocks, sets, own):
    half = blocks // 2
    if own:
        return clip_ref[blocks * (pos_ref[1] % sets) + (b + pos_ref[0] * half) % blocks]
    return clip_ref[blocks * (b // blocks) + (b % blocks + pos_ref[0] * half) % blocks]


def cross_forward_body(
    pos_ref, idx_ref, lat_ref, src_ref, gain_one_ref, gain_src_ref, wq_ref, wk_ref, wv_ref,
    n1_ref, ns_ref, q_ref, kvp_ref, keep_ref, send_ref, kv_s, *, steps,
):
    i = pl.program_id(0)
    width = wq_ref.shape[1]
    heads = width // HEAD
    rows_src = src_ref.shape[0]
    norm_into(ns_ref, src_ref, gain_src_ref)
    normed_src = ns_ref[...]
    row0 = pl.multiple_of(i * rows_src, rows_src)
    kv_s[pl.ds(row0, rows_src), 0:width] = dot(normed_src, wk_ref[...]).astype(bf16)
    kv_s[pl.ds(row0, rows_src), width:] = dot(normed_src, wv_ref[...]).astype(bf16)
    norm_into(n1_ref, lat_ref, gain_one_ref)
    normed_one = n1_ref[...]
    grp0 = pl.multiple_of(i * GROUP, GROUP)
    q_ref[pl.ds(grp0, GROUP), :] = dot(normed_one, wq_ref[...]).astype(bf16)

    @pl.when(i == steps - 1)
    def _():
        count = kv_s.shape[0]
        lanes = lax.broadcasted_iota(jnp.int32, (128, count), 1).astype(f32)
        for b in range(steps):
            for part in range(SRC // 128):
                row = index_row(idx_ref, pos_ref, b, steps, count)[:, part * 128 : (part + 1) * 128]
                column = jnp.transpose(jnp.broadcast_to(row, (128, 128)))
                picks = jnp.where(jnp.tile(column, (1, count // 128)) == lanes, 1.0, 0.0).astype(bf16)
                r0 = b * SRC + part * 128
                kvp_ref[r0 : r0 + 128, :] = dot(picks, kv_s[...]).astype(bf16)
        for b in range(steps):
            for h in range(heads):
                cols = slice(h * HEAD, (h + 1) * HEAD)
                q = q_ref[b * GROUP : (b + 1) * GROUP, cols]
                k = kvp_ref[b * SRC : (b + 1) * SRC, cols]
                v = kvp_ref[b * SRC : (b + 1) * SRC, width + h * HEAD : width + (h + 1) * HEAD]
                s = dot_t(q, k) * (HEAD ** (-0.5) * LOG2E)
                p = jnp.exp2(s - jnp.max(s, axis=-1, keepdims=True))
                total = jnp.sum(p, axis=-1, keepdims=True)
                mixed = (dot(p.astype(bf16), v) / total).astype(bf16)
                if b < steps // 2:
                    keep_ref[b * GROUP : (b + 1) * GROUP, cols] = mixed
                else:
                    r0 = (b - steps // 2) * GROUP
                    send_ref[r0 : r0 + GROUP, cols] = mixed


def cross_forward(pos, idx, latents, sources, gain_one, gain_src, wq, wk, wv):
    rows, width_d = latents.shape
    steps = rows // GROUP
    count = sources.shape[0]
    blk = count // steps
    width = wq.shape[1]
    whole = lambda shape: pl.BlockSpec(shape, lambda i, c: (0,) * len(shape))
    return call(
        functools.partial(cross_forward_body, steps=steps),
        [
            (sds((rows, width_d), bf16), pl.BlockSpec((GROUP, width_d), lambda i, c: (i, 0))),
            (sds((count, width_d), bf16), pl.BlockSpec((blk, width_d), lambda i, c: (i, 0))),
            (sds((rows, width), bf16), whole((rows, width))),
            (sds((count, 2 * width), bf16), whole((count, 2 * width))),
            (sds((rows // 2, width), bf16), whole((rows // 2, width))),
            (sds((rows // 2, width), bf16), whole((rows // 2, width))),
        ],
        [
            whole(idx.shape),
            pl.BlockSpec((GROUP, width_d), lambda i, c: ((i + c[0] * (steps // 2)) % steps, 0)),
            pl.BlockSpec((blk, width_d), lambda i, c: (i, 0)),
            whole((1, width_d)),
            whole((1, width_d)),
            whole(wq.shape),
            whole(wk.shape),
            whole(wv.shape),
        ],
        (pos, idx, latents, sources, gain_one, gain_src, wq, wk, wv),
        "cross_forward",
        scratch=[pltpu.VMEM((count, 2 * width), bf16)],
        grid=(steps,),
        prefetch=1,
        flops=4e9,
        nbytes=12e6,
        spare=44,
    )


def project_body(pos_ref, *refs, parts, own_half):
    pieces, weights = refs[:parts], refs[parts : 2 * parts]
    base_ref, gain_ref, after_ref, normed_ref, left_s, right_s = refs[2 * parts :]
    half = after_ref.shape[0]
    width = pieces[0].shape[1]
    for k in range(parts):
        at = pl.multiple_of((pos_ref[2] ^ k) * width, width)
        left_s[:, pl.ds(at, width)] = pieces[k][...]
        right_s[pl.ds(at, width), :] = weights[k][...]
    after_ref[...] = dot(left_s[...], right_s[...])
    first = pos_ref[0] * half if own_half else 0
    gain_vec = gain_ref[...]

    def step(r, held):
        base = base_ref[pl.ds(pl.multiple_of(first + r.start, CHUNK), CHUNK), :]
        after = base.astype(f32) + after_ref[r, :]
        after_ref[r, :] = after
        normed_ref[r, :] = (centre(after)[0] * gain_vec).astype(bf16)
        return held

    by_chunks(half, step)


def project(pos, pieces, weights, base, gain, own_half, ties=()):
    parts = len(pieces)
    half, width = pieces[0].shape
    width_d = weights[0].shape[1]
    return call(
        functools.partial(project_body, parts=parts, own_half=own_half),
        [(sds((half, width_d), f32), VMEM), (sds((half, width_d), bf16), VMEM)],
        [SMEM] + [VMEM] * (2 * parts + 2),
        (pos, *pieces, *weights, base, gain),
        "project",
        scratch=[pltpu.VMEM((half, parts * width), bf16), pltpu.VMEM((parts * width, width_d), bf16)],
        flops=2 * half * width * parts * width_d,
        nbytes=5e6,
        ties=ties,
    )


def qkv_body(mine_ref, other_ref, wq_ref, wk_ref, wv_ref, q_ref, kv_ref):
    half = mine_ref.shape[0]
    width = wq_ref.shape[1]
    for part, ref in enumerate((mine_ref, other_ref)):
        rows = slice(part * half, (part + 1) * half)
        x = ref[...]
        kv_ref[rows, 0:width] = dot(x, wk_ref[...]).astype(bf16)
        kv_ref[rows, width:] = dot(x, wv_ref[...]).astype(bf16)
        q_ref[rows, :] = dot(x, wq_ref[...]).astype(bf16)


def qkv(mine, other, wq, wk, wv):
    half, width_d = mine.shape
    width = wq.shape[1]
    return call(
        qkv_body,
        [(sds((2 * half, width), bf16), VMEM), (sds((2 * half, 2 * width), bf16), VMEM)],
        [VMEM] * 5,
        (mine, other, wq, wk, wv),
        "qkv",
        flops=2 * 2 * half * width_d * 3 * width,
        nbytes=4e6,
    )


def assemble(refs, entries, dst, rows_blocks):
    for ri, base, p, k in entries:
        for j in range(rows_blocks):
            dst[p * rows_blocks + j, pl.ds(place_start(k), GROUP), :] = refs[ri][
                base + j * GROUP : base + (j + 1) * GROUP, :
            ]


def place_start(k):
    return k * GROUP if isinstance(k, int) else pl.multiple_of(k * GROUP, GROUP)


def split_rows(rows_value):
    high = rows_value.astype(bf16)
    rest = rows_value - high.astype(f32)
    middle = rest.astype(bf16)
    low = (rest - middle.astype(f32)).astype(bf16)
    return high, middle, low


def pack_extra(row_tiles, heads, blocks, width):
    per_row = width // 128
    out = []
    for h in range(heads):
        flat = [
            jnp.concatenate(row_tiles[h][r * per_row : (r + 1) * per_row], axis=1)
            for r in range(blocks // per_row)
        ]
        rows_value = jnp.concatenate(flat, axis=0)
        out += [part.astype(f32) for part in split_rows(rows_value)]
    used = heads * 3 * (blocks // per_row)
    if used < EXTRA:
        out.append(jnp.zeros((EXTRA - used, width), f32))
    return jnp.concatenate(out, axis=0).astype(bf16)


def unpack_extra(extra, h, j, blocks, width):
    per_row = width // 128
    rows_per = blocks // per_row
    row, lane = j // per_row, (j % per_row) * 128
    parts = [
        extra[(h * 3 + t) * rows_per + row : (h * 3 + t) * rows_per + row + 1, lane : lane + 128]
        for t in range(3)
    ]
    return (parts[0] + parts[1]) + parts[2]


def attend_body(
    pos_ref, clip_ref, *refs, pieces, entries, heads, blocks, period,
):
    q_ref = refs[0]
    kv_refs = refs[1 : 1 + pieces]
    keep_ref, send_ref, lsex_ref, lsec_ref, kv_s, m_s, l_s, acc_s, row_s, o_s = refs[1 + pieces :]
    width = heads * HEAD
    sets = period // blocks
    assemble(kv_refs, entries, kv_s, blocks)

    def per_block(i, carry):
        r0 = pl.multiple_of(i * GROUP, GROUP)
        own_clip = clip_of(clip_ref, pos_ref, i, blocks, sets, True)
        m_s[...] = jnp.full(m_s.shape, masked_value, f32)
        l_s[...] = jnp.zeros(l_s.shape, f32)
        acc_s[...] = jnp.zeros(acc_s.shape, f32)

        def per_keys(g, inner):
            @pl.when(own_clip == clip_of(clip_ref, pos_ref, g, blocks, sets, False))
            def _():
                for h in range(heads):
                    cols = slice(h * HEAD, (h + 1) * HEAD)
                    q = q_ref[pl.ds(r0, GROUP), cols]
                    k = kv_s[g, :, cols]
                    v = kv_s[g, :, width + h * HEAD : width + (h + 1) * HEAD]
                    s = dot_t(q, k) * (HEAD ** (-0.5) * LOG2E)
                    m_old = m_s[h][:, 0:1]
                    m_new = jnp.maximum(m_old, jnp.max(s, axis=-1, keepdims=True))
                    p = jnp.exp2(s - m_new)
                    alpha = jnp.exp2(m_old - m_new)
                    l_new = l_s[h][:, 0:1] * alpha + jnp.sum(p, axis=-1, keepdims=True)
                    acc_s[h] = acc_s[h] * alpha + dot(p.astype(bf16), v)
                    m_s[h] = jnp.broadcast_to(m_new, (GROUP, 128))
                    l_s[h] = jnp.broadcast_to(l_new, (GROUP, 128))

            return inner

        lax.fori_loop(0, period, per_keys, 0)
        for h in range(heads):
            total = l_s[h]
            o_s[pl.ds(r0, GROUP), h * HEAD : (h + 1) * HEAD] = (acc_s[h] / total).astype(bf16)
            lse = m_s[h] + jnp.log2(total)
            lsec_ref[h, pl.ds(r0, GROUP), :] = lse
            row_s[h, i] = jnp.transpose(lse)[0:8]
        return carry

    lax.fori_loop(0, blocks, per_block, 0)
    half = blocks // 2 * GROUP
    keep_ref[...] = o_s[0:half, :]
    send_ref[...] = o_s[half:, :]
    tiles = [[row_s[h, j][0:1] for j in range(blocks)] for h in range(heads)]
    lsex_ref[...] = pack_extra(tiles, heads, blocks, width)


def attend(pos, clips, q, kv_pieces, entries, ties):
    rows, width = q.shape
    heads, blocks, period = width // HEAD, rows // GROUP, clips.shape[0] // GROUPS_FRAME
    pieces = len(kv_pieces)
    body = functools.partial(
        attend_body, pieces=pieces, entries=entries, heads=heads, blocks=blocks, period=period
    )
    return call(
        body,
        [
            (sds((rows // 2, width), bf16), VMEM),
            (sds((rows // 2, width), bf16), VMEM),
            (sds((EXTRA, width), bf16), VMEM),
            (sds((heads, rows, 128), f32), VMEM),
        ],
        [SMEM, SMEM] + [VMEM] * (1 + pieces),
        (pos, clips, q, *kv_pieces),
        "attend",
        ties=ties,
        scratch=[
            pltpu.VMEM((period, GROUPS_FRAME * GROUP, 2 * width), bf16),
            pltpu.VMEM((heads, GROUP, 128), f32),
            pltpu.VMEM((heads, GROUP, 128), f32),
            pltpu.VMEM((heads, GROUP, HEAD), f32),
            pltpu.VMEM((heads, blocks, 8, 128), f32),
            pltpu.VMEM((rows, width), bf16),
        ],
        flops=2e9,
        nbytes=7e6,
        trans=2e6,
    )


def out_back_body(mine_ref, other_ref, wo_ref, okeep_ref, osend_ref, lsex_ref, dox_ref, dc_ref, *, heads, blocks):
    half = mine_ref.shape[0]
    rows = 2 * half
    tiles = [[] for h in range(heads)]
    for part, (ref, o_ref) in enumerate(((mine_ref, okeep_ref), (other_ref, osend_ref))):
        grad = dot_t(ref[...], wo_ref[...]).astype(bf16)
        dox_ref[part * half : (part + 1) * half, :] = grad
        product = grad.astype(f32) * o_ref[...].astype(f32)
        for h in range(heads):
            delta = jnp.sum(product[:, h * HEAD : (h + 1) * HEAD], axis=-1, keepdims=True)
            delta = jnp.broadcast_to(delta, (half, 128))
            dc_ref[h, part * half : (part + 1) * half, :] = delta
            for j in range(half // GROUP):
                tiles[h].append(jnp.transpose(delta[j * GROUP : (j + 1) * GROUP])[0:1])
    dox_ref[rows : rows + EXTRA, :] = pack_extra(tiles, heads, blocks, heads * HEAD)
    dox_ref[rows + EXTRA :, :] = lsex_ref[...]


def out_back(mine, other, wo, okeep, osend, lsex):
    half, width_d = mine.shape
    width = wo.shape[0]
    heads, blocks = width // HEAD, 2 * half // GROUP
    return call(
        functools.partial(out_back_body, heads=heads, blocks=blocks),
        [(sds((2 * half + 2 * EXTRA, width), bf16), VMEM), (sds((heads, 2 * half, 128), f32), VMEM)],
        [VMEM] * 6,
        (mine, other, wo, okeep, osend, lsex),
        "out_back",
        flops=2 * 2 * half * width * width_d,
        nbytes=4e6,
    )


def query_back_body(pos_ref, clip_ref, *refs, pieces, entries, heads, blocks, period):
    qx_ref, dox_ref, lsec_ref, dc_ref = refs[0:4]
    kv_refs = refs[4 : 4 + pieces]
    dq_ref, kv_s, acc_s = refs[4 + pieces :]
    width = heads * HEAD
    sets = period // blocks
    assemble(kv_refs, entries, kv_s, blocks)

    def per_block(i, carry):
        r0 = pl.multiple_of(i * GROUP, GROUP)
        own_clip = clip_of(clip_ref, pos_ref, i, blocks, sets, True)
        acc_s[...] = jnp.zeros(acc_s.shape, f32)

        def per_keys(g, inner):
            @pl.when(own_clip == clip_of(clip_ref, pos_ref, g, blocks, sets, False))
            def _():
                for h in range(heads):
                    cols = slice(h * HEAD, (h + 1) * HEAD)
                    k = kv_s[g, :, cols]
                    v = kv_s[g, :, width + h * HEAD : width + (h + 1) * HEAD]
                    s = dot_t(qx_ref[pl.ds(r0, GROUP), cols], k) * (HEAD ** (-0.5) * LOG2E)
                    p = jnp.exp2(s - lsec_ref[h, pl.ds(r0, GROUP), :][:, 0:1])
                    dp = dot_t(dox_ref[pl.ds(r0, GROUP), cols], v)
                    delta = dc_ref[h, pl.ds(r0, GROUP), :][:, 0:1]
                    ds = (p * (dp - delta) * (HEAD ** (-0.5))).astype(bf16)
                    acc_s[h] = acc_s[h] + dot(ds, k)

            return inner

        lax.fori_loop(0, period, per_keys, 0)
        for h in range(heads):
            dq_ref[pl.ds(r0, GROUP), h * HEAD : (h + 1) * HEAD] = acc_s[h].astype(bf16)
        return carry

    lax.fori_loop(0, blocks, per_block, 0)


def query_back(pos, clips, qx, dox, lsec, dc, kv_pieces, entries):
    rows, width = qx.shape
    heads, blocks, period = width // HEAD, rows // GROUP, clips.shape[0] // GROUPS_FRAME
    pieces = len(kv_pieces)
    return call(
        functools.partial(
            query_back_body, pieces=pieces, entries=entries, heads=heads, blocks=blocks, period=period
        ),
        [(sds((rows, width), bf16), VMEM)],
        [SMEM, SMEM] + [VMEM] * (4 + pieces),
        (pos, clips, qx, dox, lsec, dc, *kv_pieces),
        "query_back",
        scratch=[
            pltpu.VMEM((period, GROUPS_FRAME * GROUP, 2 * width), bf16),
            pltpu.VMEM((heads, GROUP, HEAD), f32),
        ],
        flops=2e9,
        nbytes=7e6,
        trans=2e6,
    )[0]


def key_back_body(
    pos_ref, clip_ref, *refs, q_pieces, do_pieces, q_entries, do_entries, heads, blocks, period
):
    kv_ref, dq_ref, wq_ref, wk_ref, wv_ref = refs[0:5]
    qx_refs = refs[5 : 5 + q_pieces]
    dox_refs = refs[5 + q_pieces : 5 + q_pieces + do_pieces]
    dqkv_ref, keep_ref, send_ref, q_s, do_s, lse_s, delta_s, dk_s, dv_s = refs[5 + q_pieces + do_pieces :]
    width = heads * HEAD
    rows = blocks * GROUP
    sets = period // blocks
    assemble(qx_refs, q_entries, q_s, blocks)
    assemble(dox_refs, do_entries, do_s, blocks)
    for first, target in ((rows, delta_s), (rows + EXTRA, lse_s)):
        for ri, base, p, k in do_entries:
            extra = dox_refs[ri][base + first : base + first + EXTRA, :].astype(f32)
            for h in range(heads):
                for j in range(blocks):
                    line = unpack_extra(extra, h, j, blocks, width)
                    target[p * blocks + j, h, :, pl.ds(place_start(k), GROUP)] = jnp.broadcast_to(
                        line, (8, 128)
                    )
    dqkv_ref[:, 0:width] = dq_ref[...]

    def per_block(j, carry):
        r0 = pl.multiple_of(j * GROUP, GROUP)
        own_clip = clip_of(clip_ref, pos_ref, j, blocks, sets, True)
        dk_s[...] = jnp.zeros(dk_s.shape, f32)
        dv_s[...] = jnp.zeros(dv_s.shape, f32)

        def per_queries(g, inner):
            @pl.when(own_clip == clip_of(clip_ref, pos_ref, g, blocks, sets, False))
            def _():
                for h in range(heads):
                    cols = slice(h * HEAD, (h + 1) * HEAD)
                    k = kv_ref[pl.ds(r0, GROUP), cols]
                    v = kv_ref[pl.ds(r0, GROUP), width + h * HEAD : width + (h + 1) * HEAD]
                    q = q_s[g, :, cols]
                    do = do_s[g, :, cols]
                    st = dot_t(k, q) * (HEAD ** (-0.5) * LOG2E)
                    pt = jnp.exp2(st - lse_s[g, h, 0:1, :])
                    dv_s[h] = dv_s[h] + dot(pt.astype(bf16), do)
                    dpt = dot_t(v, do)
                    dst = (pt * (dpt - delta_s[g, h, 0:1, :]) * (HEAD ** (-0.5))).astype(bf16)
                    dk_s[h] = dk_s[h] + dot(dst, q)

            return inner

        lax.fori_loop(0, period, per_queries, 0)
        for h in range(heads):
            dqkv_ref[pl.ds(r0, GROUP), width + h * HEAD : width + (h + 1) * HEAD] = dk_s[h].astype(bf16)
            dqkv_ref[pl.ds(r0, GROUP), 2 * width + h * HEAD : 2 * width + (h + 1) * HEAD] = dv_s[
                h
            ].astype(bf16)
        return carry

    lax.fori_loop(0, blocks, per_block, 0)
    half = rows // 2
    for part, ref in enumerate((keep_ref, send_ref)):
        r = slice(part * half, (part + 1) * half)
        total = dot_t(dqkv_ref[r, 0:width], wq_ref[...])
        total = total + dot_t(dqkv_ref[r, width : 2 * width], wk_ref[...])
        total = total + dot_t(dqkv_ref[r, 2 * width :], wv_ref[...])
        ref[...] = total.astype(bf16)


def key_back(pos, clips, kv, dq, wq, wk, wv, qx_pieces, q_entries, dox_pieces, do_entries, ties):
    rows, width = dq.shape
    width_d = wq.shape[0]
    heads, blocks, period = width // HEAD, rows // GROUP, clips.shape[0] // GROUPS_FRAME
    tall = GROUPS_FRAME * GROUP
    return call(
        functools.partial(
            key_back_body, q_pieces=len(qx_pieces), do_pieces=len(dox_pieces), q_entries=q_entries,
            do_entries=do_entries, heads=heads, blocks=blocks, period=period,
        ),
        [
            (sds((rows, 3 * width), bf16), VMEM),
            (sds((rows // 2, width_d), bf16), VMEM),
            (sds((rows // 2, width_d), bf16), VMEM),
        ],
        [SMEM, SMEM] + [VMEM] * (5 + len(qx_pieces) + len(dox_pieces)),
        (pos, clips, kv, dq, wq, wk, wv, *qx_pieces, *dox_pieces),
        "key_back",
        ties=ties,
        scratch=[
            pltpu.VMEM((period, tall, width), bf16),
            pltpu.VMEM((period, tall, width), bf16),
            pltpu.VMEM((period, heads, 8, tall), f32),
            pltpu.VMEM((period, heads, 8, tall), f32),
            pltpu.VMEM((heads, GROUP, HEAD), f32),
            pltpu.VMEM((heads, GROUP, HEAD), f32),
        ],
        flops=4e9,
        nbytes=9e6,
        trans=2e6,
    )


def mlp_body(mine_ref, other_ref, win_ref, ag_ref, act_ref, hg_ref, keep_ref, send_ref, *, steps):
    i = pl.program_id(0)
    x = jnp.where(i < steps // 2, mine_ref[...], other_ref[...])
    units = win_ref.shape[1]
    chunk = 256
    total = None
    for n in range(units // chunk):
        cols = slice(n * chunk, (n + 1) * chunk)
        w = win_ref[:, cols]
        hidden = dot(x, w)
        cdf = 0.5 * (1.0 + lax.erf(hidden * 0.7071067811865476))
        act_ref[:, cols] = (hidden * cdf).astype(bf16)
        density = jnp.exp2(hidden * hidden * (-0.5 * LOG2E)) * 0.3989422804014327
        grad = (ag_ref[:, cols] * (cdf + hidden * density)).astype(bf16)
        hg_ref[:, cols] = grad
        term = dot_t(grad, w)
        total = term if total is None else total + term
    total = total.astype(bf16)

    @pl.when(i < steps // 2)
    def _():
        keep_ref[...] = total

    @pl.when(i >= steps // 2)
    def _():
        send_ref[...] = total


def mlp(mine, other, w_in, act_grad):
    half, width_d = mine.shape
    units = w_in.shape[1]
    steps = 2 * half // GROUP
    rows = 2 * half
    low = lambda i: (jnp.minimum(i, steps // 2 - 1), 0)
    high = lambda i: (jnp.maximum(i - steps // 2, 0), 0)
    return call(
        functools.partial(mlp_body, steps=steps),
        [
            (sds((rows, units), bf16), pl.BlockSpec((GROUP, units), lambda i: (i, 0))),
            (sds((rows, units), bf16), pl.BlockSpec((GROUP, units), lambda i: (i, 0))),
            (sds((half, width_d), bf16), pl.BlockSpec((GROUP, width_d), low)),
            (sds((half, width_d), bf16), pl.BlockSpec((GROUP, width_d), high)),
        ],
        [
            pl.BlockSpec((GROUP, width_d), low),
            pl.BlockSpec((GROUP, width_d), high),
            pl.BlockSpec((width_d, units), lambda i: (0, 0)),
            pl.BlockSpec((GROUP, units), lambda i: (i, 0)),
        ],
        (mine, other, w_in, act_grad),
        "mlp",
        grid=(steps,),
        flops=4 * rows * width_d * units,
        nbytes=9e6,
        trans=2 * rows * units,
    )


def mlp_down_body(act_ref, w_ref, keep_ref, send_ref, *, steps):
    i = pl.program_id(0)
    total = dot(act_ref[...], w_ref[...]).astype(bf16)

    @pl.when(i < steps // 2)
    def _():
        keep_ref[...] = total

    @pl.when(i >= steps // 2)
    def _():
        send_ref[...] = total


def mlp_down(activated, w_out, ties):
    rows, units = activated.shape
    width_d = w_out.shape[1]
    steps = rows // GROUP
    half = sds((rows // 2, width_d), bf16)
    return call(
        functools.partial(mlp_down_body, steps=steps),
        [
            (half, pl.BlockSpec((GROUP, width_d), lambda i: (jnp.minimum(i, steps // 2 - 1), 0))),
            (half, pl.BlockSpec((GROUP, width_d), lambda i: (jnp.maximum(i - steps // 2, 0), 0))),
        ],
        [
            pl.BlockSpec((GROUP, units), lambda i: (i, 0)),
            pl.BlockSpec((units, width_d), lambda i: (0, 0)),
        ],
        (activated, w_out),
        "mlp_down",
        grid=(steps,),
        flops=2 * rows * units * width_d,
        nbytes=4e6,
        ties=ties,
    )


def act_back_body(pos_ref, og_ref, w_ref, rel_ref, ag_ref):
    rel_ref[...] = og_ref[...]
    ag_ref[...] = dot_t(og_ref[...], w_ref[...])


def act_back(pos, out_grad, w_out):
    rows, width_d = out_grad.shape
    units = w_out.shape[0]
    steps = rows // GROUP
    blk = pl.BlockSpec((GROUP, width_d), lambda i, c: (i, 0))
    return call(
        act_back_body,
        [
            (sds((rows, width_d), bf16), blk),
            (sds((rows, units), f32), pl.BlockSpec((GROUP, units), lambda i, c: (i, 0))),
        ],
        [
            pl.BlockSpec((GROUP, width_d), lambda i, c: ((i + c[0] * (steps // 2)) % steps, 0)),
            pl.BlockSpec((units, width_d), lambda i, c: (0, 0)),
        ],
        (pos, out_grad, w_out),
        "act_back",
        grid=(steps,),
        prefetch=1,
        flops=2 * rows * width_d * units,
        nbytes=6e6,
    )


def through_norm(n, v, gain_vec):
    unit, inverse = centre(v)
    t = n * gain_vec
    back = inverse * (
        t - jnp.mean(t, axis=-1, keepdims=True) - unit * jnp.mean(t * unit, axis=-1, keepdims=True)
    )
    return back, unit


def norm_back_body(s_ref, r_ref, v_ref, gain_ref, base_ref, after_ref, branch_ref, gg_ref):
    gain_vec = gain_ref[...]

    def step(r, held):
        n = s_ref[r, :].astype(f32) + r_ref[r, :].astype(f32)
        back, unit = through_norm(n, v_ref[r, :], gain_vec)
        after = base_ref[r, :].astype(f32) + back
        after_ref[r, :] = after
        branch_ref[r, :] = after.astype(bf16)
        return held + folded(n * unit)

    total = by_chunks(s_ref.shape[0], step, jnp.zeros((8, s_ref.shape[1]), f32))
    gg_ref[...] = jnp.sum(total, axis=0, keepdims=True)


def norm_back(s, r, v, gain, base, ties):
    half, width_d = s.shape
    return call(
        norm_back_body,
        [
            (sds((half, width_d), f32), VMEM),
            (sds((half, width_d), bf16), VMEM),
            (sds((1, width_d), f32), VMEM),
        ],
        [VMEM] * 5,
        (s, r, v, gain, base),
        "norm_back",
        ties=ties,
        flops=20 * half * width_d,
        nbytes=5e6,
    )


def final_body(pos_ref, s_ref, r_ref, v_ref, gain_ref, *refs, with_base):
    gain_vec = gain_ref[...]

    def step(r, held):
        n = s_ref[r, :].astype(f32) + r_ref[r, :].astype(f32)
        back = through_norm(n, v_ref[r, :].astype(f32), gain_vec)[0]
        if with_base:
            back = refs[0][r, :] + back
        refs[-2][r, :] = back.astype(bf16)
        refs[-1][r, :] = back.astype(bf16)
        return held

    by_chunks(s_ref.shape[0], step)


def final_norm(pos, s, r, v, gain, base, ties):
    half, width_d = s.shape
    rows = 128
    steps = half // rows
    blk = pl.BlockSpec((rows, width_d), lambda i, c: (i, 0))
    own = pl.BlockSpec((rows, width_d), lambda i, c: (c[0] * steps + i, 0))
    more = () if base is None else (base,)
    return call(
        functools.partial(final_body, with_base=base is not None),
        [(sds((half, width_d), bf16), blk), (sds((2 * half, width_d), bf16), own)],
        [blk, blk, own, pl.BlockSpec((1, width_d), lambda i, c: (0, 0))] + [blk] * len(more),
        (pos, s, r, v, gain, *more),
        "final_norm",
        ties=ties,
        grid=(steps,),
        prefetch=1,
        flops=20 * half * width_d,
        nbytes=8 * half * width_d,
    )


def place_body(pos_ref, other_ref, whole_ref, out_ref):
    out_ref[...] = other_ref[...]


def place_other(pos, whole, other):
    half, width_d = other.shape
    rows = 256
    steps = half // rows
    return call(
        place_body,
        [(sds(whole.shape, bf16), pl.BlockSpec((rows, width_d), lambda i, c: ((1 - c[0]) * steps + i, 0)))],
        [pl.BlockSpec((rows, width_d), lambda i, c: (i, 0)), ANY],
        (pos, other, whole),
        "place_other",
        grid=(steps,),
        prefetch=1,
        nbytes=4 * half * width_d,
        aliases={2: 0},
    )[0]


def result_body(pos_ref, s_ref, r_ref, after_ref, half_ref, whole_ref, squares_ref):
    def step(r, held):
        result = after_ref[r, :] + (s_ref[r, :].astype(f32) + r_ref[r, :].astype(f32))
        half_ref[r, :] = result.astype(bf16)
        whole_ref[r, :] = result.astype(bf16)
        return held + folded(result * result)

    total = by_chunks(s_ref.shape[0], step, jnp.zeros((8, s_ref.shape[1]), f32))
    squares_ref[pl.ds(pl.program_id(0), 1), :] = jnp.sum(total, axis=0, keepdims=True)


def result_half(pos, s, r, after):
    half, width_d = s.shape
    steps = half // GROUP
    blk = pl.BlockSpec((GROUP, width_d), lambda i, c: (i, 0))
    own = pl.BlockSpec((GROUP, width_d), lambda i, c: (c[0] * steps + i, 0))
    return call(
        result_body,
        [
            (sds((half, width_d), bf16), blk),
            (sds((2 * half, width_d), bf16), own),
            (sds((steps, width_d), f32), pl.BlockSpec((steps, width_d), lambda i, c: (0, 0))),
        ],
        [blk] * 3,
        (pos, s, r, after),
        "result",
        grid=(steps,),
        prefetch=1,
        flops=6 * half * width_d,
        nbytes=5e6,
    )


def gains_body(
    pos_ref, clip_ref, frames_ref, one_keep, one_send, src_keep, src_send, lat_ref, src_ref,
    self_ref, mlp_ref, squares_ref, out_ref, *, one_steps, src_steps, blocks, sets, copies, clips,
):
    i = pl.program_id(0)

    @pl.when(i == 0)
    def _():
        width_d = out_ref.shape[1]
        share = jnp.zeros((1, 1), f32)
        for b in range(blocks // 2):
            total = jnp.sum(squares_ref[b : b + 1, :], axis=1, keepdims=True)
            frames = frames_ref[clip_of(clip_ref, pos_ref, b, blocks, sets, True)].astype(f32)
            norm = jnp.sqrt(total / (GROUP * width_d) + 1e-06)
            share = share + norm / (jnp.broadcast_to(frames, (1, 1)) * (GROUPS_FRAME * clips))
        out_ref[0:2, :] = jnp.zeros((2, width_d), f32)
        out_ref[2:3, :] = self_ref[...] * copies
        out_ref[3:4, :] = mlp_ref[...] * copies
        out_ref[4:8, :] = jnp.broadcast_to(share * copies, (4, width_d))

    def add(row, v_ref, keep_ref, send_ref, kept):
        def step(r, held):
            n = jnp.where(kept, keep_ref[r, :].astype(f32), send_ref[r, :].astype(f32))
            return held + folded(n * centre(v_ref[r, :].astype(f32))[0])

        total = by_chunks(v_ref.shape[0], step, jnp.zeros((8, v_ref.shape[1]), f32))
        out_ref[row : row + 1, :] = out_ref[row : row + 1, :] + jnp.sum(total, axis=0, keepdims=True)

    pl.when(i < one_steps)(lambda: add(1, lat_ref, one_keep, one_send, i < one_steps // 2))
    pl.when(i >= one_steps)(lambda: add(0, src_ref, src_keep, src_send, i - one_steps < src_steps // 2))


def gains(pos, clips, frames, one_keep, one_send, src_keep, src_send, latents, sources, self_gain, mlp_gain,
          squares, copies, ties):
    half, width_d = one_keep.shape
    count = sources.shape[0]
    blk = 256
    one_steps, src_steps = 2 * half // blk, count // blk
    blocks = 2 * half // GROUP
    sets = clips.shape[0] // GROUPS_FRAME // blocks
    clamp = lambda v, top: jnp.minimum(jnp.maximum(v, 0), top)
    spec = lambda f: pl.BlockSpec((blk, width_d), lambda i, *c: (f(i, c[0]), 0))
    fixed = lambda n: pl.BlockSpec((n, width_d), lambda i, *c: (0, 0))
    turn = lambda i, c, steps: (clamp(i, steps - 1) + c[0] * (steps // 2)) % steps
    return call(
        functools.partial(
            gains_body, one_steps=one_steps, src_steps=src_steps, blocks=blocks, sets=sets, copies=copies,
            clips=frames.shape[0],
        ),
        [(sds((8, width_d), f32), fixed(8))],
        [
            spec(lambda i, c: clamp(i, one_steps // 2 - 1)),
            spec(lambda i, c: clamp(i - one_steps // 2, one_steps // 2 - 1)),
            spec(lambda i, c: clamp(i - one_steps, src_steps // 2 - 1)),
            spec(lambda i, c: clamp(i - one_steps - src_steps // 2, src_steps // 2 - 1)),
            spec(lambda i, c: turn(i, c, one_steps)),
            spec(lambda i, c: turn(i - one_steps, c, src_steps)),
            fixed(1), fixed(1), fixed(blocks // 2),
        ],
        (pos, clips, frames, one_keep, one_send, src_keep, src_send, latents, sources, self_gain, mlp_gain, squares),
        "gains",
        grid=(one_steps + src_steps,),
        prefetch=3,
        flops=20 * (2 * half + count) * width_d,
        nbytes=4 * (2 * half + count) * width_d,
        ties=ties,
    )[0]


def feature_grads_body(pos_ref, *refs, items, split, blk):
    given = sum(a + b for a, b in items)
    outs = refs[given:]
    at, column = 0, 0
    for lefts, rights in items:
        total, row = None, 0
        for k in range(lefts):
            left = refs[at + k]
            rows = left.shape[0]
            if rights == 1:
                right = refs[at + lefts][row : row + rows, :]
            else:
                right = refs[at + lefts + k][...]
            term = dot_ta(left[...], right)
            total = term if total is None else total + term
            row += rows
        at += lefts + rights
        cols = slice(column, column + total.shape[1])
        column += total.shape[1]
        total = total.astype(bf16)
        for j in range(blk // 128):
            part = total[j * 128 : (j + 1) * 128]
            if split:
                mine = (pos_ref[1] + j) % 2 == 0

                @pl.when(mine)
                def _():
                    outs[0][j // 2, :, cols] = part

                @pl.when(jnp.logical_not(mine))
                def _():
                    outs[1][j // 2, :, cols] = part
            else:
                outs[0][j, :, cols] = part


def feature_grads(pos, items, split, ties=()):
    arrays, specs, counts, columns, flops = [], [], [], 0, 0
    features = items[0][0][0].shape[1]
    blk = 512
    for lefts, rights in items:
        counts.append((len(lefts), len(rights)))
        for v in lefts:
            arrays.append(v)
            specs.append(pl.BlockSpec((v.shape[0], blk), lambda i, c: (0, i)))
            flops += 2 * v.shape[0] * v.shape[1] * rights[0].shape[1]
        for v in rights:
            arrays.append(v)
            specs.append(pl.BlockSpec(v.shape, lambda i, c: (0, 0)))
        columns += rights[0].shape[1]
    steps = features // blk
    sets = features // 256 if split else features // 128
    count = 2 if split else 1
    outs = [
        (sds((sets, 128, columns), bf16), pl.BlockSpec((sets // steps, 128, columns), lambda i, c: (i, 0, 0)))
    ] * count
    return call(
        functools.partial(feature_grads_body, items=tuple(counts), split=split, blk=blk),
        outs,
        specs,
        (pos, *arrays),
        "feature_grads",
        grid=(steps,),
        prefetch=1,
        flops=flops,
        nbytes=2 * features * columns + sum(2 * v.size for v in arrays),
        ties=ties,
    )


def middle_body(pos_ref, keep_ref, got_ref, own_ref, one_ref, two_ref, three_ref):
    z = pos_ref[1] // 2
    own_ref[...] = keep_ref[z].astype(f32) + got_ref[z].astype(f32)
    for d, ref in ((1, one_ref), (2, two_ref), (3, three_ref)):
        at = (z + d) % 4
        ref[...] = (keep_ref[at].astype(f32) + got_ref[at].astype(f32)).astype(bf16)


def ended_body(own_ref, one_ref, two_ref, three_ref, *outs, turned):
    total = own_ref[...] + (one_ref[...].astype(f32) + (two_ref[...].astype(f32) + three_ref[...].astype(f32)))
    width = total.shape[1] // len(outs)
    for k, ref in enumerate(outs):
        part = total[:, k * width : (k + 1) * width]
        ref[...] = part.T if k in turned else part


def scatter_middle(pos, keep, got, ties=()):
    blk = keep.shape[1:]
    return call(
        middle_body,
        [(sds(blk, f32), VMEM)] + [(sds(blk, bf16), VMEM)] * 3,
        [SMEM, VMEM, VMEM],
        (pos, keep, got),
        "middle",
        nbytes=4 * keep.size,
        ties=ties,
    )


def scatter_end(own, moved, parts, turned, ties=()):
    blk = own.shape
    width = blk[1] // parts
    return call(
        functools.partial(ended_body, turned=turned),
        [(sds((width, blk[0]) if k in turned else (blk[0], width), f32), VMEM) for k in range(parts)],
        [VMEM] * 4,
        (own, *moved),
        "ended",
        nbytes=10 * blk[0] * blk[1],
        ties=ties,
    )


def flip_x(v):
    return lax.ppermute(v, "seq", xor_pairs(1, 8))


def spread_z(pieces):
    return [lax.ppermute(pieces[d - 1], "seq", ring_pairs(d)) for d in (1, 2, 3)]


def scatter_whole(pos, items, parts, turned, ties):
    whole = feature_grads(pos, items, False, ties)[0]
    whole = whole.reshape(-1, whole.shape[2])
    total = lax.psum_scatter(whole, "seq", scatter_dimension=0, tiled=True).astype(f32)
    width = total.shape[1] // parts
    pieces = [total[:, k * width : (k + 1) * width] for k in range(parts)]
    return [piece.T if k in turned else piece for k, piece in enumerate(pieces)]


def tied(values, other):
    out = lax.optimization_barrier((other, *values))
    return list(out[1:]), out[0]


def cross_back_body(
    pos_ref, mine_ref, other_ref, wo_ref, q_ref, kvp_ref, idx_ref, wq_ref, wk_ref, wv_ref,
    dq_ref, dkv_ref, one_keep_ref, one_send_ref, src_keep_ref, src_send_ref, dkvp_s, *, blocks,
):
    width = wq_ref.shape[1]
    heads = width // HEAD
    count = kvp_ref.shape[0]
    scale = HEAD ** (-0.5)
    for b in range(blocks):
        ref = mine_ref if b < blocks // 2 else other_ref
        part = (b % (blocks // 2)) * GROUP
        grad = dot_t(ref[part : part + GROUP, :], wo_ref[...]).astype(bf16)
        for h in range(heads):
            cols = slice(h * HEAD, (h + 1) * HEAD)
            vcols = slice(width + h * HEAD, width + (h + 1) * HEAD)
            q = q_ref[b * GROUP : (b + 1) * GROUP, cols]
            k = kvp_ref[b * SRC : (b + 1) * SRC, cols]
            v = kvp_ref[b * SRC : (b + 1) * SRC, vcols]
            do = grad[:, cols]
            s = dot_t(q, k) * (scale * LOG2E)
            p = jnp.exp2(s - jnp.max(s, axis=-1, keepdims=True))
            p = p / jnp.sum(p, axis=-1, keepdims=True)
            dp = dot_t(do, v)
            delta = jnp.sum(p * dp, axis=-1, keepdims=True)
            ds = (p * (dp - delta) * scale).astype(bf16)
            dq_ref[b * GROUP : (b + 1) * GROUP, cols] = dot(ds, k).astype(bf16)
            dkvp_s[b * SRC : (b + 1) * SRC, cols] = dot_ta(ds, q).astype(bf16)
            dkvp_s[b * SRC : (b + 1) * SRC, vcols] = dot_ta(p.astype(bf16), do).astype(bf16)
        one = dot_t(dq_ref[b * GROUP : (b + 1) * GROUP, :], wq_ref[...]).astype(bf16)
        if b < blocks // 2:
            one_keep_ref[part : part + GROUP, :] = one
        else:
            one_send_ref[part : part + GROUP, :] = one
    half = count // 2
    blk = 256
    row = jnp.concatenate([index_row(idx_ref, pos_ref, b, blocks, count) for b in range(blocks)], axis=1)
    for n in range(count // blk):
        r0 = pl.multiple_of(
            (pos_ref[0] if n * blk < half else 1 - pos_ref[0]) * half + (n * blk) % half, blk
        )
        wanted = lax.broadcasted_iota(jnp.int32, (blk, count), 0).astype(f32) + r0.astype(f32)
        picks = jnp.where(row == wanted, 1.0, 0.0).astype(bf16)
        dkv = dot(picks, dkvp_s[...]).astype(bf16)
        dkv_ref[pl.ds(r0, blk), :] = dkv
        total = (dot_t(dkv[:, 0:width], wk_ref[...]) + dot_t(dkv[:, width:], wv_ref[...])).astype(bf16)
        at = (n * blk) % half
        if n * blk < half:
            src_keep_ref[at : at + blk, :] = total
        else:
            src_send_ref[at : at + blk, :] = total


def cross_back(pos, mine, other, wo, q, kvp, idx, wq, wk, wv, ties):
    rows, width = q.shape
    width_d = wq.shape[0]
    count = kvp.shape[0]
    blocks = rows // GROUP
    return call(
        functools.partial(cross_back_body, blocks=blocks),
        [
            (sds((rows, width), bf16), VMEM),
            (sds((count, 2 * width), bf16), VMEM),
            (sds((rows // 2, width_d), bf16), VMEM),
            (sds((rows // 2, width_d), bf16), VMEM),
            (sds((count // 2, width_d), bf16), VMEM),
            (sds((count // 2, width_d), bf16), VMEM),
        ],
        [SMEM] + [VMEM] * 9,
        (pos, mine, other, wo, q, kvp, idx, wq, wk, wv),
        "cross_back",
        ties=ties,
        scratch=[pltpu.VMEM((count, 2 * width), bf16)],
        flops=4e9,
        nbytes=12e6,
    )


def xor_pairs(bit, size):
    return [(i, i ^ bit) for i in range(size)]


def ring_pairs(d):
    return [(s, ((s // 2 + d) % 4) * 2 + s % 2) for s in range(8)]


def tensor_swap(x, bit):
    return lax.ppermute(x, "tensor", xor_pairs(bit, lax.axis_size("tensor")))


def seq_gather(x):
    size = lax.axis_size("seq")
    if size == 8:
        move = lambda v, pairs: lax.ppermute(v, "seq", pairs)
        flip = xor_pairs(1, 8)
        beside = move(x, flip)
        up = move(x, ring_pairs(1))
        down = move(x, ring_pairs(-1))
        far = move(up, ring_pairs(1))
        up_beside = move(up, flip)
        down_beside = move(beside, ring_pairs(-1))
        far_beside = move(far, flip)
        return [x, beside, up, down, far, up_beside, down_beside, far_beside]
    return gather_whole(x)


def gather_whole(x):
    return [lax.all_gather(x, "seq", axis=0, tiled=True)]


def gather_entries(size, rows, sets):
    if size == 8:
        return tuple((k, 0, 0, k) for k in range(8))
    return whole_entries(size, rows, sets)


def whole_entries(size, rows, sets):
    return tuple((0, s * rows, s % sets, s // sets) for s in range(size))


def half_sum(keep, send):
    size = lax.axis_size("tensor")
    got = tensor_swap(send, 1)
    own = (keep.astype(f32) + got.astype(f32)).astype(bf16)
    bit = 2
    while True:
        other = tensor_swap(own, bit)
        if bit * 2 >= size:
            return own, other
        own = (own.astype(f32) + other.astype(f32)).astype(bf16)
        bit *= 2


def tensor_pieces(keep, send):
    size = lax.axis_size("tensor")
    return [keep if k == 0 else tensor_swap(send if k % 2 else keep, k) for k in range(size)]


def weight_far(weight):
    pieces = {0: weight}
    bit = lax.axis_size("tensor") // 2
    while bit >= 2:
        pieces.update({k + bit: tensor_swap(v, bit) for k, v in list(pieces.items())})
        bit //= 2
    return pieces


def weight_pieces(pieces):
    pieces = dict(pieces)
    pieces.update({k + 1: tensor_swap(v, 1) for k, v in list(pieces.items())})
    return [pieces[k] for k in range(len(pieces))]


def tie_all(pieces, other):
    keys = sorted(pieces)
    tied = lax.optimization_barrier((other, *[pieces[k] for k in keys]))
    return dict(zip(keys, tied[1:])), tied[0]


def sum_everywhere(v):
    for axis in ("tensor", "seq"):
        bit = 1
        while bit < lax.axis_size(axis):
            v = v + lax.ppermute(v, axis, xor_pairs(bit, lax.axis_size(axis)))
            bit *= 2
    return v


def local(
    latents, sources, source_index, block_clip, clip_frames, norm_src, norm_cross, norm_self, norm_mlp,
    cross_q, cross_k, cross_v, cross_o, self_q, self_k, self_v, self_o, mlp_in, mlp_out, out_grad,
):
    rows, width_d = latents.shape
    blocks = rows // GROUP
    width = cross_q.shape[1]
    units = mlp_in.shape[1]
    tensor_size, seq_size = lax.axis_size("tensor"), lax.axis_size("seq")
    core = lax.axis_index("tensor") % 2
    pos = jnp.stack((core, lax.axis_index("seq"), lax.axis_index("tensor"))).astype(jnp.int32)
    sets = block_clip.shape[0] // GROUPS_FRAME // blocks
    gain = lambda g: g.reshape(1, width_d)
    kv_entries = gather_entries(seq_size, rows, sets)
    out_entries = gather_entries(seq_size, rows + 2 * EXTRA, sets)

    cross_o_far = weight_far(cross_o)
    normed_one, normed_src, cross_query, cross_kv, mixed_keep, mixed_send = cross_forward(
        pos, source_index, latents, sources, gain(norm_cross), gain(norm_src), cross_q, cross_k, cross_v
    )
    cross_o_far, mixed_keep = tie_all(cross_o_far, mixed_keep)
    after_cross, two_mine = project(
        pos, tensor_pieces(mixed_keep, mixed_send), weight_pieces(cross_o_far), latents, gain(norm_self), True
    )
    two_other = tensor_swap(two_mine, 1)
    query, key_value = qkv(two_mine, two_other, self_q, self_k, self_v)
    kv_pieces = seq_gather(key_value)
    self_o_tied, two_mine = tie_all({0: self_o}, two_mine)
    self_o_all = weight_pieces(weight_far(self_o_tied[0]))
    out_rel, act_grad = act_back(pos, out_grad, mlp_out)
    split = seq_size == 8
    query_pieces = seq_gather(query)
    self_keep, self_send, lse_rows, lse_columns = attend(
        pos, block_clip, query, kv_pieces, kv_entries, (act_grad, *self_o_all[1:], *query_pieces[2:4])
    )
    after_self, three_mine = project(
        pos, tensor_pieces(self_keep, self_send), self_o_all, after_cross, gain(norm_mlp), False,
        (query_pieces[1], query_pieces[4]) if split else (),
    )
    three_other = tensor_swap(three_mine, 1)
    activated, hidden_grad, three_keep, three_send = mlp(three_mine, three_other, mlp_in, act_grad)

    three_sum, three_got = half_sum(three_keep, three_send)
    in_items = (((three_mine, three_other), (hidden_grad,)),)
    out_items = (((out_rel,), (activated,)),)
    early = ()
    if split:
        in_keep, in_send = feature_grads(pos, in_items, True, (three_sum,))
        early = (in_keep, *query_pieces[5:])
    after_self_grad, self_branch, mlp_gain = norm_back(
        three_sum, three_got, after_self, gain(norm_mlp), out_rel, early
    )
    self_branch_other = tensor_swap(self_branch, 1)

    out_more, delta_columns = out_back(self_branch, self_branch_other, self_o, self_keep, self_send, lse_rows)
    if split:
        in_got = flip_x(in_send)
    out_pieces = seq_gather(out_more)
    self_query_grad = query_back(
        pos, block_clip, query, out_more, lse_columns, delta_columns, kv_pieces, kv_entries
    )
    begun = tuple(out_pieces[1:4]) if split else (out_more,)
    down_keep, down_send = mlp_down(activated, mlp_out, begun)
    result_sum, result_got = half_sum(down_keep, down_send)
    output_half, output_whole, squares = result_half(pos, result_sum, result_got, after_self)
    output = place_other(pos, output_whole, tensor_swap(output_half, 1))
    early = ()
    if split:
        out_keep, out_send = feature_grads(pos, out_items, True, begun)
        in_own, *in_parts = scatter_middle(pos, in_keep, in_got)
        (*in_parts, out_send), out_pieces[-1] = tied([*in_parts, out_send], out_pieces[-1])
        out_got = flip_x(out_send)
        in_moved = spread_z(in_parts)
        early = (squares,)
    self_grads, two_keep, two_send = key_back(
        pos, block_clip, key_value, self_query_grad, self_q, self_k, self_v,
        query_pieces, kv_entries, out_pieces, out_entries, early,
    )
    two_sum, two_got = half_sum(two_keep, two_send)
    self_items = (
        ((two_mine, two_other), (self_grads,)),
        ((self_branch, self_branch_other), (self_keep, self_send)),
    )
    early = ()
    if split:
        self_wkeep, self_wsend = feature_grads(pos, self_items, True, (two_sum,))
        early = (self_wkeep, out_got, *in_moved)
    after_cross_grad, cross_branch, self_gain = norm_back(
        two_sum, two_got, after_cross, gain(norm_self), after_self_grad, early
    )
    cross_branch_other = tensor_swap(cross_branch, 1)

    cross_query_grad, cross_kv_grad, one_keep, one_send, src_keep, src_send = cross_back(
        pos, cross_branch, cross_branch_other, cross_o, cross_query, cross_kv, source_index,
        cross_q, cross_k, cross_v, (output,),
    )
    src_sum, src_got = half_sum(src_keep, src_send)
    one_sum, one_got = half_sum(one_keep, one_send)
    cross_items = (
        ((normed_one,), (cross_query_grad,)),
        ((normed_src,), (cross_kv_grad,)),
        ((cross_branch, cross_branch_other), (mixed_keep, mixed_send)),
    )
    early = ()
    if split:
        (self_wsend,), src_sum = tied([self_wsend], src_sum)
        self_wgot = flip_x(self_wsend)
        out_own, *out_parts = scatter_middle(pos, out_keep, out_got, (one_sum, src_sum))
        out_moved = spread_z(out_parts)
        cross_wkeep, cross_wsend = feature_grads(pos, cross_items, True, (src_sum, one_sum, out_own))
        (cross_wsend,), self_wgot = tied([cross_wsend], self_wgot)
        cross_wgot = flip_x(cross_wsend)
        self_own, *self_parts = scatter_middle(pos, self_wkeep, self_wgot, (cross_wkeep,))
        self_moved = spread_z(self_parts)
        early = (cross_wkeep, *out_moved)
    small = gains(
        pos, block_clip, clip_frames, one_keep, one_send, src_keep, src_send, latents, sources,
        self_gain, mlp_gain, squares, 2.0 / tensor_size, (src_sum, one_sum, *early[0:1]),
    )
    early = (*early, small)
    src_half, src_whole = final_norm(pos, src_sum, src_got, sources, gain(norm_src), None, early)
    lat_half, lat_whole = final_norm(pos, one_sum, one_got, latents, gain(norm_cross), after_cross_grad, early)
    (small,), lat_half = tied([small], lat_half)
    small = sum_everywhere(small)
    sources_grad = place_other(pos, src_whole, tensor_swap(src_half, 1))
    latents_grad = place_other(pos, lat_whole, tensor_swap(lat_half, 1))
    if split:
        cross_own, *cross_parts = scatter_middle(pos, cross_wkeep, cross_wgot, self_moved)
        cross_outs = scatter_end(cross_own, spread_z(cross_parts), 4, (3,))
        self_outs = scatter_end(self_own, self_moved, 4, (3,))
        mlp_outs = [
            scatter_end(in_own, in_moved, 1, ())[0],
            scatter_end(out_own, out_moved, 1, (0,))[0],
        ]
    else:
        cross_outs = scatter_whole(pos, cross_items, 4, (3,), ())
        self_outs = scatter_whole(pos, self_items, 4, (3,), ())
        mlp_outs = scatter_whole(pos, in_items, 1, (), ()) + scatter_whole(pos, out_items, 1, (0,), ())
    return (
        output, latents_grad, sources_grad, small[0], small[1], small[2], small[3],
        *cross_outs, *self_outs, *mlp_outs, small[4, 0],
    )


def solution(mesh):
    in_specs = (
        P("seq", None), P("seq", None), P("seq", None), P(), P(), P(), P(), P(), P(),
        P(None, "tensor"), P(None, "tensor"), P(None, "tensor"), P("tensor", None),
        P(None, "tensor"), P(None, "tensor"), P(None, "tensor"), P("tensor", None),
        P(None, "tensor"), P("tensor", None), P("seq", None),
    )
    out_specs = (
        P("seq", None), P("seq", None), P("seq", None), P(), P(), P(), P(),
        P("seq", "tensor"), P("seq", "tensor"), P("seq", "tensor"), P("tensor", "seq"),
        P("seq", "tensor"), P("seq", "tensor"), P("seq", "tensor"), P("tensor", "seq"),
        P("seq", "tensor"), P("tensor", "seq"), P(),
    )
    return jax.shard_map(local, mesh=mesh, in_specs=in_specs, out_specs=out_specs, check_vma=False)
```

```python
import functools
import math

import jax
import jax.numpy as jnp
from jax import lax
from jax.experimental import pallas as pl
from jax.experimental.pallas import tpu as pltpu
from jax.sharding import PartitionSpec as P

HEAD = 128
GROUP = 128
SRC = 256
GROUPS_FRAME = 8
LOG2E = 1.4426950408889634
epsilon = 1e-05
masked_value = -1e30
bf16 = jnp.bfloat16
f32 = jnp.float32
EXTRA = 16
WEIGHT = 1

VMEM = pl.BlockSpec(memory_space=pltpu.VMEM)
SMEM = pl.BlockSpec(memory_space=pltpu.SMEM)


def sds(shape, dtype):
    return jax.ShapeDtypeStruct(shape, dtype)


def dot(a, b):
    return lax.dot_general(a, b, (((1,), (0,)), ((), ())), preferred_element_type=f32)


def dot_t(a, b):
    return lax.dot_general(a, b, (((1,), (1,)), ((), ())), preferred_element_type=f32)


def dot_ta(a, b):
    return lax.dot_general(a, b, (((0,), (0,)), ((), ())), preferred_element_type=f32)


def centre(values):
    centred = values - jnp.mean(values, axis=-1, keepdims=True)
    variance = jnp.mean(centred * centred, axis=-1, keepdims=True)
    inverse = lax.rsqrt(variance + epsilon)
    return centred * inverse, inverse


ANY = pl.BlockSpec(memory_space=pl.ANY)
CHUNK = 64


def by_chunks(rows, step, carry=0):
    for first in range(0, rows, CHUNK):
        carry = step(slice(first, first + CHUNK), carry)
    return carry


def norm_into(out_ref, in_ref, gain_ref):
    gain_vec = gain_ref[...]

    def step(r, held):
        out_ref[r, :] = (centre(in_ref[r, :].astype(f32))[0] * gain_vec).astype(bf16)
        return held

    by_chunks(in_ref.shape[0], step)


def folded(rows_value):
    parts = [rows_value[k : k + 8] for k in range(0, CHUNK, 8)]
    while len(parts) > 1:
        parts = [parts[k] + parts[k + 1] for k in range(0, len(parts), 2)]
    return parts[0]


def call(
    body, outs, ins, args, name, scratch=(), grid=None, prefetch=0, flops=0, nbytes=0, trans=0, ties=(), aliases=None,
    spare=6,
):
    given = prefetch + len(ins)
    room = 0
    for spec, v in [*zip(ins, args[prefetch:]), *[(spec, shape) for shape, spec in outs]]:
        if spec.block_shape is not None:
            room += 2 * math.prod(spec.block_shape) * v.dtype.itemsize
        elif spec is VMEM:
            room += math.prod(v.shape) * v.dtype.itemsize
    room += sum(math.prod(v.shape) * jnp.dtype(v.dtype).itemsize for v in scratch)

    def run(*refs):
        body(*refs[:given], *refs[given + len(ties) :])

    return pl.pallas_call(
        run,
        out_shape=[shape for shape, ignored in outs],
        grid_spec=pltpu.PrefetchScalarGridSpec(
            num_scalar_prefetch=prefetch,
            grid=() if grid is None else grid,
            in_specs=list(ins) + [ANY] * len(ties),
            out_specs=[spec for ignored, spec in outs],
            scratch_shapes=list(scratch),
        ),
        compiler_params=pltpu.CompilerParams(vmem_limit_bytes=room + spare * 2**20),
        cost_estimate=pl.CostEstimate(
            flops=int(flops * WEIGHT), bytes_accessed=int(nbytes * WEIGHT), transcendentals=int(trans * WEIGHT)
        ),
        input_output_aliases=aliases or {},
        name=name,
    )(*args, *ties)


def index_row(idx_ref, pos_ref, b, blocks, count):
    at = (b + pos_ref[0] * (blocks // 2)) % blocks
    return (idx_ref[pl.ds(at, 1), :] - pos_ref[1] * count).astype(f32)


def clip_of(clip_ref, pos_ref, b, blocks, sets, own):
    half = blocks // 2
    if own:
        return clip_ref[blocks * (pos_ref[1] % sets) + (b + pos_ref[0] * half) % blocks]
    return clip_ref[blocks * (b // blocks) + (b % blocks + pos_ref[0] * half) % blocks]


def cross_forward_body(
    pos_ref, idx_ref, lat_ref, src_ref, gain_one_ref, gain_src_ref, wq_ref, wk_ref, wv_ref,
    n1_ref, ns_ref, q_ref, kvp_ref, keep_ref, send_ref, kv_s, *, steps,
):
    i = pl.program_id(0)
    width = wq_ref.shape[1]
    heads = width // HEAD
    rows_src = src_ref.shape[0]
    norm_into(ns_ref, src_ref, gain_src_ref)
    normed_src = ns_ref[...]
    row0 = pl.multiple_of(i * rows_src, rows_src)
    kv_s[pl.ds(row0, rows_src), 0:width] = dot(normed_src, wk_ref[...]).astype(bf16)
    kv_s[pl.ds(row0, rows_src), width:] = dot(normed_src, wv_ref[...]).astype(bf16)
    norm_into(n1_ref, lat_ref, gain_one_ref)
    normed_one = n1_ref[...]
    grp0 = pl.multiple_of(i * GROUP, GROUP)
    q_ref[pl.ds(grp0, GROUP), :] = dot(normed_one, wq_ref[...]).astype(bf16)

    @pl.when(i == steps - 1)
    def _():
        count = kv_s.shape[0]
        lanes = lax.broadcasted_iota(jnp.int32, (128, count), 1).astype(f32)
        for b in range(steps):
            for part in range(SRC // 128):
                row = index_row(idx_ref, pos_ref, b, steps, count)[:, part * 128 : (part + 1) * 128]
                column = jnp.transpose(jnp.broadcast_to(row, (128, 128)))
                picks = jnp.where(jnp.tile(column, (1, count // 128)) == lanes, 1.0, 0.0).astype(bf16)
                r0 = b * SRC + part * 128
                kvp_ref[r0 : r0 + 128, :] = dot(picks, kv_s[...]).astype(bf16)
        for b in range(steps):
            for h in range(heads):
                cols = slice(h * HEAD, (h + 1) * HEAD)
                q = q_ref[b * GROUP : (b + 1) * GROUP, cols]
                k = kvp_ref[b * SRC : (b + 1) * SRC, cols]
                v = kvp_ref[b * SRC : (b + 1) * SRC, width + h * HEAD : width + (h + 1) * HEAD]
                s = dot_t(q, k) * (HEAD ** (-0.5) * LOG2E)
                p = jnp.exp2(s - jnp.max(s, axis=-1, keepdims=True))
                total = jnp.sum(p, axis=-1, keepdims=True)
                mixed = (dot(p.astype(bf16), v) / total).astype(bf16)
                if b < steps // 2:
                    keep_ref[b * GROUP : (b + 1) * GROUP, cols] = mixed
                else:
                    r0 = (b - steps // 2) * GROUP
                    send_ref[r0 : r0 + GROUP, cols] = mixed


def cross_forward(pos, idx, latents, sources, gain_one, gain_src, wq, wk, wv):
    rows, width_d = latents.shape
    steps = rows // GROUP
    count = sources.shape[0]
    blk = count // steps
    width = wq.shape[1]
    whole = lambda shape: pl.BlockSpec(shape, lambda i, c: (0,) * len(shape))
    return call(
        functools.partial(cross_forward_body, steps=steps),
        [
            (sds((rows, width_d), bf16), pl.BlockSpec((GROUP, width_d), lambda i, c: (i, 0))),
            (sds((count, width_d), bf16), pl.BlockSpec((blk, width_d), lambda i, c: (i, 0))),
            (sds((rows, width), bf16), whole((rows, width))),
            (sds((count, 2 * width), bf16), whole((count, 2 * width))),
            (sds((rows // 2, width), bf16), whole((rows // 2, width))),
            (sds((rows // 2, width), bf16), whole((rows // 2, width))),
        ],
        [
            whole(idx.shape),
            pl.BlockSpec((GROUP, width_d), lambda i, c: ((i + c[0] * (steps // 2)) % steps, 0)),
            pl.BlockSpec((blk, width_d), lambda i, c: (i, 0)),
            whole((1, width_d)),
            whole((1, width_d)),
            whole(wq.shape),
            whole(wk.shape),
            whole(wv.shape),
        ],
        (pos, idx, latents, sources, gain_one, gain_src, wq, wk, wv),
        "cross_forward",
        scratch=[pltpu.VMEM((count, 2 * width), bf16)],
        grid=(steps,),
        prefetch=1,
        flops=4e9,
        nbytes=12e6,
        spare=44,
    )


def project_body(pos_ref, *refs, parts, own_half):
    pieces, weights = refs[:parts], refs[parts : 2 * parts]
    base_ref, gain_ref, after_ref, normed_ref, left_s, right_s = refs[2 * parts :]
    half = after_ref.shape[0]
    width = pieces[0].shape[1]
    for k in range(parts):
        at = pl.multiple_of((pos_ref[2] ^ k) * width, width)
        left_s[:, pl.ds(at, width)] = pieces[k][...]
        right_s[pl.ds(at, width), :] = weights[k][...]
    after_ref[...] = dot(left_s[...], right_s[...])
    first = pos_ref[0] * half if own_half else 0
    gain_vec = gain_ref[...]

    def step(r, held):
        base = base_ref[pl.ds(pl.multiple_of(first + r.start, CHUNK), CHUNK), :]
        after = base.astype(f32) + after_ref[r, :]
        after_ref[r, :] = after
        normed_ref[r, :] = (centre(after)[0] * gain_vec).astype(bf16)
        return held

    by_chunks(half, step)


def project(pos, pieces, weights, base, gain, own_half, ties=()):
    parts = len(pieces)
    half, width = pieces[0].shape
    width_d = weights[0].shape[1]
    return call(
        functools.partial(project_body, parts=parts, own_half=own_half),
        [(sds((half, width_d), f32), VMEM), (sds((half, width_d), bf16), VMEM)],
        [SMEM] + [VMEM] * (2 * parts + 2),
        (pos, *pieces, *weights, base, gain),
        "project",
        scratch=[pltpu.VMEM((half, parts * width), bf16), pltpu.VMEM((parts * width, width_d), bf16)],
        flops=2 * half * width * parts * width_d,
        nbytes=5e6,
        ties=ties,
    )


def qkv_body(mine_ref, other_ref, wq_ref, wk_ref, wv_ref, q_ref, kv_ref):
    half = mine_ref.shape[0]
    width = wq_ref.shape[1]
    for part, ref in enumerate((mine_ref, other_ref)):
        rows = slice(part * half, (part + 1) * half)
        x = ref[...]
        kv_ref[rows, 0:width] = dot(x, wk_ref[...]).astype(bf16)
        kv_ref[rows, width:] = dot(x, wv_ref[...]).astype(bf16)
        q_ref[rows, :] = dot(x, wq_ref[...]).astype(bf16)


def qkv(mine, other, wq, wk, wv):
    half, width_d = mine.shape
    width = wq.shape[1]
    return call(
        qkv_body,
        [(sds((2 * half, width), bf16), VMEM), (sds((2 * half, 2 * width), bf16), VMEM)],
        [VMEM] * 5,
        (mine, other, wq, wk, wv),
        "qkv",
        flops=2 * 2 * half * width_d * 3 * width,
        nbytes=4e6,
    )


def assemble(refs, entries, dst, rows_blocks):
    for ri, base, p, k in entries:
        for j in range(rows_blocks):
            dst[p * rows_blocks + j, pl.ds(place_start(k), GROUP), :] = refs[ri][
                base + j * GROUP : base + (j + 1) * GROUP, :
            ]


def place_start(k):
    return k * GROUP if isinstance(k, int) else pl.multiple_of(k * GROUP, GROUP)


def split_rows(rows_value):
    high = rows_value.astype(bf16)
    rest = rows_value - high.astype(f32)
    middle = rest.astype(bf16)
    low = (rest - middle.astype(f32)).astype(bf16)
    return high, middle, low


def pack_extra(row_tiles, heads, blocks, width):
    per_row = width // 128
    out = []
    for h in range(heads):
        flat = [
            jnp.concatenate(row_tiles[h][r * per_row : (r + 1) * per_row], axis=1)
            for r in range(blocks // per_row)
        ]
        rows_value = jnp.concatenate(flat, axis=0)
        out += [part.astype(f32) for part in split_rows(rows_value)]
    used = heads * 3 * (blocks // per_row)
    if used < EXTRA:
        out.append(jnp.zeros((EXTRA - used, width), f32))
    return jnp.concatenate(out, axis=0).astype(bf16)


def unpack_extra(extra, h, j, blocks, width):
    per_row = width // 128
    rows_per = blocks // per_row
    row, lane = j // per_row, (j % per_row) * 128
    parts = [
        extra[(h * 3 + t) * rows_per + row : (h * 3 + t) * rows_per + row + 1, lane : lane + 128]
        for t in range(3)
    ]
    return (parts[0] + parts[1]) + parts[2]


def attend_body(
    pos_ref, clip_ref, *refs, pieces, entries, heads, blocks, period,
):
    q_ref = refs[0]
    kv_refs = refs[1 : 1 + pieces]
    keep_ref, send_ref, lsex_ref, lsec_ref, kv_s, m_s, l_s, acc_s, row_s, o_s = refs[1 + pieces :]
    width = heads * HEAD
    sets = period // blocks
    assemble(kv_refs, entries, kv_s, blocks)

    def per_block(i, carry):
        r0 = pl.multiple_of(i * GROUP, GROUP)
        own_clip = clip_of(clip_ref, pos_ref, i, blocks, sets, True)
        m_s[...] = jnp.full(m_s.shape, masked_value, f32)
        l_s[...] = jnp.zeros(l_s.shape, f32)
        acc_s[...] = jnp.zeros(acc_s.shape, f32)

        def per_keys(g, inner):
            @pl.when(own_clip == clip_of(clip_ref, pos_ref, g, blocks, sets, False))
            def _():
                for h in range(heads):
                    cols = slice(h * HEAD, (h + 1) * HEAD)
                    q = q_ref[pl.ds(r0, GROUP), cols]
                    k = kv_s[g, :, cols]
                    v = kv_s[g, :, width + h * HEAD : width + (h + 1) * HEAD]
                    s = dot_t(q, k) * (HEAD ** (-0.5) * LOG2E)
                    m_old = m_s[h][:, 0:1]
                    m_new = jnp.maximum(m_old, jnp.max(s, axis=-1, keepdims=True))
                    p = jnp.exp2(s - m_new)
                    alpha = jnp.exp2(m_old - m_new)
                    l_new = l_s[h][:, 0:1] * alpha + jnp.sum(p, axis=-1, keepdims=True)
                    acc_s[h] = acc_s[h] * alpha + dot(p.astype(bf16), v)
                    m_s[h] = jnp.broadcast_to(m_new, (GROUP, 128))
                    l_s[h] = jnp.broadcast_to(l_new, (GROUP, 128))

            return inner

        lax.fori_loop(0, period, per_keys, 0)
        for h in range(heads):
            total = l_s[h]
            o_s[pl.ds(r0, GROUP), h * HEAD : (h + 1) * HEAD] = (acc_s[h] / total).astype(bf16)
            lse = m_s[h] + jnp.log2(total)
            lsec_ref[h, pl.ds(r0, GROUP), :] = lse
            row_s[h, i] = jnp.transpose(lse)[0:8]
        return carry

    lax.fori_loop(0, blocks, per_block, 0)
    half = blocks // 2 * GROUP
    keep_ref[...] = o_s[0:half, :]
    send_ref[...] = o_s[half:, :]
    tiles = [[row_s[h, j][0:1] for j in range(blocks)] for h in range(heads)]
    lsex_ref[...] = pack_extra(tiles, heads, blocks, width)


def attend(pos, clips, q, kv_pieces, entries, ties):
    rows, width = q.shape
    heads, blocks, period = width // HEAD, rows // GROUP, clips.shape[0] // GROUPS_FRAME
    pieces = len(kv_pieces)
    body = functools.partial(
        attend_body, pieces=pieces, entries=entries, heads=heads, blocks=blocks, period=period
    )
    return call(
        body,
        [
            (sds((rows // 2, width), bf16), VMEM),
            (sds((rows // 2, width), bf16), VMEM),
            (sds((EXTRA, width), bf16), VMEM),
            (sds((heads, rows, 128), f32), VMEM),
        ],
        [SMEM, SMEM] + [VMEM] * (1 + pieces),
        (pos, clips, q, *kv_pieces),
        "attend",
        ties=ties,
        scratch=[
            pltpu.VMEM((period, GROUPS_FRAME * GROUP, 2 * width), bf16),
            pltpu.VMEM((heads, GROUP, 128), f32),
            pltpu.VMEM((heads, GROUP, 128), f32),
            pltpu.VMEM((heads, GROUP, HEAD), f32),
            pltpu.VMEM((heads, blocks, 8, 128), f32),
            pltpu.VMEM((rows, width), bf16),
        ],
        flops=2e9,
        nbytes=7e6,
        trans=2e6,
    )


def out_back_body(mine_ref, other_ref, wo_ref, okeep_ref, osend_ref, lsex_ref, dox_ref, dc_ref, *, heads, blocks):
    half = mine_ref.shape[0]
    rows = 2 * half
    tiles = [[] for h in range(heads)]
    for part, (ref, o_ref) in enumerate(((mine_ref, okeep_ref), (other_ref, osend_ref))):
        grad = dot_t(ref[...], wo_ref[...]).astype(bf16)
        dox_ref[part * half : (part + 1) * half, :] = grad
        product = grad.astype(f32) * o_ref[...].astype(f32)
        for h in range(heads):
            delta = jnp.sum(product[:, h * HEAD : (h + 1) * HEAD], axis=-1, keepdims=True)
            delta = jnp.broadcast_to(delta, (half, 128))
            dc_ref[h, part * half : (part + 1) * half, :] = delta
            for j in range(half // GROUP):
                tiles[h].append(jnp.transpose(delta[j * GROUP : (j + 1) * GROUP])[0:1])
    dox_ref[rows : rows + EXTRA, :] = pack_extra(tiles, heads, blocks, heads * HEAD)
    dox_ref[rows + EXTRA :, :] = lsex_ref[...]


def out_back(mine, other, wo, okeep, osend, lsex):
    half, width_d = mine.shape
    width = wo.shape[0]
    heads, blocks = width // HEAD, 2 * half // GROUP
    return call(
        functools.partial(out_back_body, heads=heads, blocks=blocks),
        [(sds((2 * half + 2 * EXTRA, width), bf16), VMEM), (sds((heads, 2 * half, 128), f32), VMEM)],
        [VMEM] * 6,
        (mine, other, wo, okeep, osend, lsex),
        "out_back",
        flops=2 * 2 * half * width * width_d,
        nbytes=4e6,
    )


def query_back_body(pos_ref, clip_ref, *refs, pieces, entries, heads, blocks, period):
    qx_ref, dox_ref, lsec_ref, dc_ref = refs[0:4]
    kv_refs = refs[4 : 4 + pieces]
    dq_ref, kv_s, acc_s = refs[4 + pieces :]
    width = heads * HEAD
    sets = period // blocks
    assemble(kv_refs, entries, kv_s, blocks)

    def per_block(i, carry):
        r0 = pl.multiple_of(i * GROUP, GROUP)
        own_clip = clip_of(clip_ref, pos_ref, i, blocks, sets, True)
        acc_s[...] = jnp.zeros(acc_s.shape, f32)

        def per_keys(g, inner):
            @pl.when(own_clip == clip_of(clip_ref, pos_ref, g, blocks, sets, False))
            def _():
                for h in range(heads):
                    cols = slice(h * HEAD, (h + 1) * HEAD)
                    k = kv_s[g, :, cols]
                    v = kv_s[g, :, width + h * HEAD : width + (h + 1) * HEAD]
                    s = dot_t(qx_ref[pl.ds(r0, GROUP), cols], k) * (HEAD ** (-0.5) * LOG2E)
                    p = jnp.exp2(s - lsec_ref[h, pl.ds(r0, GROUP), :][:, 0:1])
                    dp = dot_t(dox_ref[pl.ds(r0, GROUP), cols], v)
                    delta = dc_ref[h, pl.ds(r0, GROUP), :][:, 0:1]
                    ds = (p * (dp - delta) * (HEAD ** (-0.5))).astype(bf16)
                    acc_s[h] = acc_s[h] + dot(ds, k)

            return inner

        lax.fori_loop(0, period, per_keys, 0)
        for h in range(heads):
            dq_ref[pl.ds(r0, GROUP), h * HEAD : (h + 1) * HEAD] = acc_s[h].astype(bf16)
        return carry

    lax.fori_loop(0, blocks, per_block, 0)


def query_back(pos, clips, qx, dox, lsec, dc, kv_pieces, entries):
    rows, width = qx.shape
    heads, blocks, period = width // HEAD, rows // GROUP, clips.shape[0] // GROUPS_FRAME
    pieces = len(kv_pieces)
    return call(
        functools.partial(
            query_back_body, pieces=pieces, entries=entries, heads=heads, blocks=blocks, period=period
        ),
        [(sds((rows, width), bf16), VMEM)],
        [SMEM, SMEM] + [VMEM] * (4 + pieces),
        (pos, clips, qx, dox, lsec, dc, *kv_pieces),
        "query_back",
        scratch=[
            pltpu.VMEM((period, GROUPS_FRAME * GROUP, 2 * width), bf16),
            pltpu.VMEM((heads, GROUP, HEAD), f32),
        ],
        flops=2e9,
        nbytes=7e6,
        trans=2e6,
    )[0]


def key_back_body(
    pos_ref, clip_ref, *refs, q_pieces, do_pieces, q_entries, do_entries, heads, blocks, period
):
    kv_ref, dq_ref, wq_ref, wk_ref, wv_ref = refs[0:5]
    qx_refs = refs[5 : 5 + q_pieces]
    dox_refs = refs[5 + q_pieces : 5 + q_pieces + do_pieces]
    dqkv_ref, keep_ref, send_ref, q_s, do_s, lse_s, delta_s, dk_s, dv_s = refs[5 + q_pieces + do_pieces :]
    width = heads * HEAD
    rows = blocks * GROUP
    sets = period // blocks
    assemble(qx_refs, q_entries, q_s, blocks)
    assemble(dox_refs, do_entries, do_s, blocks)
    for first, target in ((rows, delta_s), (rows + EXTRA, lse_s)):
        for ri, base, p, k in do_entries:
            extra = dox_refs[ri][base + first : base + first + EXTRA, :].astype(f32)
            for h in range(heads):
                for j in range(blocks):
                    line = unpack_extra(extra, h, j, blocks, width)
                    target[p * blocks + j, h, :, pl.ds(place_start(k), GROUP)] = jnp.broadcast_to(
                        line, (8, 128)
                    )
    dqkv_ref[:, 0:width] = dq_ref[...]

    def per_block(j, carry):
        r0 = pl.multiple_of(j * GROUP, GROUP)
        own_clip = clip_of(clip_ref, pos_ref, j, blocks, sets, True)
        dk_s[...] = jnp.zeros(dk_s.shape, f32)
        dv_s[...] = jnp.zeros(dv_s.shape, f32)

        def per_queries(g, inner):
            @pl.when(own_clip == clip_of(clip_ref, pos_ref, g, blocks, sets, False))
            def _():
                for h in range(heads):
                    cols = slice(h * HEAD, (h + 1) * HEAD)
                    k = kv_ref[pl.ds(r0, GROUP), cols]
                    v = kv_ref[pl.ds(r0, GROUP), width + h * HEAD : width + (h + 1) * HEAD]
                    q = q_s[g, :, cols]
                    do = do_s[g, :, cols]
                    st = dot_t(k, q) * (HEAD ** (-0.5) * LOG2E)
                    pt = jnp.exp2(st - lse_s[g, h, 0:1, :])
                    dv_s[h] = dv_s[h] + dot(pt.astype(bf16), do)
                    dpt = dot_t(v, do)
                    dst = (pt * (dpt - delta_s[g, h, 0:1, :]) * (HEAD ** (-0.5))).astype(bf16)
                    dk_s[h] = dk_s[h] + dot(dst, q)

            return inner

        lax.fori_loop(0, period, per_queries, 0)
        for h in range(heads):
            dqkv_ref[pl.ds(r0, GROUP), width + h * HEAD : width + (h + 1) * HEAD] = dk_s[h].astype(bf16)
            dqkv_ref[pl.ds(r0, GROUP), 2 * width + h * HEAD : 2 * width + (h + 1) * HEAD] = dv_s[
                h
            ].astype(bf16)
        return carry

    lax.fori_loop(0, blocks, per_block, 0)
    half = rows // 2
    for part, ref in enumerate((keep_ref, send_ref)):
        r = slice(part * half, (part + 1) * half)
        total = dot_t(dqkv_ref[r, 0:width], wq_ref[...])
        total = total + dot_t(dqkv_ref[r, width : 2 * width], wk_ref[...])
        total = total + dot_t(dqkv_ref[r, 2 * width :], wv_ref[...])
        ref[...] = total.astype(bf16)


def key_back(pos, clips, kv, dq, wq, wk, wv, qx_pieces, q_entries, dox_pieces, do_entries, ties):
    rows, width = dq.shape
    width_d = wq.shape[0]
    heads, blocks, period = width // HEAD, rows // GROUP, clips.shape[0] // GROUPS_FRAME
    tall = GROUPS_FRAME * GROUP
    return call(
        functools.partial(
            key_back_body, q_pieces=len(qx_pieces), do_pieces=len(dox_pieces), q_entries=q_entries,
            do_entries=do_entries, heads=heads, blocks=blocks, period=period,
        ),
        [
            (sds((rows, 3 * width), bf16), VMEM),
            (sds((rows // 2, width_d), bf16), VMEM),
            (sds((rows // 2, width_d), bf16), VMEM),
        ],
        [SMEM, SMEM] + [VMEM] * (5 + len(qx_pieces) + len(dox_pieces)),
        (pos, clips, kv, dq, wq, wk, wv, *qx_pieces, *dox_pieces),
        "key_back",
        ties=ties,
        scratch=[
            pltpu.VMEM((period, tall, width), bf16),
            pltpu.VMEM((period, tall, width), bf16),
            pltpu.VMEM((period, heads, 8, tall), f32),
            pltpu.VMEM((period, heads, 8, tall), f32),
            pltpu.VMEM((heads, GROUP, HEAD), f32),
            pltpu.VMEM((heads, GROUP, HEAD), f32),
        ],
        flops=4e9,
        nbytes=9e6,
        trans=2e6,
    )


def mlp_body(mine_ref, other_ref, win_ref, ag_ref, act_ref, hg_ref, keep_ref, send_ref, *, steps):
    i = pl.program_id(0)
    x = jnp.where(i < steps // 2, mine_ref[...], other_ref[...])
    units = win_ref.shape[1]
    chunk = 256
    total = None
    for n in range(units // chunk):
        cols = slice(n * chunk, (n + 1) * chunk)
        w = win_ref[:, cols]
        hidden = dot(x, w)
        cdf = 0.5 * (1.0 + lax.erf(hidden * 0.7071067811865476))
        act_ref[:, cols] = (hidden * cdf).astype(bf16)
        density = jnp.exp2(hidden * hidden * (-0.5 * LOG2E)) * 0.3989422804014327
        grad = (ag_ref[:, cols] * (cdf + hidden * density)).astype(bf16)
        hg_ref[:, cols] = grad
        term = dot_t(grad, w)
        total = term if total is None else total + term
    total = total.astype(bf16)

    @pl.when(i < steps // 2)
    def _():
        keep_ref[...] = total

    @pl.when(i >= steps // 2)
    def _():
        send_ref[...] = total


def mlp(mine, other, w_in, act_grad):
    half, width_d = mine.shape
    units = w_in.shape[1]
    steps = 2 * half // GROUP
    rows = 2 * half
    low = lambda i: (jnp.minimum(i, steps // 2 - 1), 0)
    high = lambda i: (jnp.maximum(i - steps // 2, 0), 0)
    return call(
        functools.partial(mlp_body, steps=steps),
        [
            (sds((rows, units), bf16), pl.BlockSpec((GROUP, units), lambda i: (i, 0))),
            (sds((rows, units), bf16), pl.BlockSpec((GROUP, units), lambda i: (i, 0))),
            (sds((half, width_d), bf16), pl.BlockSpec((GROUP, width_d), low)),
            (sds((half, width_d), bf16), pl.BlockSpec((GROUP, width_d), high)),
        ],
        [
            pl.BlockSpec((GROUP, width_d), low),
            pl.BlockSpec((GROUP, width_d), high),
            pl.BlockSpec((width_d, units), lambda i: (0, 0)),
            pl.BlockSpec((GROUP, units), lambda i: (i, 0)),
        ],
        (mine, other, w_in, act_grad),
        "mlp",
        grid=(steps,),
        flops=4 * rows * width_d * units,
        nbytes=9e6,
        trans=2 * rows * units,
    )


def mlp_down_body(act_ref, w_ref, keep_ref, send_ref, *, steps):
    i = pl.program_id(0)
    total = dot(act_ref[...], w_ref[...]).astype(bf16)

    @pl.when(i < steps // 2)
    def _():
        keep_ref[...] = total

    @pl.when(i >= steps // 2)
    def _():
        send_ref[...] = total


def mlp_down(activated, w_out, ties):
    rows, units = activated.shape
    width_d = w_out.shape[1]
    steps = rows // GROUP
    half = sds((rows // 2, width_d), bf16)
    return call(
        functools.partial(mlp_down_body, steps=steps),
        [
            (half, pl.BlockSpec((GROUP, width_d), lambda i: (jnp.minimum(i, steps // 2 - 1), 0))),
            (half, pl.BlockSpec((GROUP, width_d), lambda i: (jnp.maximum(i - steps // 2, 0), 0))),
        ],
        [
            pl.BlockSpec((GROUP, units), lambda i: (i, 0)),
            pl.BlockSpec((units, width_d), lambda i: (0, 0)),
        ],
        (activated, w_out),
        "mlp_down",
        grid=(steps,),
        flops=2 * rows * units * width_d,
        nbytes=4e6,
        ties=ties,
    )


def act_back_body(pos_ref, og_ref, w_ref, rel_ref, ag_ref):
    rel_ref[...] = og_ref[...]
    ag_ref[...] = dot_t(og_ref[...], w_ref[...])


def act_back(pos, out_grad, w_out):
    rows, width_d = out_grad.shape
    units = w_out.shape[0]
    steps = rows // GROUP
    blk = pl.BlockSpec((GROUP, width_d), lambda i, c: (i, 0))
    return call(
        act_back_body,
        [
            (sds((rows, width_d), bf16), blk),
            (sds((rows, units), f32), pl.BlockSpec((GROUP, units), lambda i, c: (i, 0))),
        ],
        [
            pl.BlockSpec((GROUP, width_d), lambda i, c: ((i + c[0] * (steps // 2)) % steps, 0)),
            pl.BlockSpec((units, width_d), lambda i, c: (0, 0)),
        ],
        (pos, out_grad, w_out),
        "act_back",
        grid=(steps,),
        prefetch=1,
        flops=2 * rows * width_d * units,
        nbytes=6e6,
    )


def through_norm(n, v, gain_vec):
    unit, inverse = centre(v)
    t = n * gain_vec
    back = inverse * (
        t - jnp.mean(t, axis=-1, keepdims=True) - unit * jnp.mean(t * unit, axis=-1, keepdims=True)
    )
    return back, unit


def norm_back_body(s_ref, r_ref, v_ref, gain_ref, base_ref, after_ref, branch_ref, gg_ref):
    gain_vec = gain_ref[...]

    def step(r, held):
        n = s_ref[r, :].astype(f32) + r_ref[r, :].astype(f32)
        back, unit = through_norm(n, v_ref[r, :], gain_vec)
        after = base_ref[r, :].astype(f32) + back
        after_ref[r, :] = after
        branch_ref[r, :] = after.astype(bf16)
        return held + folded(n * unit)

    total = by_chunks(s_ref.shape[0], step, jnp.zeros((8, s_ref.shape[1]), f32))
    gg_ref[...] = jnp.sum(total, axis=0, keepdims=True)


def norm_back(s, r, v, gain, base, ties):
    half, width_d = s.shape
    return call(
        norm_back_body,
        [
            (sds((half, width_d), f32), VMEM),
            (sds((half, width_d), bf16), VMEM),
            (sds((1, width_d), f32), VMEM),
        ],
        [VMEM] * 5,
        (s, r, v, gain, base),
        "norm_back",
        ties=ties,
        flops=20 * half * width_d,
        nbytes=5e6,
    )


def final_body(
    pos_ref, s_ref, r_ref, lat_ref, src_ref, gain_one_ref, gain_src_ref, base_ref, half_ref, lat_out, src_out, *, first,
):
    def run(v_ref, gain_ref, base, out_ref):
        gain_vec = gain_ref[...]

        def step(r, held):
            n = s_ref[r, :].astype(f32) + r_ref[r, :].astype(f32)
            back = through_norm(n, v_ref[r, :].astype(f32), gain_vec)[0]
            if base is not None:
                back = base[r, :] + back
            half_ref[r, :] = back.astype(bf16)
            out_ref[r, :] = back.astype(bf16)
            return held

        by_chunks(s_ref.shape[0], step)

    i = pl.program_id(0)
    pl.when(i < first)(lambda: run(lat_ref, gain_one_ref, base_ref, lat_out))
    pl.when(i >= first)(lambda: run(src_ref, gain_src_ref, None, src_out))


def final_norm(pos, s, r, latents, sources, gain_one, gain_src, base, ties):
    width_d = s.shape[1]
    blk = 128
    one, src = latents.shape[0] // 2 // blk, sources.shape[0] // 2 // blk
    at_one = lambda i: jnp.minimum(i, one - 1)
    at_src = lambda i: jnp.maximum(i - one, 0)
    spec = lambda f: pl.BlockSpec((blk, width_d), lambda i, c: (f(i, c), 0))
    gain_spec = pl.BlockSpec((1, width_d), lambda i, c: (0, 0))
    own_one, own_src = spec(lambda i, c: c[0] * one + at_one(i)), spec(lambda i, c: c[0] * src + at_src(i))
    each = spec(lambda i, c: i)
    return call(
        functools.partial(final_body, first=one),
        [(sds(s.shape, bf16), each), (sds(latents.shape, bf16), own_one), (sds(sources.shape, bf16), own_src)],
        [each, each, own_one, own_src, gain_spec, gain_spec, spec(lambda i, c: at_one(i))],
        (pos, s, r, latents, sources, gain_one, gain_src, base),
        "final_norm",
        grid=(one + src,),
        prefetch=1,
        flops=20 * s.size,
        nbytes=8 * s.size,
        ties=ties,
    )


def place_both_body(pos_ref, other_ref, lat_in, src_in, lat_out, src_out):
    i = pl.program_id(0)

    @pl.when(i == 0)
    def _():
        lat_out[...] = other_ref[...]

    @pl.when(i > 0)
    def _():
        src_out[...] = other_ref[...]


def place_both(pos, other, lat_whole, src_whole):
    blk, width_d = lat_whole.shape[0] // 2, other.shape[1]
    steps = other.shape[0] // blk
    spec = lambda f: pl.BlockSpec((blk, width_d), lambda i, c: (f(i, c), 0))
    return call(
        place_both_body,
        [
            (sds(lat_whole.shape, bf16), spec(lambda i, c: 1 - c[0])),
            (sds(src_whole.shape, bf16), spec(lambda i, c: (1 - c[0]) * (steps - 1) + jnp.maximum(i - 1, 0))),
        ],
        [spec(lambda i, c: i), ANY, ANY],
        (pos, other, lat_whole, src_whole),
        "place_both",
        grid=(steps,),
        prefetch=1,
        nbytes=4 * other.size,
        aliases={2: 0, 3: 1},
    )


def place_body(pos_ref, other_ref, whole_ref, out_ref):
    out_ref[...] = other_ref[...]


def place_other(pos, whole, other):
    half, width_d = other.shape
    rows = 256
    steps = half // rows
    return call(
        place_body,
        [(sds(whole.shape, bf16), pl.BlockSpec((rows, width_d), lambda i, c: ((1 - c[0]) * steps + i, 0)))],
        [pl.BlockSpec((rows, width_d), lambda i, c: (i, 0)), ANY],
        (pos, other, whole),
        "place_other",
        grid=(steps,),
        prefetch=1,
        nbytes=4 * half * width_d,
        aliases={2: 0},
    )[0]


def result_body(pos_ref, s_ref, r_ref, after_ref, half_ref, whole_ref, squares_ref):
    def step(r, held):
        result = after_ref[r, :] + (s_ref[r, :].astype(f32) + r_ref[r, :].astype(f32))
        half_ref[r, :] = result.astype(bf16)
        whole_ref[r, :] = result.astype(bf16)
        return held + folded(result * result)

    total = by_chunks(s_ref.shape[0], step, jnp.zeros((8, s_ref.shape[1]), f32))
    squares_ref[pl.ds(pl.program_id(0), 1), :] = jnp.sum(total, axis=0, keepdims=True)


def result_half(pos, s, r, after):
    half, width_d = s.shape
    steps = half // GROUP
    blk = pl.BlockSpec((GROUP, width_d), lambda i, c: (i, 0))
    own = pl.BlockSpec((GROUP, width_d), lambda i, c: (c[0] * steps + i, 0))
    return call(
        result_body,
        [
            (sds((half, width_d), bf16), blk),
            (sds((2 * half, width_d), bf16), own),
            (sds((steps, width_d), f32), pl.BlockSpec((steps, width_d), lambda i, c: (0, 0))),
        ],
        [blk] * 3,
        (pos, s, r, after),
        "result",
        grid=(steps,),
        prefetch=1,
        flops=6 * half * width_d,
        nbytes=5e6,
    )


def gains_body(
    pos_ref, clip_ref, frames_ref, keep, send, lat_ref, src_ref,
    self_ref, mlp_ref, squares_ref, out_ref, *, one_steps, src_steps, blocks, sets, copies, clips,
):
    i = pl.program_id(0)

    @pl.when(i == 0)
    def _():
        width_d = out_ref.shape[1]
        share = jnp.zeros((1, 1), f32)
        for b in range(blocks // 2):
            total = jnp.sum(squares_ref[b : b + 1, :], axis=1, keepdims=True)
            frames = frames_ref[clip_of(clip_ref, pos_ref, b, blocks, sets, True)].astype(f32)
            norm = jnp.sqrt(total / (GROUP * width_d) + 1e-06)
            share = share + norm / (jnp.broadcast_to(frames, (1, 1)) * (GROUPS_FRAME * clips))
        out_ref[0:2, :] = jnp.zeros((2, width_d), f32)
        out_ref[2:3, :] = self_ref[...] * copies
        out_ref[3:4, :] = mlp_ref[...] * copies
        out_ref[4:8, :] = jnp.broadcast_to(share * copies, (4, width_d))

    def add(row, v_ref, keep_ref, send_ref, kept):
        def step(r, held):
            n = jnp.where(kept, keep_ref[r, :].astype(f32), send_ref[r, :].astype(f32))
            return held + folded(n * centre(v_ref[r, :].astype(f32))[0])

        total = by_chunks(v_ref.shape[0], step, jnp.zeros((8, v_ref.shape[1]), f32))
        out_ref[row : row + 1, :] = out_ref[row : row + 1, :] + jnp.sum(total, axis=0, keepdims=True)

    pl.when(i < one_steps)(lambda: add(1, lat_ref, keep, send, i < one_steps // 2))
    pl.when(i >= one_steps)(lambda: add(0, src_ref, keep, send, i - one_steps < src_steps // 2))


def gains(pos, clips, frames, keep, send, latents, sources, self_gain, mlp_gain, squares, copies, ties):
    rows, width_d = latents.shape
    count = sources.shape[0]
    blk = 256
    one_steps, src_steps = rows // blk, count // blk
    one_half, src_half = one_steps // 2, src_steps // 2
    blocks = rows // GROUP
    sets = clips.shape[0] // GROUPS_FRAME // blocks
    clamp = lambda v, top: jnp.minimum(jnp.maximum(v, 0), top)
    spec = lambda f: pl.BlockSpec((blk, width_d), lambda i, *c: (f(i, c[0]), 0))
    fixed = lambda n: pl.BlockSpec((n, width_d), lambda i, *c: (0, 0))
    turn = lambda i, c, steps: (clamp(i, steps - 1) + c[0] * (steps // 2)) % steps
    kept = lambda i, c: jnp.where(
        i < one_steps, clamp(i, one_half - 1), one_half + clamp(i - one_steps, src_half - 1)
    )
    sent = lambda i, c: jnp.where(
        i < one_steps, clamp(i - one_half, one_half - 1), one_half + clamp(i - one_steps - src_half, src_half - 1)
    )
    return call(
        functools.partial(
            gains_body, one_steps=one_steps, src_steps=src_steps, blocks=blocks, sets=sets, copies=copies,
            clips=frames.shape[0],
        ),
        [(sds((8, width_d), f32), fixed(8))],
        [
            spec(kept),
            spec(sent),
            spec(lambda i, c: turn(i, c, one_steps)),
            spec(lambda i, c: turn(i - one_steps, c, src_steps)),
            fixed(1), fixed(1), fixed(blocks // 2),
        ],
        (pos, clips, frames, keep, send, latents, sources, self_gain, mlp_gain, squares),
        "gains",
        grid=(one_steps + src_steps,),
        prefetch=3,
        flops=20 * (rows + count) * width_d,
        nbytes=4 * (rows + count) * width_d,
        ties=ties,
    )[0]


def feature_grads_body(pos_ref, *refs, items, sends, blk):
    given = sum(a + b for a, b in items)
    keep_ref, send_refs = refs[given], refs[given + 1 :]
    at, column = 0, 0
    for lefts, rights in items:
        total, row = None, 0
        for k in range(lefts):
            left = refs[at + k]
            rows = left.shape[0]
            if rights == 1:
                right = refs[at + lefts][row : row + rows, :]
            else:
                right = refs[at + lefts + k][...]
            term = dot_ta(left[...], right)
            total = term if total is None else total + term
            row += rows
        at += lefts + rights
        first, column = column, column + total.shape[1]
        total = total.astype(bf16)
        for j in range(blk // 128):
            part = total[j * 128 : (j + 1) * 128]
            if sends == 0:
                keep_ref[j, :, first:column] = part
                continue
            mine = (pos_ref[1] + j) % 2 == 0

            @pl.when(mine)
            def _():
                keep_ref[j // 2, :, first:column] = part

            @pl.when(jnp.logical_not(mine))
            def _():
                width = send_refs[0].shape[2]
                for h, ref in enumerate(send_refs):
                    low, high = max(first, h * width), min(column, (h + 1) * width)
                    if low < high:
                        ref[j // 2, :, low - h * width : high - h * width] = part[:, low - first : high - first]


def feature_grads(pos, items, sends, ties=()):
    arrays, specs, counts, columns, flops = [], [], [], 0, 0
    features = items[0][0][0].shape[1]
    blk = 512
    for lefts, rights in items:
        counts.append((len(lefts), len(rights)))
        for v in lefts:
            arrays.append(v)
            specs.append(pl.BlockSpec((v.shape[0], blk), lambda i, c: (0, i)))
            flops += 2 * v.shape[0] * v.shape[1] * rights[0].shape[1]
        for v in rights:
            arrays.append(v)
            specs.append(pl.BlockSpec(v.shape, lambda i, c: (0, 0)))
        columns += rights[0].shape[1]
    steps = features // blk
    sets = features // 256 if sends else features // 128
    out = lambda n: (sds((sets, 128, n), bf16), pl.BlockSpec((sets // steps, 128, n), lambda i, c: (i, 0, 0)))
    return call(
        functools.partial(feature_grads_body, items=tuple(counts), sends=sends, blk=blk),
        [out(columns)] + [out(columns // sends)] * sends if sends else [out(columns)],
        specs,
        (pos, *arrays),
        "feature_grads",
        grid=(steps,),
        prefetch=1,
        flops=flops,
        nbytes=2 * features * columns + sum(2 * v.size for v in arrays),
        ties=ties,
    )


def stage_one_body(pos_ref, keep_ref, *refs):
    z = pos_ref[1] // 2
    gots, (own_ref, send_ref) = refs[:-2], refs[-2:]
    width = gots[0].shape[2]
    for h, got_ref in enumerate(gots):
        cols = slice(h * width, (h + 1) * width)
        for k in range(2):
            at = z ^ (2 * k)
            own_ref[k, :, cols] = keep_ref[at, :, cols].astype(f32) + got_ref[at].astype(f32)
            at = z ^ 1 ^ (2 * k)
            send_ref[k, :, cols] = (keep_ref[at, :, cols].astype(f32) + got_ref[at].astype(f32)).astype(bf16)


def stage_one(pos, keep, gots, ties=()):
    shape = (2, *keep.shape[1:])
    return call(
        stage_one_body,
        [(sds(shape, f32), VMEM), (sds(shape, bf16), VMEM)],
        [SMEM] + [VMEM] * (1 + len(gots)),
        (pos, keep, *gots),
        "stage_one",
        nbytes=4 * keep.size,
        ties=ties,
    )


def stage_two_body(keep_ref, got_ref, own_ref, send_ref):
    own_ref[...] = keep_ref[0] + got_ref[0].astype(f32)
    send_ref[...] = (keep_ref[1] + got_ref[1].astype(f32)).astype(bf16)


def stage_two(keep, got, ties=()):
    shape = keep.shape[1:]
    return call(
        stage_two_body,
        [(sds(shape, f32), VMEM), (sds(shape, bf16), VMEM)],
        [VMEM] * 2,
        (keep, got),
        "stage_two",
        nbytes=4 * keep.size,
        ties=ties,
    )


def stage_end_body(own_ref, got_ref, *outs, turned):
    total = own_ref[...] + got_ref[...].astype(f32)
    width = total.shape[1] // len(outs)
    for k, ref in enumerate(outs):
        part = total[:, k * width : (k + 1) * width]
        ref[...] = part.T if k in turned else part


def stage_end(own, got, parts, turned, ties=()):
    blk = own.shape
    width = blk[1] // parts
    return call(
        functools.partial(stage_end_body, turned=turned),
        [(sds((width, blk[0]) if k in turned else (blk[0], width), f32), VMEM) for k in range(parts)],
        [VMEM] * 2,
        (own, got),
        "stage_end",
        nbytes=10 * blk[0] * blk[1],
        ties=ties,
    )


def flip_x(v):
    return lax.ppermute(v, "seq", xor_pairs(1, 8))


def near_z(v):
    return lax.ppermute(v, "seq", xor_pairs(2, 8))


def far_z(v):
    return lax.ppermute(v, "seq", xor_pairs(4, 8))


def scatter_whole(pos, items, parts, turned, ties):
    whole = feature_grads(pos, items, 0, ties)[0]
    whole = whole.reshape(-1, whole.shape[2])
    total = lax.psum_scatter(whole, "seq", scatter_dimension=0, tiled=True).astype(f32)
    width = total.shape[1] // parts
    pieces = [total[:, k * width : (k + 1) * width] for k in range(parts)]
    return [piece.T if k in turned else piece for k, piece in enumerate(pieces)]


def tied(values, other):
    out = lax.optimization_barrier((other, *values))
    return list(out[1:]), out[0]


def cross_back_body(
    pos_ref, mine_ref, other_ref, wo_ref, q_ref, kvp_ref, idx_ref, wq_ref, wk_ref, wv_ref,
    dq_ref, dk_ref, dv_ref, keep_ref, send_ref, dkvp_s, *, blocks,
):
    width = wq_ref.shape[1]
    heads = width // HEAD
    count = kvp_ref.shape[0]
    scale = HEAD ** (-0.5)
    for b in range(blocks):
        ref = mine_ref if b < blocks // 2 else other_ref
        part = (b % (blocks // 2)) * GROUP
        grad = dot_t(ref[part : part + GROUP, :], wo_ref[...]).astype(bf16)
        for h in range(heads):
            cols = slice(h * HEAD, (h + 1) * HEAD)
            vcols = slice(width + h * HEAD, width + (h + 1) * HEAD)
            q = q_ref[b * GROUP : (b + 1) * GROUP, cols]
            k = kvp_ref[b * SRC : (b + 1) * SRC, cols]
            v = kvp_ref[b * SRC : (b + 1) * SRC, vcols]
            do = grad[:, cols]
            s = dot_t(q, k) * (scale * LOG2E)
            p = jnp.exp2(s - jnp.max(s, axis=-1, keepdims=True))
            p = p / jnp.sum(p, axis=-1, keepdims=True)
            dp = dot_t(do, v)
            delta = jnp.sum(p * dp, axis=-1, keepdims=True)
            ds = (p * (dp - delta) * scale).astype(bf16)
            dq_ref[b * GROUP : (b + 1) * GROUP, cols] = dot(ds, k).astype(bf16)
            dkvp_s[b * SRC : (b + 1) * SRC, cols] = dot_ta(ds, q).astype(bf16)
            dkvp_s[b * SRC : (b + 1) * SRC, vcols] = dot_ta(p.astype(bf16), do).astype(bf16)
        one = dot_t(dq_ref[b * GROUP : (b + 1) * GROUP, :], wq_ref[...]).astype(bf16)
        if b < blocks // 2:
            keep_ref[part : part + GROUP, :] = one
        else:
            send_ref[part : part + GROUP, :] = one
    half = count // 2
    blk = 256
    row = jnp.concatenate([index_row(idx_ref, pos_ref, b, blocks, count) for b in range(blocks)], axis=1)
    for n in range(count // blk):
        r0 = pl.multiple_of(
            (pos_ref[0] if n * blk < half else 1 - pos_ref[0]) * half + (n * blk) % half, blk
        )
        wanted = lax.broadcasted_iota(jnp.int32, (blk, count), 0).astype(f32) + r0.astype(f32)
        picks = jnp.where(row == wanted, 1.0, 0.0).astype(bf16)
        dkv = dot(picks, dkvp_s[...]).astype(bf16)
        dk_ref[pl.ds(r0, blk), :] = dkv[:, 0:width]
        dv_ref[pl.ds(r0, blk), :] = dkv[:, width:]
        total = (dot_t(dkv[:, 0:width], wk_ref[...]) + dot_t(dkv[:, width:], wv_ref[...])).astype(bf16)
        at = blocks // 2 * GROUP + (n * blk) % half
        if n * blk < half:
            keep_ref[at : at + blk, :] = total
        else:
            send_ref[at : at + blk, :] = total


def cross_back(pos, mine, other, wo, q, kvp, idx, wq, wk, wv, ties):
    rows, width = q.shape
    width_d = wq.shape[0]
    count = kvp.shape[0]
    blocks = rows // GROUP
    return call(
        functools.partial(cross_back_body, blocks=blocks),
        [
            (sds((rows, width), bf16), VMEM),
            (sds((count, width), bf16), VMEM),
            (sds((count, width), bf16), VMEM),
            (sds(((rows + count) // 2, width_d), bf16), VMEM),
            (sds(((rows + count) // 2, width_d), bf16), VMEM),
        ],
        [SMEM] + [VMEM] * 9,
        (pos, mine, other, wo, q, kvp, idx, wq, wk, wv),
        "cross_back",
        ties=ties,
        scratch=[pltpu.VMEM((count, 2 * width), bf16)],
        flops=4e9,
        nbytes=12e6,
    )


def xor_pairs(bit, size):
    return [(i, i ^ bit) for i in range(size)]


def ring_pairs(d):
    return [(s, ((s // 2 + d) % 4) * 2 + s % 2) for s in range(8)]


def tensor_swap(x, bit):
    return lax.ppermute(x, "tensor", xor_pairs(bit, lax.axis_size("tensor")))


def seq_gather(x, between=None):
    size = lax.axis_size("seq")
    if size == 8:
        move = lambda v, pairs: lax.ppermute(v, "seq", pairs)
        flip = xor_pairs(1, 8)
        beside = move(x, flip)
        up = move(x, ring_pairs(1))
        down = move(x, ring_pairs(-1))
        if between is not None:
            (beside, up), between = tied([beside, up], between)
        far = move(up, ring_pairs(1))
        up_beside = move(up, flip)
        down_beside = move(beside, ring_pairs(-1))
        far_beside = move(far, flip)
        pieces = [x, beside, up, down, far, up_beside, down_beside, far_beside]
    else:
        pieces = gather_whole(x)
    return pieces if between is None else (pieces, between)


def gather_whole(x):
    return [lax.all_gather(x, "seq", axis=0, tiled=True)]


def gather_entries(size, rows, sets):
    if size == 8:
        return tuple((k, 0, 0, k) for k in range(8))
    return whole_entries(size, rows, sets)


def whole_entries(size, rows, sets):
    return tuple((0, s * rows, s % sets, s // sets) for s in range(size))


def half_sum(keep, send):
    size = lax.axis_size("tensor")
    got = tensor_swap(send, 1)
    own = (keep.astype(f32) + got.astype(f32)).astype(bf16)
    bit = 2
    while True:
        other = tensor_swap(own, bit)
        if bit * 2 >= size:
            return own, other
        own = (own.astype(f32) + other.astype(f32)).astype(bf16)
        bit *= 2


def tensor_pieces(keep, send):
    size = lax.axis_size("tensor")
    return [keep if k == 0 else tensor_swap(send if k % 2 else keep, k) for k in range(size)]


def weight_far(weight):
    pieces = {0: weight}
    bit = lax.axis_size("tensor") // 2
    while bit >= 2:
        pieces.update({k + bit: tensor_swap(v, bit) for k, v in list(pieces.items())})
        bit //= 2
    return pieces


def weight_pieces(pieces):
    pieces = dict(pieces)
    pieces.update({k + 1: tensor_swap(v, 1) for k, v in list(pieces.items())})
    return [pieces[k] for k in range(len(pieces))]


def tie_all(pieces, other):
    keys = sorted(pieces)
    tied = lax.optimization_barrier((other, *[pieces[k] for k in keys]))
    return dict(zip(keys, tied[1:])), tied[0]


def sum_over(v, axis, only):
    size = lax.axis_size(axis)
    bit = only or 1
    while bit < size:
        v = v + lax.ppermute(v, axis, xor_pairs(bit, size))
        bit = size if only else bit * 2
    return v


def local(
    latents, sources, source_index, block_clip, clip_frames, norm_src, norm_cross, norm_self, norm_mlp,
    cross_q, cross_k, cross_v, cross_o, self_q, self_k, self_v, self_o, mlp_in, mlp_out, out_grad,
):
    rows, width_d = latents.shape
    blocks = rows // GROUP
    width = cross_q.shape[1]
    units = mlp_in.shape[1]
    tensor_size, seq_size = lax.axis_size("tensor"), lax.axis_size("seq")
    core = lax.axis_index("tensor") % 2
    pos = jnp.stack((core, lax.axis_index("seq"), lax.axis_index("tensor"))).astype(jnp.int32)
    sets = block_clip.shape[0] // GROUPS_FRAME // blocks
    gain = lambda g: g.reshape(1, width_d)
    kv_entries = gather_entries(seq_size, rows, sets)
    out_entries = gather_entries(seq_size, rows + 2 * EXTRA, sets)

    cross_o_far = weight_far(cross_o)
    normed_one, normed_src, cross_query, cross_kv, mixed_keep, mixed_send = cross_forward(
        pos, source_index, latents, sources, gain(norm_cross), gain(norm_src), cross_q, cross_k, cross_v
    )
    cross_o_far, mixed_keep = tie_all(cross_o_far, mixed_keep)
    after_cross, two_mine = project(
        pos, tensor_pieces(mixed_keep, mixed_send), weight_pieces(cross_o_far), latents, gain(norm_self), True
    )
    two_other = tensor_swap(two_mine, 1)
    query, key_value = qkv(two_mine, two_other, self_q, self_k, self_v)
    kv_pieces = seq_gather(key_value)
    self_o_tied, two_mine = tie_all({0: self_o}, two_mine)
    self_o_all = weight_pieces(weight_far(self_o_tied[0]))
    out_rel, act_grad = act_back(pos, out_grad, mlp_out)
    split = seq_size == 8
    query_pieces = seq_gather(query)
    self_keep, self_send, lse_rows, lse_columns = attend(
        pos, block_clip, query, kv_pieces, kv_entries, (act_grad, *self_o_all[1:])
    )
    after_self, three_mine = project(
        pos, tensor_pieces(self_keep, self_send), self_o_all, after_cross, gain(norm_mlp), False,
        query_pieces[1:4],
    )
    three_other = tensor_swap(three_mine, 1)
    activated, hidden_grad, three_keep, three_send = mlp(three_mine, three_other, mlp_in, act_grad)

    three_sum, three_got = half_sum(three_keep, three_send)
    in_items = (((three_mine, three_other), (hidden_grad,)),)
    out_items = (((out_rel,), (activated,)),)
    early = ()
    if split:
        in_keep, in_send = feature_grads(pos, in_items, 1, (three_sum,))
        out_keep, out_send_a, out_send_b = feature_grads(pos, out_items, 2, (in_keep,))
        early = (out_keep, *query_pieces[4:])
    down_keep, down_send = mlp_down(activated, mlp_out, (three_sum, *early[0:1]))
    early = (*early, down_keep)
    after_self_grad, self_branch, mlp_gain = norm_back(
        three_sum, three_got, after_self, gain(norm_mlp), out_rel, early
    )
    self_branch_other = tensor_swap(self_branch, 1)

    out_more, delta_columns = out_back(self_branch, self_branch_other, self_o, self_keep, self_send, lse_rows)
    if split:
        in_got = flip_x(in_send)
    self_query_grad = query_back(
        pos, block_clip, query, out_more, lse_columns, delta_columns, kv_pieces, kv_entries
    )
    out_pieces, self_query_grad = seq_gather(out_more, self_query_grad)
    result_sum, result_got = half_sum(down_keep, down_send)
    output_half, output_whole, squares = result_half(pos, result_sum, result_got, after_self)
    output = place_other(pos, output_whole, tensor_swap(output_half, 1))
    early = ()
    if split:
        in_keep, in_send = stage_one(pos, in_keep, [in_got])
        (out_send_a, in_send), out_pieces[-1] = tied([out_send_a, in_send], out_pieces[-1])
        out_got_a = flip_x(out_send_a)
        early = (squares,)
    self_grads, two_keep, two_send = key_back(
        pos, block_clip, key_value, self_query_grad, self_q, self_k, self_v,
        query_pieces, kv_entries, out_pieces, out_entries, early,
    )
    if split:
        (two_send, out_send_b), out_got_a = tied([two_send, out_send_b], out_got_a)
        out_got_b = flip_x(out_send_b)
        in_got = near_z(in_send)
    two_sum, two_got = half_sum(two_keep, two_send)
    self_items = (
        ((two_mine, two_other), (self_grads,)),
        ((self_branch, self_branch_other), (self_keep, self_send)),
    )
    early = ()
    if split:
        self_wkeep, self_send_a, self_send_b = feature_grads(pos, self_items, 2, (two_sum,))
        in_own, in_send = stage_two(in_keep, in_got, (two_sum,))
        out_keep, out_send = stage_one(pos, out_keep, [out_got_a, out_got_b], (in_send,))
        early = (self_wkeep, in_own, out_keep, output)
    after_cross_grad, cross_branch, self_gain = norm_back(
        two_sum, two_got, after_cross, gain(norm_self), after_self_grad, early
    )
    cross_branch_other = tensor_swap(cross_branch, 1)

    if split:
        (self_send_a, in_send), cross_branch_other = tied([self_send_a, in_send], cross_branch_other)
        self_got_a = flip_x(self_send_a)
        in_got = far_z(in_send)
    cross_query_grad, cross_key_grad, cross_value_grad, both_keep, both_send = cross_back(
        pos, cross_branch, cross_branch_other, cross_o, cross_query, cross_kv, source_index,
        cross_q, cross_k, cross_v, (),
    )
    first_items = (((normed_one,), (cross_query_grad,)), ((normed_src,), (cross_key_grad,)))
    second_items = (
        ((normed_src,), (cross_value_grad,)),
        ((cross_branch, cross_branch_other), (mixed_keep, mixed_send)),
    )
    gains_of = lambda ties: gains(
        pos, block_clip, clip_frames, both_keep, both_send, latents, sources,
        self_gain, mlp_gain, squares, 2.0 / tensor_size, ties,
    )
    final_of = lambda ties: final_norm(
        pos, both_sum, both_got, latents, sources, gain(norm_cross), gain(norm_src), after_cross_grad, ties
    )
    if split:
        both_send, self_send_b, out_send, self_got_a, in_got = lax.optimization_barrier(
            (both_send, self_send_b, out_send, self_got_a, in_got)
        )
        self_got_b = flip_x(self_send_b)
        out_got = near_z(out_send)
        both_sum, both_got = half_sum(both_keep, both_send)
        small = gains_of((both_sum,))
        first_keep, first_send = feature_grads(pos, first_items, 1, (small,))
        second_keep, second_send = feature_grads(pos, second_items, 1, (first_keep,))
        out_own, out_send = stage_two(out_keep, out_got, (second_keep,))
        self_wkeep, self_wsend = stage_one(pos, self_wkeep, [self_got_a, self_got_b], (out_own,))

        first_send, out_send, self_wsend, small = lax.optimization_barrier((first_send, out_send, self_wsend, small))
        first_got = flip_x(first_send)
        out_got = far_z(out_send)
        self_wgot = near_z(self_wsend)
        small = sum_over(sum_over(small, "tensor", 1), "seq", 1)
        first_keep, first_send = stage_one(pos, first_keep, [first_got], (out_got, small))
        self_own, self_wsend = stage_two(self_wkeep, self_wgot, (first_keep,))

        second_send, first_send, self_wsend, small = lax.optimization_barrier(
            (second_send, first_send, self_wsend, small)
        )
        second_got = flip_x(second_send)
        first_got = near_z(first_send)
        self_wgot = far_z(self_wsend)
        small = sum_over(small, "seq", 2)
        both_half, lat_whole, src_whole = final_of(())
        second_keep, second_send = stage_one(pos, second_keep, [second_got], (self_wgot, small))
        first_own, first_send = stage_two(first_keep, first_got, (second_keep,))

        second_send, first_send, small, both_half = lax.optimization_barrier(
            (second_send, first_send, small, both_half)
        )
        second_got = near_z(second_send)
        first_got = far_z(first_send)
        small = sum_over(small, "seq", 4)
        both_other = tensor_swap(both_half, 1)
        second_own, second_send = stage_two(second_keep, second_got, (first_got, small))

        second_send, both_other, small = lax.optimization_barrier((second_send, both_other, small))
        second_got = far_z(second_send)
        bit = 2
        while bit < tensor_size:
            small = sum_over(small, "tensor", bit)
            bit *= 2
        latents_grad, sources_grad = place_both(pos, both_other, lat_whole, src_whole)
        mlp_outs = [stage_end(in_own, in_got, 1, ())[0], stage_end(out_own, out_got, 1, (0,))[0]]
        self_outs = stage_end(self_own, self_wgot, 4, (3,))
        cross_outs = [*stage_end(first_own, first_got, 2, ()), *stage_end(second_own, second_got, 2, (1,))]
    else:
        both_sum, both_got = half_sum(both_keep, both_send)
        small = gains_of((both_sum,))
        small = sum_over(small, "tensor", 0)
        small = sum_over(small, "seq", 0)
        both_half, lat_whole, src_whole = final_of(())
        latents_grad, sources_grad = place_both(pos, tensor_swap(both_half, 1), lat_whole, src_whole)
        cross_outs = scatter_whole(pos, first_items, 2, (), ()) + scatter_whole(pos, second_items, 2, (1,), ())
        self_outs = scatter_whole(pos, self_items, 4, (3,), ())
        mlp_outs = scatter_whole(pos, in_items, 1, (), ()) + scatter_whole(pos, out_items, 1, (0,), ())
    return (
        output, latents_grad, sources_grad, small[0], small[1], small[2], small[3],
        *cross_outs, *self_outs, *mlp_outs, small[4, 0],
    )


def solution(mesh):
    in_specs = (
        P("seq", None), P("seq", None), P("seq", None), P(), P(), P(), P(), P(), P(),
        P(None, "tensor"), P(None, "tensor"), P(None, "tensor"), P("tensor", None),
        P(None, "tensor"), P(None, "tensor"), P(None, "tensor"), P("tensor", None),
        P(None, "tensor"), P("tensor", None), P("seq", None),
    )
    out_specs = (
        P("seq", None), P("seq", None), P("seq", None), P(), P(), P(), P(),
        P("seq", "tensor"), P("seq", "tensor"), P("seq", "tensor"), P("tensor", "seq"),
        P("seq", "tensor"), P("seq", "tensor"), P("seq", "tensor"), P("tensor", "seq"),
        P("seq", "tensor"), P("tensor", "seq"), P(),
    )
    return jax.shard_map(local, mesh=mesh, in_specs=in_specs, out_specs=out_specs, check_vma=False)
```

```python
import functools
import math

import jax
import jax.numpy as jnp
from jax import lax
from jax.experimental import pallas as pl
from jax.experimental.pallas import tpu as pltpu
from jax.sharding import PartitionSpec as P

HEAD = 128
GROUP = 128
SRC = 256
GROUPS_FRAME = 8
LOG2E = 1.4426950408889634
epsilon = 1e-05
masked_value = -1e30
bf16 = jnp.bfloat16
f32 = jnp.float32
EXTRA = 16
WEIGHT = 1

VMEM = pl.BlockSpec(memory_space=pltpu.VMEM)
SMEM = pl.BlockSpec(memory_space=pltpu.SMEM)


def sds(shape, dtype):
    return jax.ShapeDtypeStruct(shape, dtype)


def dot(a, b):
    return lax.dot_general(a, b, (((1,), (0,)), ((), ())), preferred_element_type=f32)


def dot_t(a, b):
    return lax.dot_general(a, b, (((1,), (1,)), ((), ())), preferred_element_type=f32)


def dot_ta(a, b):
    return lax.dot_general(a, b, (((0,), (0,)), ((), ())), preferred_element_type=f32)


def centre(values):
    centred = values - jnp.mean(values, axis=-1, keepdims=True)
    variance = jnp.mean(centred * centred, axis=-1, keepdims=True)
    inverse = lax.rsqrt(variance + epsilon)
    return centred * inverse, inverse


ANY = pl.BlockSpec(memory_space=pl.ANY)
CHUNK = 64


def by_chunks(rows, step, carry=0):
    for first in range(0, rows, CHUNK):
        carry = step(slice(first, first + CHUNK), carry)
    return carry


def norm_into(out_ref, in_ref, gain_ref):
    gain_vec = gain_ref[...]

    def step(r, held):
        out_ref[r, :] = (centre(in_ref[r, :].astype(f32))[0] * gain_vec).astype(bf16)
        return held

    by_chunks(in_ref.shape[0], step)


def folded(rows_value):
    parts = [rows_value[k : k + 8] for k in range(0, CHUNK, 8)]
    while len(parts) > 1:
        parts = [parts[k] + parts[k + 1] for k in range(0, len(parts), 2)]
    return parts[0]


def call(
    body, outs, ins, args, name, scratch=(), grid=None, prefetch=0, flops=0, nbytes=0, trans=0, ties=(), aliases=None,
    spare=6,
):
    given = prefetch + len(ins)
    room = 0
    for spec, v in [*zip(ins, args[prefetch:]), *[(spec, shape) for shape, spec in outs]]:
        if spec.block_shape is not None:
            room += 2 * math.prod(spec.block_shape) * v.dtype.itemsize
        elif spec is VMEM:
            room += math.prod(v.shape) * v.dtype.itemsize
    room += sum(math.prod(v.shape) * jnp.dtype(v.dtype).itemsize for v in scratch)

    def run(*refs):
        body(*refs[:given], *refs[given + len(ties) :])

    return pl.pallas_call(
        run,
        out_shape=[shape for shape, ignored in outs],
        grid_spec=pltpu.PrefetchScalarGridSpec(
            num_scalar_prefetch=prefetch,
            grid=() if grid is None else grid,
            in_specs=list(ins) + [ANY] * len(ties),
            out_specs=[spec for ignored, spec in outs],
            scratch_shapes=list(scratch),
        ),
        compiler_params=pltpu.CompilerParams(vmem_limit_bytes=room + spare * 2**20),
        cost_estimate=pl.CostEstimate(
            flops=int(flops * WEIGHT), bytes_accessed=int(nbytes * WEIGHT), transcendentals=int(trans * WEIGHT)
        ),
        input_output_aliases=aliases or {},
        name=name,
    )(*args, *ties)


def index_row(idx_ref, pos_ref, b, blocks, count):
    at = (b + pos_ref[0] * (blocks // 2)) % blocks
    return (idx_ref[pl.ds(at, 1), :] - pos_ref[1] * count).astype(f32)


def clip_of(clip_ref, pos_ref, b, blocks, sets, own):
    half = blocks // 2
    if own:
        return clip_ref[blocks * (pos_ref[1] % sets) + (b + pos_ref[0] * half) % blocks]
    return clip_ref[blocks * (b // blocks) + (b % blocks + pos_ref[0] * half) % blocks]


def cross_forward_body(
    pos_ref, idx_ref, lat_ref, src_ref, gain_one_ref, gain_src_ref, wq_ref, wk_ref, wv_ref,
    n1_ref, ns_ref, q_ref, kvp_ref, keep_ref, send_ref, kv_s, *, steps,
):
    i = pl.program_id(0)
    width = wq_ref.shape[1]
    heads = width // HEAD
    rows_src = src_ref.shape[0]
    norm_into(ns_ref, src_ref, gain_src_ref)
    normed_src = ns_ref[...]
    row0 = pl.multiple_of(i * rows_src, rows_src)
    kv_s[pl.ds(row0, rows_src), 0:width] = dot(normed_src, wk_ref[...]).astype(bf16)
    kv_s[pl.ds(row0, rows_src), width:] = dot(normed_src, wv_ref[...]).astype(bf16)
    norm_into(n1_ref, lat_ref, gain_one_ref)
    normed_one = n1_ref[...]
    grp0 = pl.multiple_of(i * GROUP, GROUP)
    q_ref[pl.ds(grp0, GROUP), :] = dot(normed_one, wq_ref[...]).astype(bf16)

    @pl.when(i == steps - 1)
    def _():
        count = kv_s.shape[0]
        lanes = lax.broadcasted_iota(jnp.int32, (128, count), 1).astype(f32)
        for b in range(steps):
            for part in range(SRC // 128):
                row = index_row(idx_ref, pos_ref, b, steps, count)[:, part * 128 : (part + 1) * 128]
                column = jnp.transpose(jnp.broadcast_to(row, (128, 128)))
                picks = jnp.where(jnp.tile(column, (1, count // 128)) == lanes, 1.0, 0.0).astype(bf16)
                r0 = b * SRC + part * 128
                kvp_ref[r0 : r0 + 128, :] = dot(picks, kv_s[...]).astype(bf16)
        for b in range(steps):
            for h in range(heads):
                cols = slice(h * HEAD, (h + 1) * HEAD)
                q = q_ref[b * GROUP : (b + 1) * GROUP, cols]
                k = kvp_ref[b * SRC : (b + 1) * SRC, cols]
                v = kvp_ref[b * SRC : (b + 1) * SRC, width + h * HEAD : width + (h + 1) * HEAD]
                s = dot_t(q, k) * (HEAD ** (-0.5) * LOG2E)
                p = jnp.exp2(s - jnp.max(s, axis=-1, keepdims=True))
                total = jnp.sum(p, axis=-1, keepdims=True)
                mixed = (dot(p.astype(bf16), v) / total).astype(bf16)
                if b < steps // 2:
                    keep_ref[b * GROUP : (b + 1) * GROUP, cols] = mixed
                else:
                    r0 = (b - steps // 2) * GROUP
                    send_ref[r0 : r0 + GROUP, cols] = mixed


def cross_forward(pos, idx, latents, sources, gain_one, gain_src, wq, wk, wv):
    rows, width_d = latents.shape
    steps = rows // GROUP
    count = sources.shape[0]
    blk = count // steps
    width = wq.shape[1]
    whole = lambda shape: pl.BlockSpec(shape, lambda i, c: (0,) * len(shape))
    return call(
        functools.partial(cross_forward_body, steps=steps),
        [
            (sds((rows, width_d), bf16), pl.BlockSpec((GROUP, width_d), lambda i, c: (i, 0))),
            (sds((count, width_d), bf16), pl.BlockSpec((blk, width_d), lambda i, c: (i, 0))),
            (sds((rows, width), bf16), whole((rows, width))),
            (sds((count, 2 * width), bf16), whole((count, 2 * width))),
            (sds((rows // 2, width), bf16), whole((rows // 2, width))),
            (sds((rows // 2, width), bf16), whole((rows // 2, width))),
        ],
        [
            whole(idx.shape),
            pl.BlockSpec((GROUP, width_d), lambda i, c: ((i + c[0] * (steps // 2)) % steps, 0)),
            pl.BlockSpec((blk, width_d), lambda i, c: (i, 0)),
            whole((1, width_d)),
            whole((1, width_d)),
            whole(wq.shape),
            whole(wk.shape),
            whole(wv.shape),
        ],
        (pos, idx, latents, sources, gain_one, gain_src, wq, wk, wv),
        "cross_forward",
        scratch=[pltpu.VMEM((count, 2 * width), bf16)],
        grid=(steps,),
        prefetch=1,
        flops=4e9,
        nbytes=12e6,
        spare=44,
    )


def project_body(pos_ref, *refs, parts, own_half):
    pieces, weights = refs[:parts], refs[parts : 2 * parts]
    base_ref, gain_ref, after_ref, normed_ref, left_s, right_s = refs[2 * parts :]
    half = after_ref.shape[0]
    width = pieces[0].shape[1]
    for k in range(parts):
        at = pl.multiple_of((pos_ref[2] ^ k) * width, width)
        left_s[:, pl.ds(at, width)] = pieces[k][...]
        right_s[pl.ds(at, width), :] = weights[k][...]
    after_ref[...] = dot(left_s[...], right_s[...])
    first = pos_ref[0] * half if own_half else 0
    gain_vec = gain_ref[...]

    def step(r, held):
        base = base_ref[pl.ds(pl.multiple_of(first + r.start, CHUNK), CHUNK), :]
        after = base.astype(f32) + after_ref[r, :]
        after_ref[r, :] = after
        normed_ref[r, :] = (centre(after)[0] * gain_vec).astype(bf16)
        return held

    by_chunks(half, step)


def project(pos, pieces, weights, base, gain, own_half, ties=()):
    parts = len(pieces)
    half, width = pieces[0].shape
    width_d = weights[0].shape[1]
    return call(
        functools.partial(project_body, parts=parts, own_half=own_half),
        [(sds((half, width_d), f32), VMEM), (sds((half, width_d), bf16), VMEM)],
        [SMEM] + [VMEM] * (2 * parts + 2),
        (pos, *pieces, *weights, base, gain),
        "project",
        scratch=[pltpu.VMEM((half, parts * width), bf16), pltpu.VMEM((parts * width, width_d), bf16)],
        flops=2 * half * width * parts * width_d,
        nbytes=5e6,
        ties=ties,
    )


def qkv_body(mine_ref, other_ref, wq_ref, wk_ref, wv_ref, q_ref, kv_ref):
    half = mine_ref.shape[0]
    width = wq_ref.shape[1]
    for part, ref in enumerate((mine_ref, other_ref)):
        rows = slice(part * half, (part + 1) * half)
        x = ref[...]
        kv_ref[rows, 0:width] = dot(x, wk_ref[...]).astype(bf16)
        kv_ref[rows, width:] = dot(x, wv_ref[...]).astype(bf16)
        q_ref[rows, :] = dot(x, wq_ref[...]).astype(bf16)


def qkv(mine, other, wq, wk, wv):
    half, width_d = mine.shape
    width = wq.shape[1]
    return call(
        qkv_body,
        [(sds((2 * half, width), bf16), VMEM), (sds((2 * half, 2 * width), bf16), VMEM)],
        [VMEM] * 5,
        (mine, other, wq, wk, wv),
        "qkv",
        flops=2 * 2 * half * width_d * 3 * width,
        nbytes=4e6,
    )


def assemble(refs, entries, dst, rows_blocks):
    for ri, base, p, k in entries:
        for j in range(rows_blocks):
            dst[p * rows_blocks + j, pl.ds(place_start(k), GROUP), :] = refs[ri][
                base + j * GROUP : base + (j + 1) * GROUP, :
            ]


def place_start(k):
    return k * GROUP if isinstance(k, int) else pl.multiple_of(k * GROUP, GROUP)


def split_rows(rows_value):
    high = rows_value.astype(bf16)
    rest = rows_value - high.astype(f32)
    middle = rest.astype(bf16)
    low = (rest - middle.astype(f32)).astype(bf16)
    return high, middle, low


def pack_extra(row_tiles, heads, blocks, width):
    per_row = width // 128
    out = []
    for h in range(heads):
        flat = [
            jnp.concatenate(row_tiles[h][r * per_row : (r + 1) * per_row], axis=1)
            for r in range(blocks // per_row)
        ]
        rows_value = jnp.concatenate(flat, axis=0)
        out += [part.astype(f32) for part in split_rows(rows_value)]
    used = heads * 3 * (blocks // per_row)
    if used < EXTRA:
        out.append(jnp.zeros((EXTRA - used, width), f32))
    return jnp.concatenate(out, axis=0).astype(bf16)


def unpack_extra(extra, h, j, blocks, width):
    per_row = width // 128
    rows_per = blocks // per_row
    row, lane = j // per_row, (j % per_row) * 128
    parts = [
        extra[(h * 3 + t) * rows_per + row : (h * 3 + t) * rows_per + row + 1, lane : lane + 128]
        for t in range(3)
    ]
    return (parts[0] + parts[1]) + parts[2]


def attend_body(
    pos_ref, clip_ref, *refs, pieces, entries, heads, blocks, period,
):
    q_ref = refs[0]
    kv_refs = refs[1 : 1 + pieces]
    keep_ref, send_ref, lsex_ref, lsec_ref, kv_s, m_s, l_s, acc_s, row_s, o_s = refs[1 + pieces :]
    width = heads * HEAD
    sets = period // blocks
    assemble(kv_refs, entries, kv_s, blocks)

    def per_block(i, carry):
        r0 = pl.multiple_of(i * GROUP, GROUP)
        own_clip = clip_of(clip_ref, pos_ref, i, blocks, sets, True)
        m_s[...] = jnp.full(m_s.shape, masked_value, f32)
        l_s[...] = jnp.zeros(l_s.shape, f32)
        acc_s[...] = jnp.zeros(acc_s.shape, f32)

        def per_keys(g, inner):
            @pl.when(own_clip == clip_of(clip_ref, pos_ref, g, blocks, sets, False))
            def _():
                for h in range(heads):
                    cols = slice(h * HEAD, (h + 1) * HEAD)
                    q = q_ref[pl.ds(r0, GROUP), cols]
                    k = kv_s[g, :, cols]
                    v = kv_s[g, :, width + h * HEAD : width + (h + 1) * HEAD]
                    s = dot_t(q, k) * (HEAD ** (-0.5) * LOG2E)
                    m_old = m_s[h][:, 0:1]
                    m_new = jnp.maximum(m_old, jnp.max(s, axis=-1, keepdims=True))
                    p = jnp.exp2(s - m_new)
                    alpha = jnp.exp2(m_old - m_new)
                    l_new = l_s[h][:, 0:1] * alpha + jnp.sum(p, axis=-1, keepdims=True)
                    acc_s[h] = acc_s[h] * alpha + dot(p.astype(bf16), v)
                    m_s[h] = jnp.broadcast_to(m_new, (GROUP, 128))
                    l_s[h] = jnp.broadcast_to(l_new, (GROUP, 128))

            return inner

        lax.fori_loop(0, period, per_keys, 0)
        for h in range(heads):
            total = l_s[h]
            o_s[pl.ds(r0, GROUP), h * HEAD : (h + 1) * HEAD] = (acc_s[h] / total).astype(bf16)
            lse = m_s[h] + jnp.log2(total)
            lsec_ref[h, pl.ds(r0, GROUP), :] = lse
            row_s[h, i] = jnp.transpose(lse)[0:8]
        return carry

    lax.fori_loop(0, blocks, per_block, 0)
    half = blocks // 2 * GROUP
    keep_ref[...] = o_s[0:half, :]
    send_ref[...] = o_s[half:, :]
    tiles = [[row_s[h, j][0:1] for j in range(blocks)] for h in range(heads)]
    lsex_ref[...] = pack_extra(tiles, heads, blocks, width)


def attend(pos, clips, q, kv_pieces, entries, ties):
    rows, width = q.shape
    heads, blocks, period = width // HEAD, rows // GROUP, clips.shape[0] // GROUPS_FRAME
    pieces = len(kv_pieces)
    body = functools.partial(
        attend_body, pieces=pieces, entries=entries, heads=heads, blocks=blocks, period=period
    )
    return call(
        body,
        [
            (sds((rows // 2, width), bf16), VMEM),
            (sds((rows // 2, width), bf16), VMEM),
            (sds((EXTRA, width), bf16), VMEM),
            (sds((heads, rows, 128), f32), VMEM),
        ],
        [SMEM, SMEM] + [VMEM] * (1 + pieces),
        (pos, clips, q, *kv_pieces),
        "attend",
        ties=ties,
        scratch=[
            pltpu.VMEM((period, GROUPS_FRAME * GROUP, 2 * width), bf16),
            pltpu.VMEM((heads, GROUP, 128), f32),
            pltpu.VMEM((heads, GROUP, 128), f32),
            pltpu.VMEM((heads, GROUP, HEAD), f32),
            pltpu.VMEM((heads, blocks, 8, 128), f32),
            pltpu.VMEM((rows, width), bf16),
        ],
        flops=2e9,
        nbytes=7e6,
        trans=2e6,
    )


def out_back_body(mine_ref, other_ref, wo_ref, okeep_ref, osend_ref, lsex_ref, dox_ref, dc_ref, *, heads, blocks):
    half = mine_ref.shape[0]
    rows = 2 * half
    tiles = [[] for h in range(heads)]
    for part, (ref, o_ref) in enumerate(((mine_ref, okeep_ref), (other_ref, osend_ref))):
        grad = dot_t(ref[...], wo_ref[...]).astype(bf16)
        dox_ref[part * half : (part + 1) * half, :] = grad
        product = grad.astype(f32) * o_ref[...].astype(f32)
        for h in range(heads):
            delta = jnp.sum(product[:, h * HEAD : (h + 1) * HEAD], axis=-1, keepdims=True)
            delta = jnp.broadcast_to(delta, (half, 128))
            dc_ref[h, part * half : (part + 1) * half, :] = delta
            for j in range(half // GROUP):
                tiles[h].append(jnp.transpose(delta[j * GROUP : (j + 1) * GROUP])[0:1])
    dox_ref[rows : rows + EXTRA, :] = pack_extra(tiles, heads, blocks, heads * HEAD)
    dox_ref[rows + EXTRA :, :] = lsex_ref[...]


def out_back(mine, other, wo, okeep, osend, lsex):
    half, width_d = mine.shape
    width = wo.shape[0]
    heads, blocks = width // HEAD, 2 * half // GROUP
    return call(
        functools.partial(out_back_body, heads=heads, blocks=blocks),
        [(sds((2 * half + 2 * EXTRA, width), bf16), VMEM), (sds((heads, 2 * half, 128), f32), VMEM)],
        [VMEM] * 6,
        (mine, other, wo, okeep, osend, lsex),
        "out_back",
        flops=2 * 2 * half * width * width_d,
        nbytes=4e6,
    )


def query_back_body(pos_ref, clip_ref, *refs, pieces, entries, heads, blocks, period):
    qx_ref, dox_ref, lsec_ref, dc_ref = refs[0:4]
    kv_refs = refs[4 : 4 + pieces]
    dq_ref, kv_s, acc_s = refs[4 + pieces :]
    width = heads * HEAD
    sets = period // blocks
    assemble(kv_refs, entries, kv_s, blocks)

    def per_block(i, carry):
        r0 = pl.multiple_of(i * GROUP, GROUP)
        own_clip = clip_of(clip_ref, pos_ref, i, blocks, sets, True)
        acc_s[...] = jnp.zeros(acc_s.shape, f32)

        def per_keys(g, inner):
            @pl.when(own_clip == clip_of(clip_ref, pos_ref, g, blocks, sets, False))
            def _():
                for h in range(heads):
                    cols = slice(h * HEAD, (h + 1) * HEAD)
                    k = kv_s[g, :, cols]
                    v = kv_s[g, :, width + h * HEAD : width + (h + 1) * HEAD]
                    s = dot_t(qx_ref[pl.ds(r0, GROUP), cols], k) * (HEAD ** (-0.5) * LOG2E)
                    p = jnp.exp2(s - lsec_ref[h, pl.ds(r0, GROUP), :][:, 0:1])
                    dp = dot_t(dox_ref[pl.ds(r0, GROUP), cols], v)
                    delta = dc_ref[h, pl.ds(r0, GROUP), :][:, 0:1]
                    ds = (p * (dp - delta) * (HEAD ** (-0.5))).astype(bf16)
                    acc_s[h] = acc_s[h] + dot(ds, k)

            return inner

        lax.fori_loop(0, period, per_keys, 0)
        for h in range(heads):
            dq_ref[pl.ds(r0, GROUP), h * HEAD : (h + 1) * HEAD] = acc_s[h].astype(bf16)
        return carry

    lax.fori_loop(0, blocks, per_block, 0)


def query_back(pos, clips, qx, dox, lsec, dc, kv_pieces, entries):
    rows, width = qx.shape
    heads, blocks, period = width // HEAD, rows // GROUP, clips.shape[0] // GROUPS_FRAME
    pieces = len(kv_pieces)
    return call(
        functools.partial(
            query_back_body, pieces=pieces, entries=entries, heads=heads, blocks=blocks, period=period
        ),
        [(sds((rows, width), bf16), VMEM)],
        [SMEM, SMEM] + [VMEM] * (4 + pieces),
        (pos, clips, qx, dox, lsec, dc, *kv_pieces),
        "query_back",
        scratch=[
            pltpu.VMEM((period, GROUPS_FRAME * GROUP, 2 * width), bf16),
            pltpu.VMEM((heads, GROUP, HEAD), f32),
        ],
        flops=2e9,
        nbytes=7e6,
        trans=2e6,
    )[0]


def key_back_body(
    pos_ref, clip_ref, *refs, q_pieces, do_pieces, q_entries, do_entries, heads, blocks, period
):
    kv_ref, dq_ref, wq_ref, wk_ref, wv_ref = refs[0:5]
    qx_refs = refs[5 : 5 + q_pieces]
    dox_refs = refs[5 + q_pieces : 5 + q_pieces + do_pieces]
    dqkv_ref, keep_ref, send_ref, q_s, do_s, lse_s, delta_s, dk_s, dv_s = refs[5 + q_pieces + do_pieces :]
    width = heads * HEAD
    rows = blocks * GROUP
    sets = period // blocks
    assemble(qx_refs, q_entries, q_s, blocks)
    assemble(dox_refs, do_entries, do_s, blocks)
    for first, target in ((rows, delta_s), (rows + EXTRA, lse_s)):
        for ri, base, p, k in do_entries:
            extra = dox_refs[ri][base + first : base + first + EXTRA, :].astype(f32)
            for h in range(heads):
                for j in range(blocks):
                    line = unpack_extra(extra, h, j, blocks, width)
                    target[p * blocks + j, h, :, pl.ds(place_start(k), GROUP)] = jnp.broadcast_to(
                        line, (8, 128)
                    )
    dqkv_ref[:, 0:width] = dq_ref[...]

    def per_block(j, carry):
        r0 = pl.multiple_of(j * GROUP, GROUP)
        own_clip = clip_of(clip_ref, pos_ref, j, blocks, sets, True)
        dk_s[...] = jnp.zeros(dk_s.shape, f32)
        dv_s[...] = jnp.zeros(dv_s.shape, f32)

        def per_queries(g, inner):
            @pl.when(own_clip == clip_of(clip_ref, pos_ref, g, blocks, sets, False))
            def _():
                for h in range(heads):
                    cols = slice(h * HEAD, (h + 1) * HEAD)
                    k = kv_ref[pl.ds(r0, GROUP), cols]
                    v = kv_ref[pl.ds(r0, GROUP), width + h * HEAD : width + (h + 1) * HEAD]
                    q = q_s[g, :, cols]
                    do = do_s[g, :, cols]
                    st = dot_t(k, q) * (HEAD ** (-0.5) * LOG2E)
                    pt = jnp.exp2(st - lse_s[g, h, 0:1, :])
                    dv_s[h] = dv_s[h] + dot(pt.astype(bf16), do)
                    dpt = dot_t(v, do)
                    dst = (pt * (dpt - delta_s[g, h, 0:1, :]) * (HEAD ** (-0.5))).astype(bf16)
                    dk_s[h] = dk_s[h] + dot(dst, q)

            return inner

        lax.fori_loop(0, period, per_queries, 0)
        for h in range(heads):
            dqkv_ref[pl.ds(r0, GROUP), width + h * HEAD : width + (h + 1) * HEAD] = dk_s[h].astype(bf16)
            dqkv_ref[pl.ds(r0, GROUP), 2 * width + h * HEAD : 2 * width + (h + 1) * HEAD] = dv_s[
                h
            ].astype(bf16)
        return carry

    lax.fori_loop(0, blocks, per_block, 0)
    half = rows // 2
    for part, ref in enumerate((keep_ref, send_ref)):
        r = slice(part * half, (part + 1) * half)
        total = dot_t(dqkv_ref[r, 0:width], wq_ref[...])
        total = total + dot_t(dqkv_ref[r, width : 2 * width], wk_ref[...])
        total = total + dot_t(dqkv_ref[r, 2 * width :], wv_ref[...])
        ref[...] = total.astype(bf16)


def key_back(pos, clips, kv, dq, wq, wk, wv, qx_pieces, q_entries, dox_pieces, do_entries, ties):
    rows, width = dq.shape
    width_d = wq.shape[0]
    heads, blocks, period = width // HEAD, rows // GROUP, clips.shape[0] // GROUPS_FRAME
    tall = GROUPS_FRAME * GROUP
    return call(
        functools.partial(
            key_back_body, q_pieces=len(qx_pieces), do_pieces=len(dox_pieces), q_entries=q_entries,
            do_entries=do_entries, heads=heads, blocks=blocks, period=period,
        ),
        [
            (sds((rows, 3 * width), bf16), VMEM),
            (sds((rows // 2, width_d), bf16), VMEM),
            (sds((rows // 2, width_d), bf16), VMEM),
        ],
        [SMEM, SMEM] + [VMEM] * (5 + len(qx_pieces) + len(dox_pieces)),
        (pos, clips, kv, dq, wq, wk, wv, *qx_pieces, *dox_pieces),
        "key_back",
        ties=ties,
        scratch=[
            pltpu.VMEM((period, tall, width), bf16),
            pltpu.VMEM((period, tall, width), bf16),
            pltpu.VMEM((period, heads, 8, tall), f32),
            pltpu.VMEM((period, heads, 8, tall), f32),
            pltpu.VMEM((heads, GROUP, HEAD), f32),
            pltpu.VMEM((heads, GROUP, HEAD), f32),
        ],
        flops=4e9,
        nbytes=9e6,
        trans=2e6,
    )


def mlp_body(mine_ref, other_ref, win_ref, ag_ref, act_ref, hg_ref, keep_ref, send_ref, *, steps):
    i = pl.program_id(0)
    x = jnp.where(i < steps // 2, mine_ref[...], other_ref[...])
    units = win_ref.shape[1]
    chunk = 256
    total = None
    for n in range(units // chunk):
        cols = slice(n * chunk, (n + 1) * chunk)
        w = win_ref[:, cols]
        hidden = dot(x, w)
        cdf = 0.5 * (1.0 + lax.erf(hidden * 0.7071067811865476))
        act_ref[:, cols] = (hidden * cdf).astype(bf16)
        density = jnp.exp2(hidden * hidden * (-0.5 * LOG2E)) * 0.3989422804014327
        grad = (ag_ref[:, cols] * (cdf + hidden * density)).astype(bf16)
        hg_ref[:, cols] = grad
        term = dot_t(grad, w)
        total = term if total is None else total + term
    total = total.astype(bf16)

    @pl.when(i < steps // 2)
    def _():
        keep_ref[...] = total

    @pl.when(i >= steps // 2)
    def _():
        send_ref[...] = total


def mlp(mine, other, w_in, act_grad):
    half, width_d = mine.shape
    units = w_in.shape[1]
    steps = 2 * half // GROUP
    rows = 2 * half
    low = lambda i: (jnp.minimum(i, steps // 2 - 1), 0)
    high = lambda i: (jnp.maximum(i - steps // 2, 0), 0)
    return call(
        functools.partial(mlp_body, steps=steps),
        [
            (sds((rows, units), bf16), pl.BlockSpec((GROUP, units), lambda i: (i, 0))),
            (sds((rows, units), bf16), pl.BlockSpec((GROUP, units), lambda i: (i, 0))),
            (sds((half, width_d), bf16), pl.BlockSpec((GROUP, width_d), low)),
            (sds((half, width_d), bf16), pl.BlockSpec((GROUP, width_d), high)),
        ],
        [
            pl.BlockSpec((GROUP, width_d), low),
            pl.BlockSpec((GROUP, width_d), high),
            pl.BlockSpec((width_d, units), lambda i: (0, 0)),
            pl.BlockSpec((GROUP, units), lambda i: (i, 0)),
        ],
        (mine, other, w_in, act_grad),
        "mlp",
        grid=(steps,),
        flops=4 * rows * width_d * units,
        nbytes=9e6,
        trans=2 * rows * units,
    )


def mlp_down_body(act_ref, w_ref, keep_ref, send_ref, *, steps):
    i = pl.program_id(0)
    total = dot(act_ref[...], w_ref[...]).astype(bf16)

    @pl.when(i < steps // 2)
    def _():
        keep_ref[...] = total

    @pl.when(i >= steps // 2)
    def _():
        send_ref[...] = total


def mlp_down(activated, w_out, ties):
    rows, units = activated.shape
    width_d = w_out.shape[1]
    steps = rows // GROUP
    half = sds((rows // 2, width_d), bf16)
    return call(
        functools.partial(mlp_down_body, steps=steps),
        [
            (half, pl.BlockSpec((GROUP, width_d), lambda i: (jnp.minimum(i, steps // 2 - 1), 0))),
            (half, pl.BlockSpec((GROUP, width_d), lambda i: (jnp.maximum(i - steps // 2, 0), 0))),
        ],
        [
            pl.BlockSpec((GROUP, units), lambda i: (i, 0)),
            pl.BlockSpec((units, width_d), lambda i: (0, 0)),
        ],
        (activated, w_out),
        "mlp_down",
        grid=(steps,),
        flops=2 * rows * units * width_d,
        nbytes=4e6,
        ties=ties,
    )


def act_back_body(pos_ref, og_ref, w_ref, rel_ref, ag_ref):
    rel_ref[...] = og_ref[...]
    ag_ref[...] = dot_t(og_ref[...], w_ref[...])


def act_back(pos, out_grad, w_out):
    rows, width_d = out_grad.shape
    units = w_out.shape[0]
    steps = rows // GROUP
    blk = pl.BlockSpec((GROUP, width_d), lambda i, c: (i, 0))
    return call(
        act_back_body,
        [
            (sds((rows, width_d), bf16), blk),
            (sds((rows, units), f32), pl.BlockSpec((GROUP, units), lambda i, c: (i, 0))),
        ],
        [
            pl.BlockSpec((GROUP, width_d), lambda i, c: ((i + c[0] * (steps // 2)) % steps, 0)),
            pl.BlockSpec((units, width_d), lambda i, c: (0, 0)),
        ],
        (pos, out_grad, w_out),
        "act_back",
        grid=(steps,),
        prefetch=1,
        flops=2 * rows * width_d * units,
        nbytes=6e6,
    )


def through_norm(n, v, gain_vec):
    unit, inverse = centre(v)
    t = n * gain_vec
    back = inverse * (
        t - jnp.mean(t, axis=-1, keepdims=True) - unit * jnp.mean(t * unit, axis=-1, keepdims=True)
    )
    return back, unit


def norm_back_body(s_ref, r_ref, v_ref, gain_ref, base_ref, after_ref, branch_ref, gg_ref):
    gain_vec = gain_ref[...]

    def step(r, held):
        n = s_ref[r, :].astype(f32) + r_ref[r, :].astype(f32)
        back, unit = through_norm(n, v_ref[r, :], gain_vec)
        after = base_ref[r, :].astype(f32) + back
        after_ref[r, :] = after
        branch_ref[r, :] = after.astype(bf16)
        return held + folded(n * unit)

    total = by_chunks(s_ref.shape[0], step, jnp.zeros((8, s_ref.shape[1]), f32))
    gg_ref[...] = jnp.sum(total, axis=0, keepdims=True)


def norm_back(s, r, v, gain, base, ties):
    half, width_d = s.shape
    return call(
        norm_back_body,
        [
            (sds((half, width_d), f32), VMEM),
            (sds((half, width_d), bf16), VMEM),
            (sds((1, width_d), f32), VMEM),
        ],
        [VMEM] * 5,
        (s, r, v, gain, base),
        "norm_back",
        ties=ties,
        flops=20 * half * width_d,
        nbytes=5e6,
    )


def final_body(
    pos_ref, s_ref, r_ref, lat_ref, src_ref, gain_one_ref, gain_src_ref, base_ref, half_ref, lat_out, src_out, *, first,
):
    def run(v_ref, gain_ref, base, out_ref):
        gain_vec = gain_ref[...]

        def step(r, held):
            n = s_ref[r, :].astype(f32) + r_ref[r, :].astype(f32)
            back = through_norm(n, v_ref[r, :].astype(f32), gain_vec)[0]
            if base is not None:
                back = base[r, :] + back
            half_ref[r, :] = back.astype(bf16)
            out_ref[r, :] = back.astype(bf16)
            return held

        by_chunks(s_ref.shape[0], step)

    i = pl.program_id(0)
    pl.when(i < first)(lambda: run(lat_ref, gain_one_ref, base_ref, lat_out))
    pl.when(i >= first)(lambda: run(src_ref, gain_src_ref, None, src_out))


def final_norm(pos, s, r, latents, sources, gain_one, gain_src, base, ties):
    width_d = s.shape[1]
    blk = 128
    one, src = latents.shape[0] // 2 // blk, sources.shape[0] // 2 // blk
    at_one = lambda i: jnp.minimum(i, one - 1)
    at_src = lambda i: jnp.maximum(i - one, 0)
    spec = lambda f: pl.BlockSpec((blk, width_d), lambda i, c: (f(i, c), 0))
    gain_spec = pl.BlockSpec((1, width_d), lambda i, c: (0, 0))
    own_one, own_src = spec(lambda i, c: c[0] * one + at_one(i)), spec(lambda i, c: c[0] * src + at_src(i))
    each = spec(lambda i, c: i)
    return call(
        functools.partial(final_body, first=one),
        [(sds(s.shape, bf16), each), (sds(latents.shape, bf16), own_one), (sds(sources.shape, bf16), own_src)],
        [each, each, own_one, own_src, gain_spec, gain_spec, spec(lambda i, c: at_one(i))],
        (pos, s, r, latents, sources, gain_one, gain_src, base),
        "final_norm",
        grid=(one + src,),
        prefetch=1,
        flops=20 * s.size,
        nbytes=8 * s.size,
        ties=ties,
    )


def place_both_body(pos_ref, other_ref, lat_in, src_in, lat_out, src_out):
    i = pl.program_id(0)

    @pl.when(i == 0)
    def _():
        lat_out[...] = other_ref[...]

    @pl.when(i > 0)
    def _():
        src_out[...] = other_ref[...]


def place_both(pos, other, lat_whole, src_whole):
    blk, width_d = lat_whole.shape[0] // 2, other.shape[1]
    steps = other.shape[0] // blk
    spec = lambda f: pl.BlockSpec((blk, width_d), lambda i, c: (f(i, c), 0))
    return call(
        place_both_body,
        [
            (sds(lat_whole.shape, bf16), spec(lambda i, c: 1 - c[0])),
            (sds(src_whole.shape, bf16), spec(lambda i, c: (1 - c[0]) * (steps - 1) + jnp.maximum(i - 1, 0))),
        ],
        [spec(lambda i, c: i), ANY, ANY],
        (pos, other, lat_whole, src_whole),
        "place_both",
        grid=(steps,),
        prefetch=1,
        nbytes=4 * other.size,
        aliases={2: 0, 3: 1},
    )


def place_body(pos_ref, other_ref, whole_ref, out_ref):
    out_ref[...] = other_ref[...]


def place_other(pos, whole, other):
    half, width_d = other.shape
    rows = 256
    steps = half // rows
    return call(
        place_body,
        [(sds(whole.shape, bf16), pl.BlockSpec((rows, width_d), lambda i, c: ((1 - c[0]) * steps + i, 0)))],
        [pl.BlockSpec((rows, width_d), lambda i, c: (i, 0)), ANY],
        (pos, other, whole),
        "place_other",
        grid=(steps,),
        prefetch=1,
        nbytes=4 * half * width_d,
        aliases={2: 0},
    )[0]


def result_body(pos_ref, s_ref, r_ref, after_ref, half_ref, whole_ref, squares_ref):
    def step(r, held):
        result = after_ref[r, :] + (s_ref[r, :].astype(f32) + r_ref[r, :].astype(f32))
        half_ref[r, :] = result.astype(bf16)
        whole_ref[r, :] = result.astype(bf16)
        return held + folded(result * result)

    total = by_chunks(s_ref.shape[0], step, jnp.zeros((8, s_ref.shape[1]), f32))
    squares_ref[pl.ds(pl.program_id(0), 1), :] = jnp.sum(total, axis=0, keepdims=True)


def result_half(pos, s, r, after):
    half, width_d = s.shape
    steps = half // GROUP
    blk = pl.BlockSpec((GROUP, width_d), lambda i, c: (i, 0))
    own = pl.BlockSpec((GROUP, width_d), lambda i, c: (c[0] * steps + i, 0))
    return call(
        result_body,
        [
            (sds((half, width_d), bf16), blk),
            (sds((2 * half, width_d), bf16), own),
            (sds((steps, width_d), f32), pl.BlockSpec((steps, width_d), lambda i, c: (0, 0))),
        ],
        [blk] * 3,
        (pos, s, r, after),
        "result",
        grid=(steps,),
        prefetch=1,
        flops=6 * half * width_d,
        nbytes=5e6,
    )


def gains_body(
    pos_ref, clip_ref, frames_ref, keep, send, lat_ref, src_ref,
    self_ref, mlp_ref, squares_ref, out_ref, *, one_steps, src_steps, blocks, sets, copies, clips,
):
    i = pl.program_id(0)

    @pl.when(i == 0)
    def _():
        width_d = out_ref.shape[1]
        share = jnp.zeros((1, 1), f32)
        for b in range(blocks // 2):
            total = jnp.sum(squares_ref[b : b + 1, :], axis=1, keepdims=True)
            frames = frames_ref[clip_of(clip_ref, pos_ref, b, blocks, sets, True)].astype(f32)
            norm = jnp.sqrt(total / (GROUP * width_d) + 1e-06)
            share = share + norm / (jnp.broadcast_to(frames, (1, 1)) * (GROUPS_FRAME * clips))
        out_ref[0:2, :] = jnp.zeros((2, width_d), f32)
        out_ref[2:3, :] = self_ref[...] * copies
        out_ref[3:4, :] = mlp_ref[...] * copies
        out_ref[4:8, :] = jnp.broadcast_to(share * copies, (4, width_d))

    def add(row, v_ref, keep_ref, send_ref, kept):
        def step(r, held):
            n = jnp.where(kept, keep_ref[r, :].astype(f32), send_ref[r, :].astype(f32))
            return held + folded(n * centre(v_ref[r, :].astype(f32))[0])

        total = by_chunks(v_ref.shape[0], step, jnp.zeros((8, v_ref.shape[1]), f32))
        out_ref[row : row + 1, :] = out_ref[row : row + 1, :] + jnp.sum(total, axis=0, keepdims=True)

    pl.when(i < one_steps)(lambda: add(1, lat_ref, keep, send, i < one_steps // 2))
    pl.when(i >= one_steps)(lambda: add(0, src_ref, keep, send, i - one_steps < src_steps // 2))


def gains(pos, clips, frames, keep, send, latents, sources, self_gain, mlp_gain, squares, copies, ties):
    rows, width_d = latents.shape
    count = sources.shape[0]
    blk = 256
    one_steps, src_steps = rows // blk, count // blk
    one_half, src_half = one_steps // 2, src_steps // 2
    blocks = rows // GROUP
    sets = clips.shape[0] // GROUPS_FRAME // blocks
    clamp = lambda v, top: jnp.minimum(jnp.maximum(v, 0), top)
    spec = lambda f: pl.BlockSpec((blk, width_d), lambda i, *c: (f(i, c[0]), 0))
    fixed = lambda n: pl.BlockSpec((n, width_d), lambda i, *c: (0, 0))
    turn = lambda i, c, steps: (clamp(i, steps - 1) + c[0] * (steps // 2)) % steps
    kept = lambda i, c: jnp.where(
        i < one_steps, clamp(i, one_half - 1), one_half + clamp(i - one_steps, src_half - 1)
    )
    sent = lambda i, c: jnp.where(
        i < one_steps, clamp(i - one_half, one_half - 1), one_half + clamp(i - one_steps - src_half, src_half - 1)
    )
    return call(
        functools.partial(
            gains_body, one_steps=one_steps, src_steps=src_steps, blocks=blocks, sets=sets, copies=copies,
            clips=frames.shape[0],
        ),
        [(sds((8, width_d), f32), fixed(8))],
        [
            spec(kept),
            spec(sent),
            spec(lambda i, c: turn(i, c, one_steps)),
            spec(lambda i, c: turn(i - one_steps, c, src_steps)),
            fixed(1), fixed(1), fixed(blocks // 2),
        ],
        (pos, clips, frames, keep, send, latents, sources, self_gain, mlp_gain, squares),
        "gains",
        grid=(one_steps + src_steps,),
        prefetch=3,
        flops=20 * (rows + count) * width_d,
        nbytes=4 * (rows + count) * width_d,
        ties=ties,
    )[0]


def feature_grads_body(pos_ref, *refs, items, sends, blk):
    given = sum(a + b for a, b in items)
    keep_ref, send_refs = refs[given], refs[given + 1 :]
    at, column = 0, 0
    for lefts, rights in items:
        total, row = None, 0
        for k in range(lefts):
            left = refs[at + k]
            rows = left.shape[0]
            if rights == 1:
                right = refs[at + lefts][row : row + rows, :]
            else:
                right = refs[at + lefts + k][...]
            term = dot_ta(left[...], right)
            total = term if total is None else total + term
            row += rows
        at += lefts + rights
        first, column = column, column + total.shape[1]
        total = total.astype(bf16)
        for j in range(blk // 128):
            part = total[j * 128 : (j + 1) * 128]
            if sends == 0:
                keep_ref[j, :, first:column] = part
                continue
            mine = (pos_ref[1] + j) % 2 == 0

            @pl.when(mine)
            def _():
                keep_ref[j // 2, :, first:column] = part

            @pl.when(jnp.logical_not(mine))
            def _():
                width = send_refs[0].shape[2]
                for h, ref in enumerate(send_refs):
                    low, high = max(first, h * width), min(column, (h + 1) * width)
                    if low < high:
                        ref[j // 2, :, low - h * width : high - h * width] = part[:, low - first : high - first]


def feature_grads(pos, items, sends, ties=()):
    arrays, specs, counts, columns, flops = [], [], [], 0, 0
    features = items[0][0][0].shape[1]
    blk = 512
    for lefts, rights in items:
        counts.append((len(lefts), len(rights)))
        for v in lefts:
            arrays.append(v)
            specs.append(pl.BlockSpec((v.shape[0], blk), lambda i, c: (0, i)))
            flops += 2 * v.shape[0] * v.shape[1] * rights[0].shape[1]
        for v in rights:
            arrays.append(v)
            specs.append(pl.BlockSpec(v.shape, lambda i, c: (0, 0)))
        columns += rights[0].shape[1]
    steps = features // blk
    sets = features // 256 if sends else features // 128
    out = lambda n: (sds((sets, 128, n), bf16), pl.BlockSpec((sets // steps, 128, n), lambda i, c: (i, 0, 0)))
    return call(
        functools.partial(feature_grads_body, items=tuple(counts), sends=sends, blk=blk),
        [out(columns)] + [out(columns // sends)] * sends if sends else [out(columns)],
        specs,
        (pos, *arrays),
        "feature_grads",
        grid=(steps,),
        prefetch=1,
        flops=flops,
        nbytes=2 * features * columns + sum(2 * v.size for v in arrays),
        ties=ties,
    )


def stage_one_body(pos_ref, keep_ref, *refs):
    z = pos_ref[1] // 2
    gots, (own_ref, send_ref) = refs[:-2], refs[-2:]
    width = gots[0].shape[2]
    for h, got_ref in enumerate(gots):
        cols = slice(h * width, (h + 1) * width)
        for k in range(2):
            at = z ^ (2 * k)
            own_ref[k, :, cols] = keep_ref[at, :, cols].astype(f32) + got_ref[at].astype(f32)
            at = z ^ 1 ^ (2 * k)
            send_ref[k, :, cols] = (keep_ref[at, :, cols].astype(f32) + got_ref[at].astype(f32)).astype(bf16)


def stage_one(pos, keep, gots, ties=()):
    shape = (2, *keep.shape[1:])
    return call(
        stage_one_body,
        [(sds(shape, f32), VMEM), (sds(shape, bf16), VMEM)],
        [SMEM] + [VMEM] * (1 + len(gots)),
        (pos, keep, *gots),
        "stage_one",
        nbytes=4 * keep.size,
        ties=ties,
    )


def stage_two_body(keep_ref, got_ref, own_ref, send_ref):
    own_ref[...] = keep_ref[0] + got_ref[0].astype(f32)
    send_ref[...] = (keep_ref[1] + got_ref[1].astype(f32)).astype(bf16)


def stage_two(keep, got, ties=()):
    shape = keep.shape[1:]
    return call(
        stage_two_body,
        [(sds(shape, f32), VMEM), (sds(shape, bf16), VMEM)],
        [VMEM] * 2,
        (keep, got),
        "stage_two",
        nbytes=4 * keep.size,
        ties=ties,
    )


def stage_end_body(own_ref, got_ref, *outs, turned):
    total = own_ref[...] + got_ref[...].astype(f32)
    width = total.shape[1] // len(outs)
    for k, ref in enumerate(outs):
        part = total[:, k * width : (k + 1) * width]
        ref[...] = part.T if k in turned else part


def stage_end(own, got, parts, turned, ties=()):
    blk = own.shape
    width = blk[1] // parts
    return call(
        functools.partial(stage_end_body, turned=turned),
        [(sds((width, blk[0]) if k in turned else (blk[0], width), f32), VMEM) for k in range(parts)],
        [VMEM] * 2,
        (own, got),
        "stage_end",
        nbytes=10 * blk[0] * blk[1],
        ties=ties,
    )


def flip_x(v):
    return lax.ppermute(v, "seq", xor_pairs(1, 8))


def near_z(v):
    return lax.ppermute(v, "seq", xor_pairs(2, 8))


def far_z(v):
    return lax.ppermute(v, "seq", xor_pairs(4, 8))


def scatter_whole(pos, items, parts, turned, ties):
    whole = feature_grads(pos, items, 0, ties)[0]
    whole = whole.reshape(-1, whole.shape[2])
    total = lax.psum_scatter(whole, "seq", scatter_dimension=0, tiled=True).astype(f32)
    width = total.shape[1] // parts
    pieces = [total[:, k * width : (k + 1) * width] for k in range(parts)]
    return [piece.T if k in turned else piece for k, piece in enumerate(pieces)]


def tied(values, other):
    out = lax.optimization_barrier((other, *values))
    return list(out[1:]), out[0]


def cross_back_body(
    pos_ref, mine_ref, other_ref, wo_ref, q_ref, kvp_ref, idx_ref, wq_ref, wk_ref, wv_ref,
    dq_ref, dk_ref, dv_ref, keep_ref, send_ref, dkvp_s, *, blocks,
):
    width = wq_ref.shape[1]
    heads = width // HEAD
    count = kvp_ref.shape[0]
    scale = HEAD ** (-0.5)
    for b in range(blocks):
        ref = mine_ref if b < blocks // 2 else other_ref
        part = (b % (blocks // 2)) * GROUP
        grad = dot_t(ref[part : part + GROUP, :], wo_ref[...]).astype(bf16)
        for h in range(heads):
            cols = slice(h * HEAD, (h + 1) * HEAD)
            vcols = slice(width + h * HEAD, width + (h + 1) * HEAD)
            q = q_ref[b * GROUP : (b + 1) * GROUP, cols]
            k = kvp_ref[b * SRC : (b + 1) * SRC, cols]
            v = kvp_ref[b * SRC : (b + 1) * SRC, vcols]
            do = grad[:, cols]
            s = dot_t(q, k) * (scale * LOG2E)
            p = jnp.exp2(s - jnp.max(s, axis=-1, keepdims=True))
            p = p / jnp.sum(p, axis=-1, keepdims=True)
            dp = dot_t(do, v)
            delta = jnp.sum(p * dp, axis=-1, keepdims=True)
            ds = (p * (dp - delta) * scale).astype(bf16)
            dq_ref[b * GROUP : (b + 1) * GROUP, cols] = dot(ds, k).astype(bf16)
            dkvp_s[b * SRC : (b + 1) * SRC, cols] = dot_ta(ds, q).astype(bf16)
            dkvp_s[b * SRC : (b + 1) * SRC, vcols] = dot_ta(p.astype(bf16), do).astype(bf16)
        one = dot_t(dq_ref[b * GROUP : (b + 1) * GROUP, :], wq_ref[...]).astype(bf16)
        if b < blocks // 2:
            keep_ref[part : part + GROUP, :] = one
        else:
            send_ref[part : part + GROUP, :] = one
    half = count // 2
    blk = 256
    row = jnp.concatenate([index_row(idx_ref, pos_ref, b, blocks, count) for b in range(blocks)], axis=1)
    for n in range(count // blk):
        r0 = pl.multiple_of(
            (pos_ref[0] if n * blk < half else 1 - pos_ref[0]) * half + (n * blk) % half, blk
        )
        wanted = lax.broadcasted_iota(jnp.int32, (blk, count), 0).astype(f32) + r0.astype(f32)
        picks = jnp.where(row == wanted, 1.0, 0.0).astype(bf16)
        dkv = dot(picks, dkvp_s[...]).astype(bf16)
        dk_ref[pl.ds(r0, blk), :] = dkv[:, 0:width]
        dv_ref[pl.ds(r0, blk), :] = dkv[:, width:]
        total = (dot_t(dkv[:, 0:width], wk_ref[...]) + dot_t(dkv[:, width:], wv_ref[...])).astype(bf16)
        at = blocks // 2 * GROUP + (n * blk) % half
        if n * blk < half:
            keep_ref[at : at + blk, :] = total
        else:
            send_ref[at : at + blk, :] = total


def cross_back(pos, mine, other, wo, q, kvp, idx, wq, wk, wv, ties):
    rows, width = q.shape
    width_d = wq.shape[0]
    count = kvp.shape[0]
    blocks = rows // GROUP
    return call(
        functools.partial(cross_back_body, blocks=blocks),
        [
            (sds((rows, width), bf16), VMEM),
            (sds((count, width), bf16), VMEM),
            (sds((count, width), bf16), VMEM),
            (sds(((rows + count) // 2, width_d), bf16), VMEM),
            (sds(((rows + count) // 2, width_d), bf16), VMEM),
        ],
        [SMEM] + [VMEM] * 9,
        (pos, mine, other, wo, q, kvp, idx, wq, wk, wv),
        "cross_back",
        ties=ties,
        scratch=[pltpu.VMEM((count, 2 * width), bf16)],
        flops=4e9,
        nbytes=12e6,
    )


def xor_pairs(bit, size):
    return [(i, i ^ bit) for i in range(size)]


def ring_pairs(d):
    return [(s, ((s // 2 + d) % 4) * 2 + s % 2) for s in range(8)]


def tensor_swap(x, bit):
    return lax.ppermute(x, "tensor", xor_pairs(bit, lax.axis_size("tensor")))


def seq_gather(x, between=None, guest=None):
    size = lax.axis_size("seq")
    if size == 8:
        move = lambda v, pairs: lax.ppermute(v, "seq", pairs)
        flip = xor_pairs(1, 8)
        beside = move(x, flip)
        up = move(x, ring_pairs(1))
        down = move(x, ring_pairs(-1))
        if guest is not None:
            (beside, up, guest), between = tied([beside, up, guest], between)
            guest = flip_x(guest)
        far = move(up, ring_pairs(1))
        down_beside = move(beside, ring_pairs(-1))
        if guest is not None:
            up_beside = move(beside, ring_pairs(1))
            (far_sent, up_beside), down_beside = tied([far, up_beside], down_beside)
        else:
            up_beside = move(up, flip)
            far_sent = far
        far_beside = move(far_sent, flip)
        pieces = [x, beside, up, down, far, up_beside, down_beside, far_beside]
    else:
        pieces = gather_whole(x)
    return pieces if guest is None else (pieces, between, guest)


def gather_whole(x):
    return [lax.all_gather(x, "seq", axis=0, tiled=True)]


def gather_entries(size, rows, sets):
    if size == 8:
        return tuple((k, 0, 0, k) for k in range(8))
    return whole_entries(size, rows, sets)


def whole_entries(size, rows, sets):
    return tuple((0, s * rows, s % sets, s // sets) for s in range(size))


def half_sum(keep, send):
    size = lax.axis_size("tensor")
    got = tensor_swap(send, 1)
    own = (keep.astype(f32) + got.astype(f32)).astype(bf16)
    bit = 2
    while True:
        other = tensor_swap(own, bit)
        if bit * 2 >= size:
            return own, other
        own = (own.astype(f32) + other.astype(f32)).astype(bf16)
        bit *= 2


def tensor_pieces(keep, send):
    size = lax.axis_size("tensor")
    return [keep if k == 0 else tensor_swap(send if k % 2 else keep, k) for k in range(size)]


def weight_far(weight):
    pieces = {0: weight}
    bit = lax.axis_size("tensor") // 2
    while bit >= 2:
        pieces.update({k + bit: tensor_swap(v, bit) for k, v in list(pieces.items())})
        bit //= 2
    return pieces


def weight_pieces(pieces):
    pieces = dict(pieces)
    pieces.update({k + 1: tensor_swap(v, 1) for k, v in list(pieces.items())})
    return [pieces[k] for k in range(len(pieces))]


def tie_all(pieces, other):
    keys = sorted(pieces)
    tied = lax.optimization_barrier((other, *[pieces[k] for k in keys]))
    return dict(zip(keys, tied[1:])), tied[0]


def sum_over(v, axis, only):
    size = lax.axis_size(axis)
    bit = only or 1
    while bit < size:
        v = v + lax.ppermute(v, axis, xor_pairs(bit, size))
        bit = size if only else bit * 2
    return v


def local(
    latents, sources, source_index, block_clip, clip_frames, norm_src, norm_cross, norm_self, norm_mlp,
    cross_q, cross_k, cross_v, cross_o, self_q, self_k, self_v, self_o, mlp_in, mlp_out, out_grad,
):
    rows, width_d = latents.shape
    blocks = rows // GROUP
    width = cross_q.shape[1]
    units = mlp_in.shape[1]
    tensor_size, seq_size = lax.axis_size("tensor"), lax.axis_size("seq")
    core = lax.axis_index("tensor") % 2
    pos = jnp.stack((core, lax.axis_index("seq"), lax.axis_index("tensor"))).astype(jnp.int32)
    sets = block_clip.shape[0] // GROUPS_FRAME // blocks
    gain = lambda g: g.reshape(1, width_d)
    kv_entries = gather_entries(seq_size, rows, sets)
    out_entries = gather_entries(seq_size, rows + 2 * EXTRA, sets)

    cross_o_far = weight_far(cross_o)
    normed_one, normed_src, cross_query, cross_kv, mixed_keep, mixed_send = cross_forward(
        pos, source_index, latents, sources, gain(norm_cross), gain(norm_src), cross_q, cross_k, cross_v
    )
    cross_o_far, mixed_keep = tie_all(cross_o_far, mixed_keep)
    after_cross, two_mine = project(
        pos, tensor_pieces(mixed_keep, mixed_send), weight_pieces(cross_o_far), latents, gain(norm_self), True
    )
    two_other = tensor_swap(two_mine, 1)
    query, key_value = qkv(two_mine, two_other, self_q, self_k, self_v)
    kv_pieces = seq_gather(key_value)
    self_o_tied, two_mine = tie_all({0: self_o}, two_mine)
    self_o_all = weight_pieces(weight_far(self_o_tied[0]))
    out_rel, act_grad = act_back(pos, out_grad, mlp_out)
    split = seq_size == 8
    query_pieces = seq_gather(query)
    self_keep, self_send, lse_rows, lse_columns = attend(
        pos, block_clip, query, kv_pieces, kv_entries, (act_grad, *self_o_all[1:])
    )
    after_self, three_mine = project(
        pos, tensor_pieces(self_keep, self_send), self_o_all, after_cross, gain(norm_mlp), False,
        query_pieces[1:4],
    )
    three_other = tensor_swap(three_mine, 1)
    activated, hidden_grad, three_keep, three_send = mlp(three_mine, three_other, mlp_in, act_grad)

    three_sum, three_got = half_sum(three_keep, three_send)
    in_items = (((three_mine, three_other), (hidden_grad,)),)
    out_items = (((out_rel,), (activated,)),)
    early = ()
    if split:
        in_keep, in_send = feature_grads(pos, in_items, 1, (three_sum,))
        out_keep, out_send_a, out_send_b = feature_grads(pos, out_items, 2, (in_keep,))
        early = (out_keep, *query_pieces[4:])
    down_keep, down_send = mlp_down(activated, mlp_out, (three_sum, *early[0:1]))
    early = (*early, down_keep)
    after_self_grad, self_branch, mlp_gain = norm_back(
        three_sum, three_got, after_self, gain(norm_mlp), out_rel, early
    )
    self_branch_other = tensor_swap(self_branch, 1)

    out_more, delta_columns = out_back(self_branch, self_branch_other, self_o, self_keep, self_send, lse_rows)
    self_query_grad = query_back(
        pos, block_clip, query, out_more, lse_columns, delta_columns, kv_pieces, kv_entries
    )
    if split:
        out_pieces, self_query_grad, in_got = seq_gather(out_more, self_query_grad, in_send)
    else:
        out_pieces = seq_gather(out_more)
    result_sum, result_got = half_sum(down_keep, down_send)
    output_half, output_whole, squares = result_half(pos, result_sum, result_got, after_self)
    output = place_other(pos, output_whole, tensor_swap(output_half, 1))
    early = ()
    if split:
        in_keep, in_send = stage_one(pos, in_keep, [in_got])
        (out_send_a, in_send), out_pieces[-1] = tied([out_send_a, in_send], out_pieces[-1])
        out_got_a = flip_x(out_send_a)
        early = (squares,)
    self_grads, two_keep, two_send = key_back(
        pos, block_clip, key_value, self_query_grad, self_q, self_k, self_v,
        query_pieces, kv_entries, out_pieces, out_entries, early,
    )
    if split:
        (two_send, out_send_b), out_got_a = tied([two_send, out_send_b], out_got_a)
        out_got_b = flip_x(out_send_b)
        in_got = near_z(in_send)
    two_sum, two_got = half_sum(two_keep, two_send)
    self_items = (
        ((two_mine, two_other), (self_grads,)),
        ((self_branch, self_branch_other), (self_keep, self_send)),
    )
    early = ()
    if split:
        self_wkeep, self_send_a, self_send_b = feature_grads(pos, self_items, 2, (two_sum,))
        in_own, in_send = stage_two(in_keep, in_got, (self_wkeep,))
        out_keep, out_send = stage_one(pos, out_keep, [out_got_a, out_got_b], (in_send,))
        early = (self_wkeep, in_own, out_keep, output)
    after_cross_grad, cross_branch, self_gain = norm_back(
        two_sum, two_got, after_cross, gain(norm_self), after_self_grad, early
    )
    cross_branch_other = tensor_swap(cross_branch, 1)

    if split:
        (self_send_a, in_send), cross_branch_other = tied([self_send_a, in_send], cross_branch_other)
        self_got_a = flip_x(self_send_a)
        in_got = far_z(in_send)
    cross_query_grad, cross_key_grad, cross_value_grad, both_keep, both_send = cross_back(
        pos, cross_branch, cross_branch_other, cross_o, cross_query, cross_kv, source_index,
        cross_q, cross_k, cross_v, (),
    )
    first_items = (((normed_one,), (cross_query_grad,)), ((normed_src,), (cross_key_grad,)))
    second_items = (
        ((normed_src,), (cross_value_grad,)),
        ((cross_branch, cross_branch_other), (mixed_keep, mixed_send)),
    )
    gains_of = lambda ties: gains(
        pos, block_clip, clip_frames, both_keep, both_send, latents, sources,
        self_gain, mlp_gain, squares, 2.0 / tensor_size, ties,
    )
    final_of = lambda ties: final_norm(
        pos, both_sum, both_got, latents, sources, gain(norm_cross), gain(norm_src), after_cross_grad, ties
    )
    if split:
        both_send, self_send_b, out_send, self_got_a, in_got = lax.optimization_barrier(
            (both_send, self_send_b, out_send, self_got_a, in_got)
        )
        self_got_b = flip_x(self_send_b)
        out_got = near_z(out_send)
        both_sum, both_got = half_sum(both_keep, both_send)
        first_keep, first_send = feature_grads(pos, first_items, 1, (both_sum,))
        second_keep, second_send = feature_grads(pos, second_items, 1, (first_keep,))
        out_own, out_send = stage_two(out_keep, out_got, (second_keep,))
        self_wkeep, self_wsend = stage_one(pos, self_wkeep, [self_got_a, self_got_b], (out_own,))

        first_send, out_send, self_wsend = lax.optimization_barrier((first_send, out_send, self_wsend))
        first_got = flip_x(first_send)
        out_got = far_z(out_send)
        self_wgot = near_z(self_wsend)
        mlp_outs = stage_end(in_own, in_got, 1, (), (self_wsend,))
        small = gains_of((first_send, mlp_outs[0]))
        small = sum_over(small, "tensor", 1)
        first_keep, first_send = stage_one(pos, first_keep, [first_got], (out_got, small))
        self_own, self_wsend = stage_two(self_wkeep, self_wgot, (first_keep,))

        second_send, first_send, self_wsend, small = lax.optimization_barrier(
            (second_send, first_send, self_wsend, small)
        )
        second_got = flip_x(second_send)
        first_got = near_z(first_send)
        self_wgot = far_z(self_wsend)
        both_half, lat_whole, src_whole = final_of(())
        mlp_outs = [*mlp_outs, stage_end(out_own, out_got, 1, (0,), (both_half,))[0]]
        small, both_half = lax.optimization_barrier((small, both_half))
        small = sum_over(small, "seq", 1)
        second_keep, second_send = stage_one(pos, second_keep, [second_got], (self_wgot, small, mlp_outs[1]))
        first_own, first_send = stage_two(first_keep, first_got, (second_keep,))

        second_send, first_send, small, both_half = lax.optimization_barrier(
            (second_send, first_send, small, both_half)
        )
        second_got = near_z(second_send)
        first_got = far_z(first_send)
        small = sum_over(small, "seq", 2)
        both_other = tensor_swap(both_half, 1)
        self_outs = stage_end(self_own, self_wgot, 4, (3,), (first_send,))
        second_own, second_send = stage_two(second_keep, second_got, (first_got, small, self_outs[0]))

        second_send, both_other, small = lax.optimization_barrier((second_send, both_other, small))
        second_got = far_z(second_send)
        small = sum_over(small, "seq", 4)
        bit = 2
        while bit < tensor_size:
            small = sum_over(small, "tensor", bit)
            bit *= 2
        latents_grad, sources_grad = place_both(pos, both_other, lat_whole, src_whole)
        cross_outs = [*stage_end(first_own, first_got, 2, ()), *stage_end(second_own, second_got, 2, (1,))]
    else:
        both_sum, both_got = half_sum(both_keep, both_send)
        small = gains_of((both_sum,))
        small = sum_over(small, "tensor", 0)
        small = sum_over(small, "seq", 0)
        both_half, lat_whole, src_whole = final_of(())
        latents_grad, sources_grad = place_both(pos, tensor_swap(both_half, 1), lat_whole, src_whole)
        cross_outs = scatter_whole(pos, first_items, 2, (), ()) + scatter_whole(pos, second_items, 2, (1,), ())
        self_outs = scatter_whole(pos, self_items, 4, (3,), ())
        mlp_outs = scatter_whole(pos, in_items, 1, (), ()) + scatter_whole(pos, out_items, 1, (0,), ())
    return (
        output, latents_grad, sources_grad, small[0], small[1], small[2], small[3],
        *cross_outs, *self_outs, *mlp_outs, small[4, 0],
    )


def solution(mesh):
    in_specs = (
        P("seq", None), P("seq", None), P("seq", None), P(), P(), P(), P(), P(), P(),
        P(None, "tensor"), P(None, "tensor"), P(None, "tensor"), P("tensor", None),
        P(None, "tensor"), P(None, "tensor"), P(None, "tensor"), P("tensor", None),
        P(None, "tensor"), P("tensor", None), P("seq", None),
    )
    out_specs = (
        P("seq", None), P("seq", None), P("seq", None), P(), P(), P(), P(),
        P("seq", "tensor"), P("seq", "tensor"), P("seq", "tensor"), P("tensor", "seq"),
        P("seq", "tensor"), P("seq", "tensor"), P("seq", "tensor"), P("tensor", "seq"),
        P("seq", "tensor"), P("tensor", "seq"), P(),
    )
    return jax.shard_map(local, mesh=mesh, in_specs=in_specs, out_specs=out_specs, check_vma=False)
```

```python
import functools
import math

import jax
import jax.numpy as jnp
from jax import lax
from jax.experimental import pallas as pl
from jax.experimental.pallas import tpu as pltpu
from jax.sharding import PartitionSpec as P

HEAD = 128
GROUP = 128
SRC = 256
GROUPS_FRAME = 8
LOG2E = 1.4426950408889634
epsilon = 1e-05
masked_value = -1e30
bf16 = jnp.bfloat16
f32 = jnp.float32
EXTRA = 16
WEIGHT = 1

VMEM = pl.BlockSpec(memory_space=pltpu.VMEM)
SMEM = pl.BlockSpec(memory_space=pltpu.SMEM)


def sds(shape, dtype):
    return jax.ShapeDtypeStruct(shape, dtype)


def dot(a, b):
    return lax.dot_general(a, b, (((1,), (0,)), ((), ())), preferred_element_type=f32)


def dot_t(a, b):
    return lax.dot_general(a, b, (((1,), (1,)), ((), ())), preferred_element_type=f32)


def dot_ta(a, b):
    return lax.dot_general(a, b, (((0,), (0,)), ((), ())), preferred_element_type=f32)


def centre(values):
    centred = values - jnp.mean(values, axis=-1, keepdims=True)
    variance = jnp.mean(centred * centred, axis=-1, keepdims=True)
    inverse = lax.rsqrt(variance + epsilon)
    return centred * inverse, inverse


ANY = pl.BlockSpec(memory_space=pl.ANY)
CHUNK = 64


def by_chunks(rows, step, carry=0):
    for first in range(0, rows, CHUNK):
        carry = step(slice(first, first + CHUNK), carry)
    return carry


def norm_into(out_ref, in_ref, gain_ref):
    gain_vec = gain_ref[...]

    def step(r, held):
        out_ref[r, :] = (centre(in_ref[r, :].astype(f32))[0] * gain_vec).astype(bf16)
        return held

    by_chunks(in_ref.shape[0], step)


def folded(rows_value):
    parts = [rows_value[k : k + 8] for k in range(0, CHUNK, 8)]
    while len(parts) > 1:
        parts = [parts[k] + parts[k + 1] for k in range(0, len(parts), 2)]
    return parts[0]


def call(
    body, outs, ins, args, name, scratch=(), grid=None, prefetch=0, flops=0, nbytes=0, trans=0, ties=(), aliases=None,
    spare=6,
):
    given = prefetch + len(ins)
    room = 0
    for spec, v in [*zip(ins, args[prefetch:]), *[(spec, shape) for shape, spec in outs]]:
        if spec.block_shape is not None:
            room += 2 * math.prod(spec.block_shape) * v.dtype.itemsize
        elif spec is VMEM:
            room += math.prod(v.shape) * v.dtype.itemsize
    room += sum(math.prod(v.shape) * jnp.dtype(v.dtype).itemsize for v in scratch)

    def run(*refs):
        body(*refs[:given], *refs[given + len(ties) :])

    return pl.pallas_call(
        run,
        out_shape=[shape for shape, ignored in outs],
        grid_spec=pltpu.PrefetchScalarGridSpec(
            num_scalar_prefetch=prefetch,
            grid=() if grid is None else grid,
            in_specs=list(ins) + [ANY] * len(ties),
            out_specs=[spec for ignored, spec in outs],
            scratch_shapes=list(scratch),
        ),
        compiler_params=pltpu.CompilerParams(vmem_limit_bytes=room + spare * 2**20),
        cost_estimate=pl.CostEstimate(
            flops=int(flops * WEIGHT), bytes_accessed=int(nbytes * WEIGHT), transcendentals=int(trans * WEIGHT)
        ),
        input_output_aliases=aliases or {},
        name=name,
    )(*args, *ties)


def index_row(idx_ref, pos_ref, b, blocks, count):
    at = (b + pos_ref[0] * (blocks // 2)) % blocks
    return (idx_ref[pl.ds(at, 1), :] - pos_ref[1] * count).astype(f32)


def clip_of(clip_ref, pos_ref, b, blocks, sets, own):
    half = blocks // 2
    if own:
        return clip_ref[blocks * (pos_ref[1] % sets) + (b + pos_ref[0] * half) % blocks]
    return clip_ref[blocks * (b // blocks) + (b % blocks + pos_ref[0] * half) % blocks]


def cross_forward_body(
    pos_ref, idx_ref, lat_ref, src_ref, gain_one_ref, gain_src_ref, wq_ref, wk_ref, wv_ref,
    n1_ref, ns_ref, q_ref, kvp_ref, keep_ref, send_ref, kv_s, picks_s, *, steps,
):
    i = pl.program_id(0)
    width = wq_ref.shape[1]
    heads = width // HEAD
    rows_src = src_ref.shape[0]
    norm_into(ns_ref, src_ref, gain_src_ref)
    normed_src = ns_ref[...]
    row0 = pl.multiple_of(i * rows_src, rows_src)
    kv_s[pl.ds(row0, rows_src), 0:width] = dot(normed_src, wk_ref[...]).astype(bf16)
    kv_s[pl.ds(row0, rows_src), width:] = dot(normed_src, wv_ref[...]).astype(bf16)
    norm_into(n1_ref, lat_ref, gain_one_ref)
    normed_one = n1_ref[...]
    grp0 = pl.multiple_of(i * GROUP, GROUP)
    q_ref[pl.ds(grp0, GROUP), :] = dot(normed_one, wq_ref[...]).astype(bf16)

    @pl.when(i == steps - 1)
    def _():
        count = kv_s.shape[0]
        lanes = lax.broadcasted_iota(jnp.int32, (128, count), 1).astype(f32)
        for b in range(steps):
            for part in range(SRC // 128):
                row = index_row(idx_ref, pos_ref, b, steps, count)[:, part * 128 : (part + 1) * 128]
                column = jnp.transpose(jnp.broadcast_to(row, (128, 128)))
                picks = jnp.where(jnp.tile(column, (1, count // 128)) == lanes, 1.0, 0.0).astype(bf16)
                r0 = b * SRC + part * 128
                picks_s[r0 : r0 + 128, :] = picks
        kvp_ref[...] = dot(picks_s[...], kv_s[...]).astype(bf16)
        for b in range(steps):
            for h in range(heads):
                cols = slice(h * HEAD, (h + 1) * HEAD)
                q = q_ref[b * GROUP : (b + 1) * GROUP, cols]
                k = kvp_ref[b * SRC : (b + 1) * SRC, cols]
                v = kvp_ref[b * SRC : (b + 1) * SRC, width + h * HEAD : width + (h + 1) * HEAD]
                s = dot_t(q, k) * (HEAD ** (-0.5) * LOG2E)
                p = jnp.exp2(s - jnp.max(s, axis=-1, keepdims=True))
                total = jnp.sum(p, axis=-1, keepdims=True)
                mixed = (dot(p.astype(bf16), v) / total).astype(bf16)
                if b < steps // 2:
                    keep_ref[b * GROUP : (b + 1) * GROUP, cols] = mixed
                else:
                    r0 = (b - steps // 2) * GROUP
                    send_ref[r0 : r0 + GROUP, cols] = mixed


def cross_forward(pos, idx, latents, sources, gain_one, gain_src, wq, wk, wv):
    rows, width_d = latents.shape
    steps = rows // GROUP
    count = sources.shape[0]
    blk = count // steps
    width = wq.shape[1]
    whole = lambda shape: pl.BlockSpec(shape, lambda i, c: (0,) * len(shape))
    return call(
        functools.partial(cross_forward_body, steps=steps),
        [
            (sds((rows, width_d), bf16), pl.BlockSpec((GROUP, width_d), lambda i, c: (i, 0))),
            (sds((count, width_d), bf16), pl.BlockSpec((blk, width_d), lambda i, c: (i, 0))),
            (sds((rows, width), bf16), whole((rows, width))),
            (sds((count, 2 * width), bf16), whole((count, 2 * width))),
            (sds((rows // 2, width), bf16), whole((rows // 2, width))),
            (sds((rows // 2, width), bf16), whole((rows // 2, width))),
        ],
        [
            whole(idx.shape),
            pl.BlockSpec((GROUP, width_d), lambda i, c: ((i + c[0] * (steps // 2)) % steps, 0)),
            pl.BlockSpec((blk, width_d), lambda i, c: (i, 0)),
            whole((1, width_d)),
            whole((1, width_d)),
            whole(wq.shape),
            whole(wk.shape),
            whole(wv.shape),
        ],
        (pos, idx, latents, sources, gain_one, gain_src, wq, wk, wv),
        "cross_forward",
        scratch=[pltpu.VMEM((count, 2 * width), bf16), pltpu.VMEM((count, count), bf16)],
        grid=(steps,),
        prefetch=1,
        flops=4e9,
        nbytes=12e6,
        spare=44,
    )


def project_body(pos_ref, *refs, parts, own_half):
    pieces, weights = refs[:parts], refs[parts : 2 * parts]
    base_ref, gain_ref, after_ref, normed_ref, left_s, right_s = refs[2 * parts :]
    half = after_ref.shape[0]
    width = pieces[0].shape[1]
    for k in range(parts):
        at = pl.multiple_of((pos_ref[2] ^ k) * width, width)
        left_s[:, pl.ds(at, width)] = pieces[k][...]
        right_s[pl.ds(at, width), :] = weights[k][...]
    after_ref[...] = dot(left_s[...], right_s[...])
    first = pos_ref[0] * half if own_half else 0
    gain_vec = gain_ref[...]

    def step(r, held):
        base = base_ref[pl.ds(pl.multiple_of(first + r.start, CHUNK), CHUNK), :]
        after = base.astype(f32) + after_ref[r, :]
        after_ref[r, :] = after
        normed_ref[r, :] = (centre(after)[0] * gain_vec).astype(bf16)
        return held

    by_chunks(half, step)


def project(pos, pieces, weights, base, gain, own_half, ties=()):
    parts = len(pieces)
    half, width = pieces[0].shape
    width_d = weights[0].shape[1]
    return call(
        functools.partial(project_body, parts=parts, own_half=own_half),
        [(sds((half, width_d), f32), VMEM), (sds((half, width_d), bf16), VMEM)],
        [SMEM] + [VMEM] * (2 * parts + 2),
        (pos, *pieces, *weights, base, gain),
        "project",
        scratch=[pltpu.VMEM((half, parts * width), bf16), pltpu.VMEM((parts * width, width_d), bf16)],
        flops=2 * half * width * parts * width_d,
        nbytes=5e6,
        ties=ties,
    )


def qkv_body(mine_ref, other_ref, wq_ref, wk_ref, wv_ref, q_ref, kv_ref):
    half = mine_ref.shape[0]
    width = wq_ref.shape[1]
    for part, ref in enumerate((mine_ref, other_ref)):
        rows = slice(part * half, (part + 1) * half)
        x = ref[...]
        kv_ref[rows, 0:width] = dot(x, wk_ref[...]).astype(bf16)
        kv_ref[rows, width:] = dot(x, wv_ref[...]).astype(bf16)
        q_ref[rows, :] = dot(x, wq_ref[...]).astype(bf16)


def qkv(mine, other, wq, wk, wv):
    half, width_d = mine.shape
    width = wq.shape[1]
    return call(
        qkv_body,
        [(sds((2 * half, width), bf16), VMEM), (sds((2 * half, 2 * width), bf16), VMEM)],
        [VMEM] * 5,
        (mine, other, wq, wk, wv),
        "qkv",
        flops=2 * 2 * half * width_d * 3 * width,
        nbytes=4e6,
    )


def assemble(refs, entries, dst, rows_blocks):
    for ri, base, p, k in entries:
        for j in range(rows_blocks):
            dst[p * rows_blocks + j, pl.ds(place_start(k), GROUP), :] = refs[ri][
                base + j * GROUP : base + (j + 1) * GROUP, :
            ]


def place_start(k):
    return k * GROUP if isinstance(k, int) else pl.multiple_of(k * GROUP, GROUP)


def split_rows(rows_value):
    high = rows_value.astype(bf16)
    rest = rows_value - high.astype(f32)
    middle = rest.astype(bf16)
    low = (rest - middle.astype(f32)).astype(bf16)
    return high, middle, low


def pack_extra(row_tiles, heads, blocks, width):
    per_row = width // 128
    out = []
    for h in range(heads):
        flat = [
            jnp.concatenate(row_tiles[h][r * per_row : (r + 1) * per_row], axis=1)
            for r in range(blocks // per_row)
        ]
        rows_value = jnp.concatenate(flat, axis=0)
        out += [part.astype(f32) for part in split_rows(rows_value)]
    used = heads * 3 * (blocks // per_row)
    if used < EXTRA:
        out.append(jnp.zeros((EXTRA - used, width), f32))
    return jnp.concatenate(out, axis=0).astype(bf16)


def unpack_extra(extra, h, j, blocks, width):
    per_row = width // 128
    rows_per = blocks // per_row
    row, lane = j // per_row, (j % per_row) * 128
    parts = [
        extra[(h * 3 + t) * rows_per + row : (h * 3 + t) * rows_per + row + 1, lane : lane + 128]
        for t in range(3)
    ]
    return (parts[0] + parts[1]) + parts[2]


def attend_body(
    pos_ref, clip_ref, *refs, pieces, entries, heads, blocks, period,
):
    q_ref = refs[0]
    kv_refs = refs[1 : 1 + pieces]
    keep_ref, send_ref, lsex_ref, lsec_ref, kv_s, m_s, l_s, acc_s, row_s, o_s = refs[1 + pieces :]
    width = heads * HEAD
    sets = period // blocks
    assemble(kv_refs, entries, kv_s, blocks)

    def per_block(i, carry):
        r0 = pl.multiple_of(i * GROUP, GROUP)
        own_clip = clip_of(clip_ref, pos_ref, i, blocks, sets, True)
        m_s[...] = jnp.full(m_s.shape, masked_value, f32)
        l_s[...] = jnp.zeros(l_s.shape, f32)
        acc_s[...] = jnp.zeros(acc_s.shape, f32)

        def per_keys(g, inner):
            @pl.when(own_clip == clip_of(clip_ref, pos_ref, g, blocks, sets, False))
            def _():
                for h in range(heads):
                    cols = slice(h * HEAD, (h + 1) * HEAD)
                    q = q_ref[pl.ds(r0, GROUP), cols]
                    k = kv_s[g, :, cols]
                    v = kv_s[g, :, width + h * HEAD : width + (h + 1) * HEAD]
                    s = dot_t(q, k) * (HEAD ** (-0.5) * LOG2E)
                    m_old = m_s[h][:, 0:1]
                    m_new = jnp.maximum(m_old, jnp.max(s, axis=-1, keepdims=True))
                    p = jnp.exp2(s - m_new)
                    alpha = jnp.exp2(m_old - m_new)
                    l_new = l_s[h][:, 0:1] * alpha + jnp.sum(p, axis=-1, keepdims=True)
                    acc_s[h] = acc_s[h] * alpha + dot(p.astype(bf16), v)
                    m_s[h] = jnp.broadcast_to(m_new, (GROUP, 128))
                    l_s[h] = jnp.broadcast_to(l_new, (GROUP, 128))

            return inner

        lax.fori_loop(0, period, per_keys, 0)
        for h in range(heads):
            total = l_s[h]
            o_s[pl.ds(r0, GROUP), h * HEAD : (h + 1) * HEAD] = (acc_s[h] / total).astype(bf16)
            lse = m_s[h] + jnp.log2(total)
            lsec_ref[h, pl.ds(r0, GROUP), :] = lse
            row_s[h, i] = jnp.transpose(lse)[0:8]
        return carry

    lax.fori_loop(0, blocks, per_block, 0)
    half = blocks // 2 * GROUP
    keep_ref[...] = o_s[0:half, :]
    send_ref[...] = o_s[half:, :]
    tiles = [[row_s[h, j][0:1] for j in range(blocks)] for h in range(heads)]
    lsex_ref[...] = pack_extra(tiles, heads, blocks, width)


def attend(pos, clips, q, kv_pieces, entries, ties):
    rows, width = q.shape
    heads, blocks, period = width // HEAD, rows // GROUP, clips.shape[0] // GROUPS_FRAME
    pieces = len(kv_pieces)
    body = functools.partial(
        attend_body, pieces=pieces, entries=entries, heads=heads, blocks=blocks, period=period
    )
    return call(
        body,
        [
            (sds((rows // 2, width), bf16), VMEM),
            (sds((rows // 2, width), bf16), VMEM),
            (sds((EXTRA, width), bf16), VMEM),
            (sds((heads, rows, 128), f32), VMEM),
        ],
        [SMEM, SMEM] + [VMEM] * (1 + pieces),
        (pos, clips, q, *kv_pieces),
        "attend",
        ties=ties,
        scratch=[
            pltpu.VMEM((period, GROUPS_FRAME * GROUP, 2 * width), bf16),
            pltpu.VMEM((heads, GROUP, 128), f32),
            pltpu.VMEM((heads, GROUP, 128), f32),
            pltpu.VMEM((heads, GROUP, HEAD), f32),
            pltpu.VMEM((heads, blocks, 8, 128), f32),
            pltpu.VMEM((rows, width), bf16),
        ],
        flops=2e9,
        nbytes=7e6,
        trans=2e6,
    )


def out_back_body(mine_ref, other_ref, wo_ref, okeep_ref, osend_ref, lsex_ref, dox_ref, dc_ref, *, heads, blocks):
    half = mine_ref.shape[0]
    rows = 2 * half
    tiles = [[] for h in range(heads)]
    for part, (ref, o_ref) in enumerate(((mine_ref, okeep_ref), (other_ref, osend_ref))):
        grad = dot_t(ref[...], wo_ref[...]).astype(bf16)
        dox_ref[part * half : (part + 1) * half, :] = grad
        product = grad.astype(f32) * o_ref[...].astype(f32)
        for h in range(heads):
            delta = jnp.sum(product[:, h * HEAD : (h + 1) * HEAD], axis=-1, keepdims=True)
            delta = jnp.broadcast_to(delta, (half, 128))
            dc_ref[h, part * half : (part + 1) * half, :] = delta
            for j in range(half // GROUP):
                tiles[h].append(jnp.transpose(delta[j * GROUP : (j + 1) * GROUP])[0:1])
    dox_ref[rows : rows + EXTRA, :] = pack_extra(tiles, heads, blocks, heads * HEAD)
    dox_ref[rows + EXTRA :, :] = lsex_ref[...]


def out_back(mine, other, wo, okeep, osend, lsex):
    half, width_d = mine.shape
    width = wo.shape[0]
    heads, blocks = width // HEAD, 2 * half // GROUP
    return call(
        functools.partial(out_back_body, heads=heads, blocks=blocks),
        [(sds((2 * half + 2 * EXTRA, width), bf16), VMEM), (sds((heads, 2 * half, 128), f32), VMEM)],
        [VMEM] * 6,
        (mine, other, wo, okeep, osend, lsex),
        "out_back",
        flops=2 * 2 * half * width * width_d,
        nbytes=4e6,
    )


def query_back_body(pos_ref, clip_ref, *refs, pieces, entries, heads, blocks, period):
    qx_ref, dox_ref, lsec_ref, dc_ref = refs[0:4]
    kv_refs = refs[4 : 4 + pieces]
    dq_ref, kv_s, acc_s = refs[4 + pieces :]
    width = heads * HEAD
    sets = period // blocks
    assemble(kv_refs, entries, kv_s, blocks)

    def per_block(i, carry):
        r0 = pl.multiple_of(i * GROUP, GROUP)
        own_clip = clip_of(clip_ref, pos_ref, i, blocks, sets, True)
        acc_s[...] = jnp.zeros(acc_s.shape, f32)

        def per_keys(g, inner):
            @pl.when(own_clip == clip_of(clip_ref, pos_ref, g, blocks, sets, False))
            def _():
                for h in range(heads):
                    cols = slice(h * HEAD, (h + 1) * HEAD)
                    k = kv_s[g, :, cols]
                    v = kv_s[g, :, width + h * HEAD : width + (h + 1) * HEAD]
                    s = dot_t(qx_ref[pl.ds(r0, GROUP), cols], k) * (HEAD ** (-0.5) * LOG2E)
                    p = jnp.exp2(s - lsec_ref[h, pl.ds(r0, GROUP), :][:, 0:1])
                    dp = dot_t(dox_ref[pl.ds(r0, GROUP), cols], v)
                    delta = dc_ref[h, pl.ds(r0, GROUP), :][:, 0:1]
                    ds = (p * (dp - delta) * (HEAD ** (-0.5))).astype(bf16)
                    acc_s[h] = acc_s[h] + dot(ds, k)

            return inner

        lax.fori_loop(0, period, per_keys, 0)
        for h in range(heads):
            dq_ref[pl.ds(r0, GROUP), h * HEAD : (h + 1) * HEAD] = acc_s[h].astype(bf16)
        return carry

    lax.fori_loop(0, blocks, per_block, 0)


def query_back(pos, clips, qx, dox, lsec, dc, kv_pieces, entries):
    rows, width = qx.shape
    heads, blocks, period = width // HEAD, rows // GROUP, clips.shape[0] // GROUPS_FRAME
    pieces = len(kv_pieces)
    return call(
        functools.partial(
            query_back_body, pieces=pieces, entries=entries, heads=heads, blocks=blocks, period=period
        ),
        [(sds((rows, width), bf16), VMEM)],
        [SMEM, SMEM] + [VMEM] * (4 + pieces),
        (pos, clips, qx, dox, lsec, dc, *kv_pieces),
        "query_back",
        scratch=[
            pltpu.VMEM((period, GROUPS_FRAME * GROUP, 2 * width), bf16),
            pltpu.VMEM((heads, GROUP, HEAD), f32),
        ],
        flops=2e9,
        nbytes=7e6,
        trans=2e6,
    )[0]


def key_back_body(
    pos_ref, clip_ref, *refs, q_pieces, do_pieces, q_entries, do_entries, heads, blocks, period
):
    kv_ref, dq_ref, wq_ref, wk_ref, wv_ref = refs[0:5]
    qx_refs = refs[5 : 5 + q_pieces]
    dox_refs = refs[5 + q_pieces : 5 + q_pieces + do_pieces]
    dqkv_ref, keep_ref, send_ref, q_s, do_s, lse_s, delta_s, dk_s, dv_s = refs[5 + q_pieces + do_pieces :]
    width = heads * HEAD
    rows = blocks * GROUP
    sets = period // blocks
    assemble(qx_refs, q_entries, q_s, blocks)
    assemble(dox_refs, do_entries, do_s, blocks)
    for first, target in ((rows, delta_s), (rows + EXTRA, lse_s)):
        for ri, base, p, k in do_entries:
            extra = dox_refs[ri][base + first : base + first + EXTRA, :].astype(f32)
            for h in range(heads):
                for j in range(blocks):
                    line = unpack_extra(extra, h, j, blocks, width)
                    target[p * blocks + j, h, :, pl.ds(place_start(k), GROUP)] = jnp.broadcast_to(
                        line, (8, 128)
                    )
    dqkv_ref[:, 0:width] = dq_ref[...]

    def per_block(j, carry):
        r0 = pl.multiple_of(j * GROUP, GROUP)
        own_clip = clip_of(clip_ref, pos_ref, j, blocks, sets, True)
        dk_s[...] = jnp.zeros(dk_s.shape, f32)
        dv_s[...] = jnp.zeros(dv_s.shape, f32)

        def per_queries(g, inner):
            @pl.when(own_clip == clip_of(clip_ref, pos_ref, g, blocks, sets, False))
            def _():
                for h in range(heads):
                    cols = slice(h * HEAD, (h + 1) * HEAD)
                    k = kv_ref[pl.ds(r0, GROUP), cols]
                    v = kv_ref[pl.ds(r0, GROUP), width + h * HEAD : width + (h + 1) * HEAD]
                    q = q_s[g, :, cols]
                    do = do_s[g, :, cols]
                    st = dot_t(k, q) * (HEAD ** (-0.5) * LOG2E)
                    pt = jnp.exp2(st - lse_s[g, h, 0:1, :])
                    dv_s[h] = dv_s[h] + dot(pt.astype(bf16), do)
                    dpt = dot_t(v, do)
                    dst = (pt * (dpt - delta_s[g, h, 0:1, :]) * (HEAD ** (-0.5))).astype(bf16)
                    dk_s[h] = dk_s[h] + dot(dst, q)

            return inner

        lax.fori_loop(0, period, per_queries, 0)
        for h in range(heads):
            dqkv_ref[pl.ds(r0, GROUP), width + h * HEAD : width + (h + 1) * HEAD] = dk_s[h].astype(bf16)
            dqkv_ref[pl.ds(r0, GROUP), 2 * width + h * HEAD : 2 * width + (h + 1) * HEAD] = dv_s[
                h
            ].astype(bf16)
        return carry

    lax.fori_loop(0, blocks, per_block, 0)
    half = rows // 2
    for part, ref in enumerate((keep_ref, send_ref)):
        r = slice(part * half, (part + 1) * half)
        total = dot_t(dqkv_ref[r, 0:width], wq_ref[...])
        total = total + dot_t(dqkv_ref[r, width : 2 * width], wk_ref[...])
        total = total + dot_t(dqkv_ref[r, 2 * width :], wv_ref[...])
        ref[...] = total.astype(bf16)


def key_back(pos, clips, kv, dq, wq, wk, wv, qx_pieces, q_entries, dox_pieces, do_entries, ties):
    rows, width = dq.shape
    width_d = wq.shape[0]
    heads, blocks, period = width // HEAD, rows // GROUP, clips.shape[0] // GROUPS_FRAME
    tall = GROUPS_FRAME * GROUP
    return call(
        functools.partial(
            key_back_body, q_pieces=len(qx_pieces), do_pieces=len(dox_pieces), q_entries=q_entries,
            do_entries=do_entries, heads=heads, blocks=blocks, period=period,
        ),
        [
            (sds((rows, 3 * width), bf16), VMEM),
            (sds((rows // 2, width_d), bf16), VMEM),
            (sds((rows // 2, width_d), bf16), VMEM),
        ],
        [SMEM, SMEM] + [VMEM] * (5 + len(qx_pieces) + len(dox_pieces)),
        (pos, clips, kv, dq, wq, wk, wv, *qx_pieces, *dox_pieces),
        "key_back",
        ties=ties,
        scratch=[
            pltpu.VMEM((period, tall, width), bf16),
            pltpu.VMEM((period, tall, width), bf16),
            pltpu.VMEM((period, heads, 8, tall), f32),
            pltpu.VMEM((period, heads, 8, tall), f32),
            pltpu.VMEM((heads, GROUP, HEAD), f32),
            pltpu.VMEM((heads, GROUP, HEAD), f32),
        ],
        flops=4e9,
        nbytes=9e6,
        trans=2e6,
    )


def mlp_body(mine_ref, other_ref, win_ref, ag_ref, act_ref, hg_ref, keep_ref, send_ref, *, steps):
    i = pl.program_id(0)
    x = jnp.where(i < steps // 2, mine_ref[...], other_ref[...])
    units = win_ref.shape[1]
    chunk = 512
    total = None
    for n in range(units // chunk):
        cols = slice(n * chunk, (n + 1) * chunk)
        w = win_ref[:, cols]
        hidden = dot(x, w)
        cdf = 0.5 * (1.0 + lax.erf(hidden * 0.7071067811865476))
        act_ref[:, cols] = (hidden * cdf).astype(bf16)
        density = jnp.exp2(hidden * hidden * (-0.5 * LOG2E)) * 0.3989422804014327
        grad = (ag_ref[:, cols] * (cdf + hidden * density)).astype(bf16)
        hg_ref[:, cols] = grad
        term = dot_t(grad, w)
        total = term if total is None else total + term
    total = total.astype(bf16)

    @pl.when(i < steps // 2)
    def _():
        keep_ref[...] = total

    @pl.when(i >= steps // 2)
    def _():
        send_ref[...] = total


def mlp(mine, other, w_in, act_grad):
    half, width_d = mine.shape
    units = w_in.shape[1]
    steps = 2
    rows = 2 * half
    low = lambda i: (jnp.minimum(i, steps // 2 - 1), 0)
    high = lambda i: (jnp.maximum(i - steps // 2, 0), 0)
    return call(
        functools.partial(mlp_body, steps=steps),
        [
            (sds((rows, units), bf16), pl.BlockSpec((half, units), lambda i: (i, 0))),
            (sds((rows, units), bf16), pl.BlockSpec((half, units), lambda i: (i, 0))),
            (sds((half, width_d), bf16), pl.BlockSpec((half, width_d), low)),
            (sds((half, width_d), bf16), pl.BlockSpec((half, width_d), high)),
        ],
        [
            pl.BlockSpec((half, width_d), low),
            pl.BlockSpec((half, width_d), high),
            pl.BlockSpec((width_d, units), lambda i: (0, 0)),
            pl.BlockSpec((half, units), lambda i: (i, 0)),
        ],
        (mine, other, w_in, act_grad),
        "mlp",
        spare=10,
        grid=(steps,),
        flops=4 * rows * width_d * units,
        nbytes=9e6,
        trans=2 * rows * units,
    )


def mlp_down_body(act_ref, w_ref, keep_ref, send_ref, *, steps):
    i = pl.program_id(0)
    total = dot(act_ref[...], w_ref[...]).astype(bf16)

    @pl.when(i < steps // 2)
    def _():
        keep_ref[...] = total

    @pl.when(i >= steps // 2)
    def _():
        send_ref[...] = total


def mlp_down(activated, w_out, ties):
    rows, units = activated.shape
    width_d = w_out.shape[1]
    steps = 2
    blk = rows // steps
    half = sds((blk, width_d), bf16)
    return call(
        functools.partial(mlp_down_body, steps=steps),
        [
            (half, pl.BlockSpec((blk, width_d), lambda i: (jnp.minimum(i, steps // 2 - 1), 0))),
            (half, pl.BlockSpec((blk, width_d), lambda i: (jnp.maximum(i - steps // 2, 0), 0))),
        ],
        [
            pl.BlockSpec((blk, units), lambda i: (i, 0)),
            pl.BlockSpec((units, width_d), lambda i: (0, 0)),
        ],
        (activated, w_out),
        "mlp_down",
        grid=(steps,),
        flops=2 * rows * units * width_d,
        nbytes=4e6,
        ties=ties,
    )


def act_back_body(pos_ref, og_ref, w_ref, rel_ref, ag_ref):
    rel_ref[...] = og_ref[...]
    ag_ref[...] = dot_t(og_ref[...], w_ref[...])


def act_back(pos, out_grad, w_out):
    rows, width_d = out_grad.shape
    units = w_out.shape[0]
    steps = rows // GROUP
    blk = pl.BlockSpec((GROUP, width_d), lambda i, c: (i, 0))
    return call(
        act_back_body,
        [
            (sds((rows, width_d), bf16), blk),
            (sds((rows, units), f32), pl.BlockSpec((GROUP, units), lambda i, c: (i, 0))),
        ],
        [
            pl.BlockSpec((GROUP, width_d), lambda i, c: ((i + c[0] * (steps // 2)) % steps, 0)),
            pl.BlockSpec((units, width_d), lambda i, c: (0, 0)),
        ],
        (pos, out_grad, w_out),
        "act_back",
        grid=(steps,),
        prefetch=1,
        flops=2 * rows * width_d * units,
        nbytes=6e6,
    )


def through_norm(n, v, gain_vec):
    unit, inverse = centre(v)
    t = n * gain_vec
    back = inverse * (
        t - jnp.mean(t, axis=-1, keepdims=True) - unit * jnp.mean(t * unit, axis=-1, keepdims=True)
    )
    return back, unit


def norm_back_body(s_ref, r_ref, v_ref, gain_ref, base_ref, after_ref, branch_ref, gg_ref):
    gain_vec = gain_ref[...]

    def step(r, held):
        n = s_ref[r, :].astype(f32) + r_ref[r, :].astype(f32)
        back, unit = through_norm(n, v_ref[r, :], gain_vec)
        after = base_ref[r, :].astype(f32) + back
        after_ref[r, :] = after
        branch_ref[r, :] = after.astype(bf16)
        return held + folded(n * unit)

    total = by_chunks(s_ref.shape[0], step, jnp.zeros((8, s_ref.shape[1]), f32))
    gg_ref[...] = jnp.sum(total, axis=0, keepdims=True)


def norm_back(s, r, v, gain, base, ties):
    half, width_d = s.shape
    return call(
        norm_back_body,
        [
            (sds((half, width_d), f32), VMEM),
            (sds((half, width_d), bf16), VMEM),
            (sds((1, width_d), f32), VMEM),
        ],
        [VMEM] * 5,
        (s, r, v, gain, base),
        "norm_back",
        ties=ties,
        flops=20 * half * width_d,
        nbytes=5e6,
    )


def final_body(
    pos_ref, s_ref, r_ref, lat_ref, src_ref, gain_one_ref, gain_src_ref, base_ref, half_ref, lat_out, src_out, *, first,
):
    def run(v_ref, gain_ref, base, out_ref):
        gain_vec = gain_ref[...]

        def step(r, held):
            n = s_ref[r, :].astype(f32) + r_ref[r, :].astype(f32)
            back = through_norm(n, v_ref[r, :].astype(f32), gain_vec)[0]
            if base is not None:
                back = base[r, :] + back
            half_ref[r, :] = back.astype(bf16)
            out_ref[r, :] = back.astype(bf16)
            return held

        by_chunks(s_ref.shape[0], step)

    i = pl.program_id(0)
    pl.when(i < first)(lambda: run(lat_ref, gain_one_ref, base_ref, lat_out))
    pl.when(i >= first)(lambda: run(src_ref, gain_src_ref, None, src_out))


def final_norm(pos, s, r, latents, sources, gain_one, gain_src, base, ties):
    width_d = s.shape[1]
    blk = 128
    one, src = latents.shape[0] // 2 // blk, sources.shape[0] // 2 // blk
    at_one = lambda i: jnp.minimum(i, one - 1)
    at_src = lambda i: jnp.maximum(i - one, 0)
    spec = lambda f: pl.BlockSpec((blk, width_d), lambda i, c: (f(i, c), 0))
    gain_spec = pl.BlockSpec((1, width_d), lambda i, c: (0, 0))
    own_one, own_src = spec(lambda i, c: c[0] * one + at_one(i)), spec(lambda i, c: c[0] * src + at_src(i))
    each = spec(lambda i, c: i)
    return call(
        functools.partial(final_body, first=one),
        [(sds(s.shape, bf16), each), (sds(latents.shape, bf16), own_one), (sds(sources.shape, bf16), own_src)],
        [each, each, own_one, own_src, gain_spec, gain_spec, spec(lambda i, c: at_one(i))],
        (pos, s, r, latents, sources, gain_one, gain_src, base),
        "final_norm",
        grid=(one + src,),
        prefetch=1,
        flops=20 * s.size,
        nbytes=8 * s.size,
        ties=ties,
    )


def place_both_body(pos_ref, other_ref, lat_in, src_in, lat_out, src_out):
    i = pl.program_id(0)

    @pl.when(i == 0)
    def _():
        lat_out[...] = other_ref[...]

    @pl.when(i > 0)
    def _():
        src_out[...] = other_ref[...]


def place_both(pos, other, lat_whole, src_whole):
    blk, width_d = lat_whole.shape[0] // 2, other.shape[1]
    steps = other.shape[0] // blk
    spec = lambda f: pl.BlockSpec((blk, width_d), lambda i, c: (f(i, c), 0))
    return call(
        place_both_body,
        [
            (sds(lat_whole.shape, bf16), spec(lambda i, c: 1 - c[0])),
            (sds(src_whole.shape, bf16), spec(lambda i, c: (1 - c[0]) * (steps - 1) + jnp.maximum(i - 1, 0))),
        ],
        [spec(lambda i, c: i), ANY, ANY],
        (pos, other, lat_whole, src_whole),
        "place_both",
        grid=(steps,),
        prefetch=1,
        nbytes=4 * other.size,
        aliases={2: 0, 3: 1},
    )


def place_body(pos_ref, other_ref, whole_ref, out_ref):
    out_ref[...] = other_ref[...]


def place_other(pos, whole, other):
    half, width_d = other.shape
    rows = 256
    steps = half // rows
    return call(
        place_body,
        [(sds(whole.shape, bf16), pl.BlockSpec((rows, width_d), lambda i, c: ((1 - c[0]) * steps + i, 0)))],
        [pl.BlockSpec((rows, width_d), lambda i, c: (i, 0)), ANY],
        (pos, other, whole),
        "place_other",
        grid=(steps,),
        prefetch=1,
        nbytes=4 * half * width_d,
        aliases={2: 0},
    )[0]


def result_body(pos_ref, s_ref, r_ref, after_ref, half_ref, whole_ref, squares_ref):
    def step(r, held):
        result = after_ref[r, :] + (s_ref[r, :].astype(f32) + r_ref[r, :].astype(f32))
        half_ref[r, :] = result.astype(bf16)
        whole_ref[r, :] = result.astype(bf16)
        return held + folded(result * result)

    total = by_chunks(s_ref.shape[0], step, jnp.zeros((8, s_ref.shape[1]), f32))
    squares_ref[pl.ds(pl.program_id(0), 1), :] = jnp.sum(total, axis=0, keepdims=True)


def result_half(pos, s, r, after):
    half, width_d = s.shape
    steps = half // GROUP
    blk = pl.BlockSpec((GROUP, width_d), lambda i, c: (i, 0))
    own = pl.BlockSpec((GROUP, width_d), lambda i, c: (c[0] * steps + i, 0))
    return call(
        result_body,
        [
            (sds((half, width_d), bf16), blk),
            (sds((2 * half, width_d), bf16), own),
            (sds((steps, width_d), f32), pl.BlockSpec((steps, width_d), lambda i, c: (0, 0))),
        ],
        [blk] * 3,
        (pos, s, r, after),
        "result",
        grid=(steps,),
        prefetch=1,
        flops=6 * half * width_d,
        nbytes=5e6,
    )


def gains_body(
    pos_ref, clip_ref, frames_ref, keep, send, lat_ref, src_ref,
    self_ref, mlp_ref, squares_ref, out_ref, *, one_steps, src_steps, blocks, sets, copies, clips,
):
    i = pl.program_id(0)

    @pl.when(i == 0)
    def _():
        width_d = out_ref.shape[1]
        share = jnp.zeros((1, 1), f32)
        for b in range(blocks // 2):
            total = jnp.sum(squares_ref[b : b + 1, :], axis=1, keepdims=True)
            frames = frames_ref[clip_of(clip_ref, pos_ref, b, blocks, sets, True)].astype(f32)
            norm = jnp.sqrt(total / (GROUP * width_d) + 1e-06)
            share = share + norm / (jnp.broadcast_to(frames, (1, 1)) * (GROUPS_FRAME * clips))
        out_ref[0:2, :] = jnp.zeros((2, width_d), f32)
        out_ref[2:3, :] = self_ref[...] * copies
        out_ref[3:4, :] = mlp_ref[...] * copies
        out_ref[4:8, :] = jnp.broadcast_to(share * copies, (4, width_d))

    def add(row, v_ref, keep_ref, send_ref, kept):
        def step(r, held):
            n = jnp.where(kept, keep_ref[r, :].astype(f32), send_ref[r, :].astype(f32))
            return held + folded(n * centre(v_ref[r, :].astype(f32))[0])

        total = by_chunks(v_ref.shape[0], step, jnp.zeros((8, v_ref.shape[1]), f32))
        out_ref[row : row + 1, :] = out_ref[row : row + 1, :] + jnp.sum(total, axis=0, keepdims=True)

    pl.when(i < one_steps)(lambda: add(1, lat_ref, keep, send, i < one_steps // 2))
    pl.when(i >= one_steps)(lambda: add(0, src_ref, keep, send, i - one_steps < src_steps // 2))


def gains(pos, clips, frames, keep, send, latents, sources, self_gain, mlp_gain, squares, copies, ties):
    rows, width_d = latents.shape
    count = sources.shape[0]
    blk = 256
    one_steps, src_steps = rows // blk, count // blk
    one_half, src_half = one_steps // 2, src_steps // 2
    blocks = rows // GROUP
    sets = clips.shape[0] // GROUPS_FRAME // blocks
    clamp = lambda v, top: jnp.minimum(jnp.maximum(v, 0), top)
    spec = lambda f: pl.BlockSpec((blk, width_d), lambda i, *c: (f(i, c[0]), 0))
    fixed = lambda n: pl.BlockSpec((n, width_d), lambda i, *c: (0, 0))
    turn = lambda i, c, steps: (clamp(i, steps - 1) + c[0] * (steps // 2)) % steps
    kept = lambda i, c: jnp.where(
        i < one_steps, clamp(i, one_half - 1), one_half + clamp(i - one_steps, src_half - 1)
    )
    sent = lambda i, c: jnp.where(
        i < one_steps, clamp(i - one_half, one_half - 1), one_half + clamp(i - one_steps - src_half, src_half - 1)
    )
    return call(
        functools.partial(
            gains_body, one_steps=one_steps, src_steps=src_steps, blocks=blocks, sets=sets, copies=copies,
            clips=frames.shape[0],
        ),
        [(sds((8, width_d), f32), fixed(8))],
        [
            spec(kept),
            spec(sent),
            spec(lambda i, c: turn(i, c, one_steps)),
            spec(lambda i, c: turn(i - one_steps, c, src_steps)),
            fixed(1), fixed(1), fixed(blocks // 2),
        ],
        (pos, clips, frames, keep, send, latents, sources, self_gain, mlp_gain, squares),
        "gains",
        grid=(one_steps + src_steps,),
        prefetch=3,
        flops=20 * (rows + count) * width_d,
        nbytes=4 * (rows + count) * width_d,
        ties=ties,
    )[0]


def feature_grads_body(pos_ref, *refs, items, sends, blk):
    given = sum(a + b for a, b in items)
    keep_ref, send_refs = refs[given], refs[given + 1 :]
    at, column = 0, 0
    for lefts, rights in items:
        total, row = None, 0
        for k in range(lefts):
            left = refs[at + k]
            rows = left.shape[0]
            if rights == 1:
                right = refs[at + lefts][row : row + rows, :]
            else:
                right = refs[at + lefts + k][...]
            term = dot_ta(left[...], right)
            total = term if total is None else total + term
            row += rows
        at += lefts + rights
        first, column = column, column + total.shape[1]
        total = total.astype(bf16)
        for j in range(blk // 128):
            part = total[j * 128 : (j + 1) * 128]
            if sends == 0:
                keep_ref[j, :, first:column] = part
                continue
            mine = (pos_ref[1] + j) % 2 == 0

            @pl.when(mine)
            def _():
                keep_ref[j // 2, :, first:column] = part

            @pl.when(jnp.logical_not(mine))
            def _():
                width = send_refs[0].shape[2]
                for h, ref in enumerate(send_refs):
                    low, high = max(first, h * width), min(column, (h + 1) * width)
                    if low < high:
                        ref[j // 2, :, low - h * width : high - h * width] = part[:, low - first : high - first]


def feature_grads(pos, items, sends, ties=()):
    arrays, specs, counts, columns, flops = [], [], [], 0, 0
    features = items[0][0][0].shape[1]
    blk = 512
    for lefts, rights in items:
        counts.append((len(lefts), len(rights)))
        for v in lefts:
            arrays.append(v)
            specs.append(pl.BlockSpec((v.shape[0], blk), lambda i, c: (0, i)))
            flops += 2 * v.shape[0] * v.shape[1] * rights[0].shape[1]
        for v in rights:
            arrays.append(v)
            specs.append(pl.BlockSpec(v.shape, lambda i, c: (0, 0)))
        columns += rights[0].shape[1]
    steps = features // blk
    sets = features // 256 if sends else features // 128
    out = lambda n: (sds((sets, 128, n), bf16), pl.BlockSpec((sets // steps, 128, n), lambda i, c: (i, 0, 0)))
    return call(
        functools.partial(feature_grads_body, items=tuple(counts), sends=sends, blk=blk),
        [out(columns)] + [out(columns // sends)] * sends if sends else [out(columns)],
        specs,
        (pos, *arrays),
        "feature_grads",
        grid=(steps,),
        prefetch=1,
        flops=flops,
        nbytes=2 * features * columns + sum(2 * v.size for v in arrays),
        ties=ties,
    )


def stage_one_body(pos_ref, keep_ref, *refs):
    z = pos_ref[1] // 2
    gots, (own_ref, send_ref) = refs[:-2], refs[-2:]
    width = gots[0].shape[2]
    for h, got_ref in enumerate(gots):
        cols = slice(h * width, (h + 1) * width)
        for k in range(2):
            at = z ^ (2 * k)
            own_ref[k, :, cols] = keep_ref[at, :, cols].astype(f32) + got_ref[at].astype(f32)
            at = z ^ 1 ^ (2 * k)
            send_ref[k, :, cols] = (keep_ref[at, :, cols].astype(f32) + got_ref[at].astype(f32)).astype(bf16)


def stage_one(pos, keep, gots, ties=()):
    shape = (2, *keep.shape[1:])
    return call(
        stage_one_body,
        [(sds(shape, f32), VMEM), (sds(shape, bf16), VMEM)],
        [SMEM] + [VMEM] * (1 + len(gots)),
        (pos, keep, *gots),
        "stage_one",
        nbytes=4 * keep.size,
        ties=ties,
    )


def stage_two_body(keep_ref, got_ref, own_ref, send_ref):
    own_ref[...] = keep_ref[0] + got_ref[0].astype(f32)
    send_ref[...] = (keep_ref[1] + got_ref[1].astype(f32)).astype(bf16)


def stage_two(keep, got, ties=()):
    shape = keep.shape[1:]
    return call(
        stage_two_body,
        [(sds(shape, f32), VMEM), (sds(shape, bf16), VMEM)],
        [VMEM] * 2,
        (keep, got),
        "stage_two",
        nbytes=4 * keep.size,
        ties=ties,
    )


def stage_end_body(own_ref, got_ref, *outs, turned):
    total = own_ref[...] + got_ref[...].astype(f32)
    width = total.shape[1] // len(outs)
    for k, ref in enumerate(outs):
        part = total[:, k * width : (k + 1) * width]
        ref[...] = part.T if k in turned else part


def stage_end(own, got, parts, turned, ties=()):
    blk = own.shape
    width = blk[1] // parts
    return call(
        functools.partial(stage_end_body, turned=turned),
        [(sds((width, blk[0]) if k in turned else (blk[0], width), f32), VMEM) for k in range(parts)],
        [VMEM] * 2,
        (own, got),
        "stage_end",
        nbytes=10 * blk[0] * blk[1],
        ties=ties,
    )


def flip_x(v):
    return lax.ppermute(v, "seq", xor_pairs(1, 8))


def near_z(v):
    return lax.ppermute(v, "seq", xor_pairs(2, 8))


def far_z(v):
    return lax.ppermute(v, "seq", xor_pairs(4, 8))


def scatter_whole(pos, items, parts, turned, ties):
    whole = feature_grads(pos, items, 0, ties)[0]
    whole = whole.reshape(-1, whole.shape[2])
    total = lax.psum_scatter(whole, "seq", scatter_dimension=0, tiled=True).astype(f32)
    width = total.shape[1] // parts
    pieces = [total[:, k * width : (k + 1) * width] for k in range(parts)]
    return [piece.T if k in turned else piece for k, piece in enumerate(pieces)]


def tied(values, other):
    out = lax.optimization_barrier((other, *values))
    return list(out[1:]), out[0]


def cross_back_body(
    pos_ref, mine_ref, other_ref, wo_ref, q_ref, kvp_ref, idx_ref, wq_ref, wk_ref, wv_ref,
    dq_ref, dk_ref, dv_ref, keep_ref, send_ref, dkvp_s, grad_s, *, blocks,
):
    width = wq_ref.shape[1]
    heads = width // HEAD
    count = kvp_ref.shape[0]
    scale = HEAD ** (-0.5)
    rows = blocks * GROUP
    for part, ref in enumerate((mine_ref, other_ref)):
        grad_s[part * rows // 2 : (part + 1) * rows // 2, :] = dot_t(ref[...], wo_ref[...]).astype(bf16)
    for b in range(blocks):
        for h in range(heads):
            cols = slice(h * HEAD, (h + 1) * HEAD)
            vcols = slice(width + h * HEAD, width + (h + 1) * HEAD)
            q = q_ref[b * GROUP : (b + 1) * GROUP, cols]
            k = kvp_ref[b * SRC : (b + 1) * SRC, cols]
            v = kvp_ref[b * SRC : (b + 1) * SRC, vcols]
            do = grad_s[b * GROUP : (b + 1) * GROUP, cols]
            s = dot_t(q, k) * (scale * LOG2E)
            p = jnp.exp2(s - jnp.max(s, axis=-1, keepdims=True))
            p = p / jnp.sum(p, axis=-1, keepdims=True)
            dp = dot_t(do, v)
            delta = jnp.sum(p * dp, axis=-1, keepdims=True)
            ds = (p * (dp - delta) * scale).astype(bf16)
            dq_ref[b * GROUP : (b + 1) * GROUP, cols] = dot(ds, k).astype(bf16)
            dkvp_s[b * SRC : (b + 1) * SRC, cols] = dot_ta(ds, q).astype(bf16)
            dkvp_s[b * SRC : (b + 1) * SRC, vcols] = dot_ta(p.astype(bf16), do).astype(bf16)
    one = dot_t(dq_ref[...], wq_ref[...]).astype(bf16)
    keep_ref[0 : rows // 2, :] = one[0 : rows // 2]
    send_ref[0 : rows // 2, :] = one[rows // 2 :]
    half = count // 2
    row = jnp.concatenate([index_row(idx_ref, pos_ref, b, blocks, count) for b in range(blocks)], axis=1)
    for part, ref in enumerate((keep_ref, send_ref)):
        r0 = pl.multiple_of((pos_ref[0] if part == 0 else 1 - pos_ref[0]) * half, half)
        wanted = lax.broadcasted_iota(jnp.int32, (half, count), 0).astype(f32) + r0.astype(f32)
        picks = jnp.where(row == wanted, 1.0, 0.0).astype(bf16)
        dkv = dot(picks, dkvp_s[...]).astype(bf16)
        dk_ref[pl.ds(r0, half), :] = dkv[:, 0:width]
        dv_ref[pl.ds(r0, half), :] = dkv[:, width:]
        total = dot_t(dkv[:, 0:width], wk_ref[...]) + dot_t(dkv[:, width:], wv_ref[...])
        ref[rows // 2 :, :] = total.astype(bf16)


def cross_back(pos, mine, other, wo, q, kvp, idx, wq, wk, wv, ties):
    rows, width = q.shape
    width_d = wq.shape[0]
    count = kvp.shape[0]
    blocks = rows // GROUP
    return call(
        functools.partial(cross_back_body, blocks=blocks),
        [
            (sds((rows, width), bf16), VMEM),
            (sds((count, width), bf16), VMEM),
            (sds((count, width), bf16), VMEM),
            (sds(((rows + count) // 2, width_d), bf16), VMEM),
            (sds(((rows + count) // 2, width_d), bf16), VMEM),
        ],
        [SMEM] + [VMEM] * 9,
        (pos, mine, other, wo, q, kvp, idx, wq, wk, wv),
        "cross_back",
        ties=ties,
        scratch=[pltpu.VMEM((count, 2 * width), bf16), pltpu.VMEM((rows, width), bf16)],
        spare=14,
        flops=4e9,
        nbytes=12e6,
    )


def xor_pairs(bit, size):
    return [(i, i ^ bit) for i in range(size)]


def ring_pairs(d):
    return [(s, ((s // 2 + d) % 4) * 2 + s % 2) for s in range(8)]


def tensor_swap(x, bit):
    return lax.ppermute(x, "tensor", xor_pairs(bit, lax.axis_size("tensor")))


def seq_gather(x, between=None, guest=None):
    size = lax.axis_size("seq")
    if size == 8:
        move = lambda v, pairs: lax.ppermute(v, "seq", pairs)
        flip = xor_pairs(1, 8)
        beside = move(x, flip)
        up = move(x, ring_pairs(1))
        down = move(x, ring_pairs(-1))
        if guest is not None:
            (beside, up, guest), between = tied([beside, up, guest], between)
            guest = flip_x(guest)
        far = move(up, ring_pairs(1))
        down_beside = move(beside, ring_pairs(-1))
        if guest is not None:
            up_beside = move(beside, ring_pairs(1))
            (far_sent, up_beside), down_beside = tied([far, up_beside], down_beside)
        else:
            up_beside = move(up, flip)
            far_sent = far
        far_beside = move(far_sent, flip)
        pieces = [x, beside, up, down, far, up_beside, down_beside, far_beside]
    else:
        pieces = gather_whole(x)
    return pieces if guest is None else (pieces, between, guest)


def gather_whole(x):
    return [lax.all_gather(x, "seq", axis=0, tiled=True)]


def gather_entries(size, rows, sets):
    if size == 8:
        return tuple((k, 0, 0, k) for k in range(8))
    return whole_entries(size, rows, sets)


def whole_entries(size, rows, sets):
    return tuple((0, s * rows, s % sets, s // sets) for s in range(size))


def half_sum(keep, send):
    size = lax.axis_size("tensor")
    got = tensor_swap(send, 1)
    own = (keep.astype(f32) + got.astype(f32)).astype(bf16)
    bit = 2
    while True:
        other = tensor_swap(own, bit)
        if bit * 2 >= size:
            return own, other
        own = (own.astype(f32) + other.astype(f32)).astype(bf16)
        bit *= 2


def tensor_pieces(keep, send):
    size = lax.axis_size("tensor")
    return [keep if k == 0 else tensor_swap(send if k % 2 else keep, k) for k in range(size)]


def weight_far(weight):
    pieces = {0: weight}
    bit = lax.axis_size("tensor") // 2
    while bit >= 2:
        pieces.update({k + bit: tensor_swap(v, bit) for k, v in list(pieces.items())})
        bit //= 2
    return pieces


def weight_pieces(pieces):
    pieces = dict(pieces)
    pieces.update({k + 1: tensor_swap(v, 1) for k, v in list(pieces.items())})
    return [pieces[k] for k in range(len(pieces))]


def tie_all(pieces, other):
    keys = sorted(pieces)
    tied = lax.optimization_barrier((other, *[pieces[k] for k in keys]))
    return dict(zip(keys, tied[1:])), tied[0]


def sum_over(v, axis, only):
    size = lax.axis_size(axis)
    bit = only or 1
    while bit < size:
        v = v + lax.ppermute(v, axis, xor_pairs(bit, size))
        bit = size if only else bit * 2
    return v


def local(
    latents, sources, source_index, block_clip, clip_frames, norm_src, norm_cross, norm_self, norm_mlp,
    cross_q, cross_k, cross_v, cross_o, self_q, self_k, self_v, self_o, mlp_in, mlp_out, out_grad,
):
    rows, width_d = latents.shape
    blocks = rows // GROUP
    width = cross_q.shape[1]
    units = mlp_in.shape[1]
    tensor_size, seq_size = lax.axis_size("tensor"), lax.axis_size("seq")
    core = lax.axis_index("tensor") % 2
    pos = jnp.stack((core, lax.axis_index("seq"), lax.axis_index("tensor"))).astype(jnp.int32)
    sets = block_clip.shape[0] // GROUPS_FRAME // blocks
    gain = lambda g: g.reshape(1, width_d)
    kv_entries = gather_entries(seq_size, rows, sets)
    out_entries = gather_entries(seq_size, rows + 2 * EXTRA, sets)

    cross_o_far = weight_far(cross_o)
    normed_one, normed_src, cross_query, cross_kv, mixed_keep, mixed_send = cross_forward(
        pos, source_index, latents, sources, gain(norm_cross), gain(norm_src), cross_q, cross_k, cross_v
    )
    cross_o_far, mixed_keep = tie_all(cross_o_far, mixed_keep)
    after_cross, two_mine = project(
        pos, tensor_pieces(mixed_keep, mixed_send), weight_pieces(cross_o_far), latents, gain(norm_self), True
    )
    two_other = tensor_swap(two_mine, 1)
    query, key_value = qkv(two_mine, two_other, self_q, self_k, self_v)
    kv_pieces = seq_gather(key_value)
    self_o_tied, two_mine = tie_all({0: self_o}, two_mine)
    self_o_all = weight_pieces(weight_far(self_o_tied[0]))
    out_rel, act_grad = act_back(pos, out_grad, mlp_out)
    split = seq_size == 8
    query_pieces = seq_gather(query)
    self_keep, self_send, lse_rows, lse_columns = attend(
        pos, block_clip, query, kv_pieces, kv_entries, (act_grad, *self_o_all[1:])
    )
    after_self, three_mine = project(
        pos, tensor_pieces(self_keep, self_send), self_o_all, after_cross, gain(norm_mlp), False,
        query_pieces[1:4],
    )
    three_other = tensor_swap(three_mine, 1)
    activated, hidden_grad, three_keep, three_send = mlp(three_mine, three_other, mlp_in, act_grad)

    three_sum, three_got = half_sum(three_keep, three_send)
    in_items = (((three_mine, three_other), (hidden_grad,)),)
    out_items = (((out_rel,), (activated,)),)
    early = ()
    if split:
        in_keep, in_send = feature_grads(pos, in_items, 1, (three_sum,))
        out_keep, out_send_a, out_send_b = feature_grads(pos, out_items, 2, (in_keep,))
        early = (out_keep, *query_pieces[4:])
    down_keep, down_send = mlp_down(activated, mlp_out, (three_sum, *early[0:1]))
    early = (*early, down_keep)
    after_self_grad, self_branch, mlp_gain = norm_back(
        three_sum, three_got, after_self, gain(norm_mlp), out_rel, early
    )
    self_branch_other = tensor_swap(self_branch, 1)

    out_more, delta_columns = out_back(self_branch, self_branch_other, self_o, self_keep, self_send, lse_rows)
    self_query_grad = query_back(
        pos, block_clip, query, out_more, lse_columns, delta_columns, kv_pieces, kv_entries
    )
    if split:
        out_pieces, self_query_grad, in_got = seq_gather(out_more, self_query_grad, in_send)
    else:
        out_pieces = seq_gather(out_more)
    result_sum, result_got = half_sum(down_keep, down_send)
    output_half, output_whole, squares = result_half(pos, result_sum, result_got, after_self)
    output = place_other(pos, output_whole, tensor_swap(output_half, 1))
    early = ()
    if split:
        in_keep, in_send = stage_one(pos, in_keep, [in_got])
        (out_send_a, in_send), out_pieces[-1] = tied([out_send_a, in_send], out_pieces[-1])
        out_got_a = flip_x(out_send_a)
        early = (squares,)
    self_grads, two_keep, two_send = key_back(
        pos, block_clip, key_value, self_query_grad, self_q, self_k, self_v,
        query_pieces, kv_entries, out_pieces, out_entries, early,
    )
    if split:
        (two_send, out_send_b), out_got_a = tied([two_send, out_send_b], out_got_a)
        out_got_b = flip_x(out_send_b)
        in_got = near_z(in_send)
    two_sum, two_got = half_sum(two_keep, two_send)
    self_items = (
        ((two_mine, two_other), (self_grads,)),
        ((self_branch, self_branch_other), (self_keep, self_send)),
    )
    early = ()
    if split:
        self_wkeep, self_send_a, self_send_b = feature_grads(pos, self_items, 2, (two_sum,))
        in_own, in_send = stage_two(in_keep, in_got, (self_wkeep,))
        out_keep, out_send = stage_one(pos, out_keep, [out_got_a, out_got_b], (in_send,))
        early = (self_wkeep, in_own, out_keep, output)
    after_cross_grad, cross_branch, self_gain = norm_back(
        two_sum, two_got, after_cross, gain(norm_self), after_self_grad, early
    )
    cross_branch_other = tensor_swap(cross_branch, 1)

    if split:
        (self_send_a, in_send), cross_branch_other = tied([self_send_a, in_send], cross_branch_other)
        self_got_a = flip_x(self_send_a)
        in_got = far_z(in_send)
    cross_query_grad, cross_key_grad, cross_value_grad, both_keep, both_send = cross_back(
        pos, cross_branch, cross_branch_other, cross_o, cross_query, cross_kv, source_index,
        cross_q, cross_k, cross_v, (),
    )
    cross_items = (
        ((normed_one,), (cross_query_grad,)),
        ((normed_src,), (cross_key_grad,)),
        ((normed_src,), (cross_value_grad,)),
        ((cross_branch, cross_branch_other), (mixed_keep, mixed_send)),
    )
    gains_of = lambda ties: gains(
        pos, block_clip, clip_frames, both_keep, both_send, latents, sources,
        self_gain, mlp_gain, squares, 2.0 / tensor_size, ties,
    )
    final_of = lambda ties: final_norm(
        pos, both_sum, both_got, latents, sources, gain(norm_cross), gain(norm_src), after_cross_grad, ties
    )
    if split:
        both_send, self_send_b, out_send, self_got_a, in_got = lax.optimization_barrier(
            (both_send, self_send_b, out_send, self_got_a, in_got)
        )
        self_got_b = flip_x(self_send_b)
        out_got = near_z(out_send)
        both_sum, both_got = half_sum(both_keep, both_send)
        cross_wkeep, cross_wsend = feature_grads(pos, cross_items, 1, (both_sum,))
        out_own, out_send = stage_two(out_keep, out_got, (cross_wkeep,))
        self_wkeep, self_wsend = stage_one(pos, self_wkeep, [self_got_a, self_got_b], (out_own,))

        cross_wsend, out_send, self_wsend = lax.optimization_barrier((cross_wsend, out_send, self_wsend))
        cross_wgot = flip_x(cross_wsend)
        out_got = far_z(out_send)
        self_wgot = near_z(self_wsend)
        mlp_outs = stage_end(in_own, in_got, 1, (), (self_wsend,))
        small = gains_of((cross_wsend, mlp_outs[0]))
        small = sum_over(sum_over(small, "tensor", 1), "seq", 1)
        self_own, self_wsend = stage_two(self_wkeep, self_wgot, (out_got, small))
        self_wgot = far_z(self_wsend)
        cross_wkeep, cross_wsend = stage_one(pos, cross_wkeep, [cross_wgot], (self_wsend,))

        cross_wsend, small = lax.optimization_barrier((cross_wsend, small))
        cross_wgot = near_z(cross_wsend)
        both_half, lat_whole, src_whole = final_of(())
        mlp_outs = [*mlp_outs, stage_end(out_own, out_got, 1, (0,), (both_half,))[0]]
        small, both_half = lax.optimization_barrier((small, both_half))
        near, far, both = [lax.ppermute(small, "seq", xor_pairs(bit, 8)) for bit in (2, 4, 6)]
        small = (small + near) + (far + both)
        cross_own, cross_wsend = stage_two(cross_wkeep, cross_wgot, (self_wgot, small, mlp_outs[1]))

        cross_wsend, small, both_half = lax.optimization_barrier((cross_wsend, small, both_half))
        cross_wgot = far_z(cross_wsend)
        bit = 2
        while bit < tensor_size:
            small = sum_over(small, "tensor", bit)
            bit *= 2
        self_outs = stage_end(self_own, self_wgot, 4, (3,))
        latents_grad, sources_grad = place_both(pos, tensor_swap(both_half, 1), lat_whole, src_whole)
        cross_outs = stage_end(cross_own, cross_wgot, 4, (3,), (latents_grad, self_outs[0]))
    else:
        both_sum, both_got = half_sum(both_keep, both_send)
        small = gains_of((both_sum,))
        small = sum_over(small, "tensor", 0)
        small = sum_over(small, "seq", 0)
        both_half, lat_whole, src_whole = final_of(())
        latents_grad, sources_grad = place_both(pos, tensor_swap(both_half, 1), lat_whole, src_whole)
        cross_outs = scatter_whole(pos, cross_items, 4, (3,), ())
        self_outs = scatter_whole(pos, self_items, 4, (3,), ())
        mlp_outs = scatter_whole(pos, in_items, 1, (), ()) + scatter_whole(pos, out_items, 1, (0,), ())
    return (
        output, latents_grad, sources_grad, small[0], small[1], small[2], small[3],
        *cross_outs, *self_outs, *mlp_outs, small[4, 0],
    )


def solution(mesh):
    in_specs = (
        P("seq", None), P("seq", None), P("seq", None), P(), P(), P(), P(), P(), P(),
        P(None, "tensor"), P(None, "tensor"), P(None, "tensor"), P("tensor", None),
        P(None, "tensor"), P(None, "tensor"), P(None, "tensor"), P("tensor", None),
        P(None, "tensor"), P("tensor", None), P("seq", None),
    )
    out_specs = (
        P("seq", None), P("seq", None), P("seq", None), P(), P(), P(), P(),
        P("seq", "tensor"), P("seq", "tensor"), P("seq", "tensor"), P("tensor", "seq"),
        P("seq", "tensor"), P("seq", "tensor"), P("seq", "tensor"), P("tensor", "seq"),
        P("seq", "tensor"), P("tensor", "seq"), P(),
    )
    return jax.shard_map(local, mesh=mesh, in_specs=in_specs, out_specs=out_specs, check_vma=False)
```

```python
import functools
import math

import jax
import jax.numpy as jnp
from jax import lax
from jax.experimental import pallas as pl
from jax.experimental.pallas import tpu as pltpu
from jax.sharding import PartitionSpec as P

HEAD = 128
GROUP = 128
SRC = 256
GROUPS_FRAME = 8
LOG2E = 1.4426950408889634
epsilon = 1e-05
masked_value = -1e30
bf16 = jnp.bfloat16
f32 = jnp.float32
EXTRA = 16
WEIGHT = 1

VMEM = pl.BlockSpec(memory_space=pltpu.VMEM)
SMEM = pl.BlockSpec(memory_space=pltpu.SMEM)


def sds(shape, dtype):
    return jax.ShapeDtypeStruct(shape, dtype)


def dot(a, b):
    return lax.dot_general(a, b, (((1,), (0,)), ((), ())), preferred_element_type=f32)


def dot_t(a, b):
    return lax.dot_general(a, b, (((1,), (1,)), ((), ())), preferred_element_type=f32)


def dot_ta(a, b):
    return lax.dot_general(a, b, (((0,), (0,)), ((), ())), preferred_element_type=f32)


def centre(values):
    centred = values - jnp.mean(values, axis=-1, keepdims=True)
    variance = jnp.mean(centred * centred, axis=-1, keepdims=True)
    inverse = lax.rsqrt(variance + epsilon)
    return centred * inverse, inverse


ANY = pl.BlockSpec(memory_space=pl.ANY)
CHUNK = 64


def by_chunks(rows, step, carry=0):
    for first in range(0, rows, CHUNK):
        carry = step(slice(first, first + CHUNK), carry)
    return carry


def norm_into(out_ref, in_ref, gain_ref):
    gain_vec = gain_ref[...]

    def step(r, held):
        out_ref[r, :] = (centre(in_ref[r, :].astype(f32))[0] * gain_vec).astype(bf16)
        return held

    by_chunks(in_ref.shape[0], step)


def folded(rows_value):
    parts = [rows_value[k : k + 8] for k in range(0, CHUNK, 8)]
    while len(parts) > 1:
        parts = [parts[k] + parts[k + 1] for k in range(0, len(parts), 2)]
    return parts[0]


def call(
    body, outs, ins, args, name, scratch=(), grid=None, prefetch=0, flops=0, nbytes=0, trans=0, ties=(), aliases=None,
    spare=6,
):
    given = prefetch + len(ins)
    room = 0
    for spec, v in [*zip(ins, args[prefetch:]), *[(spec, shape) for shape, spec in outs]]:
        if spec.block_shape is not None:
            room += 2 * math.prod(spec.block_shape) * v.dtype.itemsize
        elif spec is VMEM:
            room += math.prod(v.shape) * v.dtype.itemsize
    room += sum(math.prod(v.shape) * jnp.dtype(v.dtype).itemsize for v in scratch)

    def run(*refs):
        body(*refs[:given], *refs[given + len(ties) :])

    return pl.pallas_call(
        run,
        out_shape=[shape for shape, ignored in outs],
        grid_spec=pltpu.PrefetchScalarGridSpec(
            num_scalar_prefetch=prefetch,
            grid=() if grid is None else grid,
            in_specs=list(ins) + [ANY] * len(ties),
            out_specs=[spec for ignored, spec in outs],
            scratch_shapes=list(scratch),
        ),
        compiler_params=pltpu.CompilerParams(vmem_limit_bytes=room + spare * 2**20),
        cost_estimate=pl.CostEstimate(
            flops=int(flops * WEIGHT), bytes_accessed=int(nbytes * WEIGHT), transcendentals=int(trans * WEIGHT)
        ),
        input_output_aliases=aliases or {},
        name=name,
    )(*args, *ties)


def index_row(idx_ref, pos_ref, b, blocks, count):
    at = (b + pos_ref[0] * (blocks // 2)) % blocks
    return (idx_ref[pl.ds(at, 1), :] - pos_ref[1] * count).astype(f32)


def clip_of(clip_ref, pos_ref, b, blocks, sets, own):
    half = blocks // 2
    if own:
        return clip_ref[blocks * (pos_ref[1] % sets) + (b + pos_ref[0] * half) % blocks]
    return clip_ref[blocks * (b // blocks) + (b % blocks + pos_ref[0] * half) % blocks]


def cross_forward_body(
    pos_ref, idx_ref, lat_ref, src_ref, gain_one_ref, gain_src_ref, wq_ref, wk_ref, wv_ref,
    n1_ref, ns_ref, q_ref, kvp_ref, keep_ref, send_ref, kv_s, picks_s, *, steps, groups,
):
    i = pl.program_id(0)
    width = wq_ref.shape[1]
    heads = width // HEAD
    rows_src = src_ref.shape[0]
    norm_into(ns_ref, src_ref, gain_src_ref)
    normed_src = ns_ref[...]
    row0 = pl.multiple_of(i * rows_src, rows_src)
    kv_s[pl.ds(row0, rows_src), 0:width] = dot(normed_src, wk_ref[...]).astype(bf16)
    kv_s[pl.ds(row0, rows_src), width:] = dot(normed_src, wv_ref[...]).astype(bf16)
    norm_into(n1_ref, lat_ref, gain_one_ref)
    normed_one = n1_ref[...]
    rows_lat = lat_ref.shape[0]
    q_ref[pl.ds(pl.multiple_of(i * rows_lat, rows_lat), rows_lat), :] = dot(normed_one, wq_ref[...]).astype(bf16)

    @pl.when(i == steps - 1)
    def _():
        count = kv_s.shape[0]
        lanes = lax.broadcasted_iota(jnp.int32, (128, count), 1).astype(f32)
        for b in range(groups):
            for part in range(SRC // 128):
                row = index_row(idx_ref, pos_ref, b, groups, count)[:, part * 128 : (part + 1) * 128]
                column = jnp.transpose(jnp.broadcast_to(row, (128, 128)))
                picks = jnp.where(jnp.tile(column, (1, count // 128)) == lanes, 1.0, 0.0).astype(bf16)
                r0 = b * SRC + part * 128
                picks_s[r0 : r0 + 128, :] = picks
        kvp_ref[...] = dot(picks_s[...], kv_s[...]).astype(bf16)
        for b in range(groups):
            for h in range(heads):
                cols = slice(h * HEAD, (h + 1) * HEAD)
                q = q_ref[b * GROUP : (b + 1) * GROUP, cols]
                k = kvp_ref[b * SRC : (b + 1) * SRC, cols]
                v = kvp_ref[b * SRC : (b + 1) * SRC, width + h * HEAD : width + (h + 1) * HEAD]
                s = dot_t(q, k) * (HEAD ** (-0.5) * LOG2E)
                p = jnp.exp2(s - jnp.max(s, axis=-1, keepdims=True))
                total = jnp.sum(p, axis=-1, keepdims=True)
                mixed = (dot(p.astype(bf16), v) / total).astype(bf16)
                if b < groups // 2:
                    keep_ref[b * GROUP : (b + 1) * GROUP, cols] = mixed
                else:
                    r0 = (b - groups // 2) * GROUP
                    send_ref[r0 : r0 + GROUP, cols] = mixed


def cross_forward(pos, idx, latents, sources, gain_one, gain_src, wq, wk, wv):
    rows, width_d = latents.shape
    steps = 2
    lat_blk = rows // steps
    count = sources.shape[0]
    blk = count // steps
    width = wq.shape[1]
    whole = lambda shape: pl.BlockSpec(shape, lambda i, c: (0,) * len(shape))
    return call(
        functools.partial(cross_forward_body, steps=steps, groups=rows // GROUP),
        [
            (sds((rows, width_d), bf16), pl.BlockSpec((lat_blk, width_d), lambda i, c: (i, 0))),
            (sds((count, width_d), bf16), pl.BlockSpec((blk, width_d), lambda i, c: (i, 0))),
            (sds((rows, width), bf16), whole((rows, width))),
            (sds((count, 2 * width), bf16), whole((count, 2 * width))),
            (sds((rows // 2, width), bf16), whole((rows // 2, width))),
            (sds((rows // 2, width), bf16), whole((rows // 2, width))),
        ],
        [
            whole(idx.shape),
            pl.BlockSpec((lat_blk, width_d), lambda i, c: ((i + c[0] * (steps // 2)) % steps, 0)),
            pl.BlockSpec((blk, width_d), lambda i, c: (i, 0)),
            whole((1, width_d)),
            whole((1, width_d)),
            whole(wq.shape),
            whole(wk.shape),
            whole(wv.shape),
        ],
        (pos, idx, latents, sources, gain_one, gain_src, wq, wk, wv),
        "cross_forward",
        scratch=[pltpu.VMEM((count, 2 * width), bf16), pltpu.VMEM((count, count), bf16)],
        grid=(steps,),
        prefetch=1,
        flops=4e9,
        nbytes=12e6,
        spare=44,
    )


def project_body(pos_ref, *refs, parts, own_half):
    pieces, weights = refs[:parts], refs[parts : 2 * parts]
    base_ref, gain_ref, after_ref, normed_ref, left_s, right_s = refs[2 * parts :]
    half = after_ref.shape[0]
    width = pieces[0].shape[1]
    for k in range(parts):
        at = pl.multiple_of((pos_ref[2] ^ k) * width, width)
        left_s[:, pl.ds(at, width)] = pieces[k][...]
        right_s[pl.ds(at, width), :] = weights[k][...]
    after_ref[...] = dot(left_s[...], right_s[...])
    first = pos_ref[0] * half if own_half else 0
    gain_vec = gain_ref[...]

    def step(r, held):
        base = base_ref[pl.ds(pl.multiple_of(first + r.start, CHUNK), CHUNK), :]
        after = base.astype(f32) + after_ref[r, :]
        after_ref[r, :] = after
        normed_ref[r, :] = (centre(after)[0] * gain_vec).astype(bf16)
        return held

    by_chunks(half, step)


def project(pos, pieces, weights, base, gain, own_half, ties=()):
    parts = len(pieces)
    half, width = pieces[0].shape
    width_d = weights[0].shape[1]
    return call(
        functools.partial(project_body, parts=parts, own_half=own_half),
        [(sds((half, width_d), f32), VMEM), (sds((half, width_d), bf16), VMEM)],
        [SMEM] + [VMEM] * (2 * parts + 2),
        (pos, *pieces, *weights, base, gain),
        "project",
        scratch=[pltpu.VMEM((half, parts * width), bf16), pltpu.VMEM((parts * width, width_d), bf16)],
        flops=2 * half * width * parts * width_d,
        nbytes=5e6,
        ties=ties,
    )


def qkv_body(mine_ref, other_ref, wq_ref, wk_ref, wv_ref, q_ref, kv_ref):
    half = mine_ref.shape[0]
    width = wq_ref.shape[1]
    for part, ref in enumerate((mine_ref, other_ref)):
        rows = slice(part * half, (part + 1) * half)
        x = ref[...]
        kv_ref[rows, 0:width] = dot(x, wk_ref[...]).astype(bf16)
        kv_ref[rows, width:] = dot(x, wv_ref[...]).astype(bf16)
        q_ref[rows, :] = dot(x, wq_ref[...]).astype(bf16)


def qkv(mine, other, wq, wk, wv):
    half, width_d = mine.shape
    width = wq.shape[1]
    return call(
        qkv_body,
        [(sds((2 * half, width), bf16), VMEM), (sds((2 * half, 2 * width), bf16), VMEM)],
        [VMEM] * 5,
        (mine, other, wq, wk, wv),
        "qkv",
        flops=2 * 2 * half * width_d * 3 * width,
        nbytes=4e6,
    )


def assemble(refs, entries, dst, rows_blocks):
    for ri, base, p, k in entries:
        for j in range(rows_blocks):
            dst[p * rows_blocks + j, pl.ds(place_start(k), GROUP), :] = refs[ri][
                base + j * GROUP : base + (j + 1) * GROUP, :
            ]


def place_start(k):
    return k * GROUP if isinstance(k, int) else pl.multiple_of(k * GROUP, GROUP)


def split_rows(rows_value):
    high = rows_value.astype(bf16)
    rest = rows_value - high.astype(f32)
    middle = rest.astype(bf16)
    low = (rest - middle.astype(f32)).astype(bf16)
    return high, middle, low


def pack_extra(row_tiles, heads, blocks, width):
    per_row = width // 128
    out = []
    for h in range(heads):
        flat = [
            jnp.concatenate(row_tiles[h][r * per_row : (r + 1) * per_row], axis=1)
            for r in range(blocks // per_row)
        ]
        rows_value = jnp.concatenate(flat, axis=0)
        out += [part.astype(f32) for part in split_rows(rows_value)]
    used = heads * 3 * (blocks // per_row)
    if used < EXTRA:
        out.append(jnp.zeros((EXTRA - used, width), f32))
    return jnp.concatenate(out, axis=0).astype(bf16)


def unpack_extra(extra, h, j, blocks, width):
    per_row = width // 128
    rows_per = blocks // per_row
    row, lane = j // per_row, (j % per_row) * 128
    parts = [
        extra[(h * 3 + t) * rows_per + row : (h * 3 + t) * rows_per + row + 1, lane : lane + 128]
        for t in range(3)
    ]
    return (parts[0] + parts[1]) + parts[2]


def attend_body(
    pos_ref, clip_ref, *refs, pieces, entries, heads, blocks, period,
):
    q_ref = refs[0]
    kv_refs = refs[1 : 1 + pieces]
    keep_ref, send_ref, lsex_ref, lsec_ref, kv_s, m_s, l_s, acc_s, row_s, o_s = refs[1 + pieces :]
    width = heads * HEAD
    sets = period // blocks
    assemble(kv_refs, entries, kv_s, blocks)

    def per_block(i, carry):
        r0 = pl.multiple_of(i * GROUP, GROUP)
        own_clip = clip_of(clip_ref, pos_ref, i, blocks, sets, True)
        m_s[...] = jnp.full(m_s.shape, masked_value, f32)
        l_s[...] = jnp.zeros(l_s.shape, f32)
        acc_s[...] = jnp.zeros(acc_s.shape, f32)

        def per_keys(g, inner):
            @pl.when(own_clip == clip_of(clip_ref, pos_ref, g, blocks, sets, False))
            def _():
                for h in range(heads):
                    cols = slice(h * HEAD, (h + 1) * HEAD)
                    q = q_ref[pl.ds(r0, GROUP), cols]
                    k = kv_s[g, :, cols]
                    v = kv_s[g, :, width + h * HEAD : width + (h + 1) * HEAD]
                    s = dot_t(q, k) * (HEAD ** (-0.5) * LOG2E)
                    m_old = m_s[h][:, 0:1]
                    m_new = jnp.maximum(m_old, jnp.max(s, axis=-1, keepdims=True))
                    p = jnp.exp2(s - m_new)
                    alpha = jnp.exp2(m_old - m_new)
                    l_new = l_s[h][:, 0:1] * alpha + jnp.sum(p, axis=-1, keepdims=True)
                    acc_s[h] = acc_s[h] * alpha + dot(p.astype(bf16), v)
                    m_s[h] = jnp.broadcast_to(m_new, (GROUP, 128))
                    l_s[h] = jnp.broadcast_to(l_new, (GROUP, 128))

            return inner

        lax.fori_loop(0, period, per_keys, 0)
        for h in range(heads):
            total = l_s[h]
            o_s[pl.ds(r0, GROUP), h * HEAD : (h + 1) * HEAD] = (acc_s[h] / total).astype(bf16)
            lse = m_s[h] + jnp.log2(total)
            lsec_ref[h, pl.ds(r0, GROUP), :] = lse
            row_s[h, i] = jnp.transpose(lse)[0:8]
        return carry

    lax.fori_loop(0, blocks, per_block, 0)
    half = blocks // 2 * GROUP
    keep_ref[...] = o_s[0:half, :]
    send_ref[...] = o_s[half:, :]
    tiles = [[row_s[h, j][0:1] for j in range(blocks)] for h in range(heads)]
    lsex_ref[...] = pack_extra(tiles, heads, blocks, width)


def attend(pos, clips, q, kv_pieces, entries, ties):
    rows, width = q.shape
    heads, blocks, period = width // HEAD, rows // GROUP, clips.shape[0] // GROUPS_FRAME
    pieces = len(kv_pieces)
    body = functools.partial(
        attend_body, pieces=pieces, entries=entries, heads=heads, blocks=blocks, period=period
    )
    return call(
        body,
        [
            (sds((rows // 2, width), bf16), VMEM),
            (sds((rows // 2, width), bf16), VMEM),
            (sds((EXTRA, width), bf16), VMEM),
            (sds((heads, rows, 128), f32), VMEM),
        ],
        [SMEM, SMEM] + [VMEM] * (1 + pieces),
        (pos, clips, q, *kv_pieces),
        "attend",
        ties=ties,
        scratch=[
            pltpu.VMEM((period, GROUPS_FRAME * GROUP, 2 * width), bf16),
            pltpu.VMEM((heads, GROUP, 128), f32),
            pltpu.VMEM((heads, GROUP, 128), f32),
            pltpu.VMEM((heads, GROUP, HEAD), f32),
            pltpu.VMEM((heads, blocks, 8, 128), f32),
            pltpu.VMEM((rows, width), bf16),
        ],
        flops=2e9,
        nbytes=7e6,
        trans=2e6,
    )


def out_back_body(mine_ref, other_ref, wo_ref, okeep_ref, osend_ref, lsex_ref, dox_ref, dc_ref, *, heads, blocks):
    half = mine_ref.shape[0]
    rows = 2 * half
    tiles = [[] for h in range(heads)]
    for part, (ref, o_ref) in enumerate(((mine_ref, okeep_ref), (other_ref, osend_ref))):
        grad = dot_t(ref[...], wo_ref[...]).astype(bf16)
        dox_ref[part * half : (part + 1) * half, :] = grad
        product = grad.astype(f32) * o_ref[...].astype(f32)
        for h in range(heads):
            delta = jnp.sum(product[:, h * HEAD : (h + 1) * HEAD], axis=-1, keepdims=True)
            delta = jnp.broadcast_to(delta, (half, 128))
            dc_ref[h, part * half : (part + 1) * half, :] = delta
            for j in range(half // GROUP):
                tiles[h].append(jnp.transpose(delta[j * GROUP : (j + 1) * GROUP])[0:1])
    dox_ref[rows : rows + EXTRA, :] = pack_extra(tiles, heads, blocks, heads * HEAD)
    dox_ref[rows + EXTRA :, :] = lsex_ref[...]


def out_back(mine, other, wo, okeep, osend, lsex):
    half, width_d = mine.shape
    width = wo.shape[0]
    heads, blocks = width // HEAD, 2 * half // GROUP
    return call(
        functools.partial(out_back_body, heads=heads, blocks=blocks),
        [(sds((2 * half + 2 * EXTRA, width), bf16), VMEM), (sds((heads, 2 * half, 128), f32), VMEM)],
        [VMEM] * 6,
        (mine, other, wo, okeep, osend, lsex),
        "out_back",
        flops=2 * 2 * half * width * width_d,
        nbytes=4e6,
    )


def query_back_body(pos_ref, clip_ref, *refs, pieces, entries, heads, blocks, period):
    qx_ref, dox_ref, lsec_ref, dc_ref = refs[0:4]
    kv_refs = refs[4 : 4 + pieces]
    dq_ref, kv_s, acc_s = refs[4 + pieces :]
    width = heads * HEAD
    sets = period // blocks
    assemble(kv_refs, entries, kv_s, blocks)

    def per_block(i, carry):
        r0 = pl.multiple_of(i * GROUP, GROUP)
        own_clip = clip_of(clip_ref, pos_ref, i, blocks, sets, True)
        acc_s[...] = jnp.zeros(acc_s.shape, f32)

        def per_keys(g, inner):
            @pl.when(own_clip == clip_of(clip_ref, pos_ref, g, blocks, sets, False))
            def _():
                for h in range(heads):
                    cols = slice(h * HEAD, (h + 1) * HEAD)
                    k = kv_s[g, :, cols]
                    v = kv_s[g, :, width + h * HEAD : width + (h + 1) * HEAD]
                    s = dot_t(qx_ref[pl.ds(r0, GROUP), cols], k) * (HEAD ** (-0.5) * LOG2E)
                    p = jnp.exp2(s - lsec_ref[h, pl.ds(r0, GROUP), :][:, 0:1])
                    dp = dot_t(dox_ref[pl.ds(r0, GROUP), cols], v)
                    delta = dc_ref[h, pl.ds(r0, GROUP), :][:, 0:1]
                    ds = (p * (dp - delta) * (HEAD ** (-0.5))).astype(bf16)
                    acc_s[h] = acc_s[h] + dot(ds, k)

            return inner

        lax.fori_loop(0, period, per_keys, 0)
        for h in range(heads):
            dq_ref[pl.ds(r0, GROUP), h * HEAD : (h + 1) * HEAD] = acc_s[h].astype(bf16)
        return carry

    lax.fori_loop(0, blocks, per_block, 0)


def query_back(pos, clips, qx, dox, lsec, dc, kv_pieces, entries):
    rows, width = qx.shape
    heads, blocks, period = width // HEAD, rows // GROUP, clips.shape[0] // GROUPS_FRAME
    pieces = len(kv_pieces)
    return call(
        functools.partial(
            query_back_body, pieces=pieces, entries=entries, heads=heads, blocks=blocks, period=period
        ),
        [(sds((rows, width), bf16), VMEM)],
        [SMEM, SMEM] + [VMEM] * (4 + pieces),
        (pos, clips, qx, dox, lsec, dc, *kv_pieces),
        "query_back",
        scratch=[
            pltpu.VMEM((period, GROUPS_FRAME * GROUP, 2 * width), bf16),
            pltpu.VMEM((heads, GROUP, HEAD), f32),
        ],
        flops=2e9,
        nbytes=7e6,
        trans=2e6,
    )[0]


def key_back_body(
    pos_ref, clip_ref, *refs, q_pieces, do_pieces, q_entries, do_entries, heads, blocks, period
):
    kv_ref, dq_ref, wq_ref, wk_ref, wv_ref = refs[0:5]
    qx_refs = refs[5 : 5 + q_pieces]
    dox_refs = refs[5 + q_pieces : 5 + q_pieces + do_pieces]
    dqkv_ref, keep_ref, send_ref, q_s, do_s, lse_s, delta_s, dk_s, dv_s = refs[5 + q_pieces + do_pieces :]
    width = heads * HEAD
    rows = blocks * GROUP
    sets = period // blocks
    assemble(qx_refs, q_entries, q_s, blocks)
    assemble(dox_refs, do_entries, do_s, blocks)
    for first, target in ((rows, delta_s), (rows + EXTRA, lse_s)):
        for ri, base, p, k in do_entries:
            extra = dox_refs[ri][base + first : base + first + EXTRA, :].astype(f32)
            for h in range(heads):
                for j in range(blocks):
                    line = unpack_extra(extra, h, j, blocks, width)
                    target[p * blocks + j, h, :, pl.ds(place_start(k), GROUP)] = jnp.broadcast_to(
                        line, (8, 128)
                    )
    dqkv_ref[:, 0:width] = dq_ref[...]

    def per_block(j, carry):
        r0 = pl.multiple_of(j * GROUP, GROUP)
        own_clip = clip_of(clip_ref, pos_ref, j, blocks, sets, True)
        dk_s[...] = jnp.zeros(dk_s.shape, f32)
        dv_s[...] = jnp.zeros(dv_s.shape, f32)

        def per_queries(g, inner):
            @pl.when(own_clip == clip_of(clip_ref, pos_ref, g, blocks, sets, False))
            def _():
                for h in range(heads):
                    cols = slice(h * HEAD, (h + 1) * HEAD)
                    k = kv_ref[pl.ds(r0, GROUP), cols]
                    v = kv_ref[pl.ds(r0, GROUP), width + h * HEAD : width + (h + 1) * HEAD]
                    q = q_s[g, :, cols]
                    do = do_s[g, :, cols]
                    st = dot_t(k, q) * (HEAD ** (-0.5) * LOG2E)
                    pt = jnp.exp2(st - lse_s[g, h, 0:1, :])
                    dv_s[h] = dv_s[h] + dot(pt.astype(bf16), do)
                    dpt = dot_t(v, do)
                    dst = (pt * (dpt - delta_s[g, h, 0:1, :]) * (HEAD ** (-0.5))).astype(bf16)
                    dk_s[h] = dk_s[h] + dot(dst, q)

            return inner

        lax.fori_loop(0, period, per_queries, 0)
        for h in range(heads):
            dqkv_ref[pl.ds(r0, GROUP), width + h * HEAD : width + (h + 1) * HEAD] = dk_s[h].astype(bf16)
            dqkv_ref[pl.ds(r0, GROUP), 2 * width + h * HEAD : 2 * width + (h + 1) * HEAD] = dv_s[
                h
            ].astype(bf16)
        return carry

    lax.fori_loop(0, blocks, per_block, 0)
    half = rows // 2
    for part, ref in enumerate((keep_ref, send_ref)):
        r = slice(part * half, (part + 1) * half)
        total = dot_t(dqkv_ref[r, 0:width], wq_ref[...])
        total = total + dot_t(dqkv_ref[r, width : 2 * width], wk_ref[...])
        total = total + dot_t(dqkv_ref[r, 2 * width :], wv_ref[...])
        ref[...] = total.astype(bf16)


def key_back(pos, clips, kv, dq, wq, wk, wv, qx_pieces, q_entries, dox_pieces, do_entries, ties):
    rows, width = dq.shape
    width_d = wq.shape[0]
    heads, blocks, period = width // HEAD, rows // GROUP, clips.shape[0] // GROUPS_FRAME
    tall = GROUPS_FRAME * GROUP
    return call(
        functools.partial(
            key_back_body, q_pieces=len(qx_pieces), do_pieces=len(dox_pieces), q_entries=q_entries,
            do_entries=do_entries, heads=heads, blocks=blocks, period=period,
        ),
        [
            (sds((rows, 3 * width), bf16), VMEM),
            (sds((rows // 2, width_d), bf16), VMEM),
            (sds((rows // 2, width_d), bf16), VMEM),
        ],
        [SMEM, SMEM] + [VMEM] * (5 + len(qx_pieces) + len(dox_pieces)),
        (pos, clips, kv, dq, wq, wk, wv, *qx_pieces, *dox_pieces),
        "key_back",
        ties=ties,
        scratch=[
            pltpu.VMEM((period, tall, width), bf16),
            pltpu.VMEM((period, tall, width), bf16),
            pltpu.VMEM((period, heads, 8, tall), f32),
            pltpu.VMEM((period, heads, 8, tall), f32),
            pltpu.VMEM((heads, GROUP, HEAD), f32),
            pltpu.VMEM((heads, GROUP, HEAD), f32),
        ],
        flops=4e9,
        nbytes=9e6,
        trans=2e6,
    )


def mlp_body(mine_ref, other_ref, win_ref, ag_ref, act_ref, hg_ref, keep_ref, send_ref, *, steps):
    i = pl.program_id(0)
    x = jnp.where(i < steps // 2, mine_ref[...], other_ref[...])
    units = win_ref.shape[1]
    chunk = 512
    total = None
    for n in range(units // chunk):
        cols = slice(n * chunk, (n + 1) * chunk)
        w = win_ref[:, cols]
        hidden = dot(x, w)
        cdf = 0.5 * (1.0 + lax.erf(hidden * 0.7071067811865476))
        act_ref[:, cols] = (hidden * cdf).astype(bf16)
        density = jnp.exp2(hidden * hidden * (-0.5 * LOG2E)) * 0.3989422804014327
        grad = (ag_ref[:, cols] * (cdf + hidden * density)).astype(bf16)
        hg_ref[:, cols] = grad
        term = dot_t(grad, w)
        total = term if total is None else total + term
    total = total.astype(bf16)

    @pl.when(i < steps // 2)
    def _():
        keep_ref[...] = total

    @pl.when(i >= steps // 2)
    def _():
        send_ref[...] = total


def mlp(mine, other, w_in, act_grad):
    half, width_d = mine.shape
    units = w_in.shape[1]
    steps = 2
    rows = 2 * half
    low = lambda i: (jnp.minimum(i, steps // 2 - 1), 0)
    high = lambda i: (jnp.maximum(i - steps // 2, 0), 0)
    return call(
        functools.partial(mlp_body, steps=steps),
        [
            (sds((rows, units), bf16), pl.BlockSpec((half, units), lambda i: (i, 0))),
            (sds((rows, units), bf16), pl.BlockSpec((half, units), lambda i: (i, 0))),
            (sds((half, width_d), bf16), pl.BlockSpec((half, width_d), low)),
            (sds((half, width_d), bf16), pl.BlockSpec((half, width_d), high)),
        ],
        [
            pl.BlockSpec((half, width_d), low),
            pl.BlockSpec((half, width_d), high),
            pl.BlockSpec((width_d, units), lambda i: (0, 0)),
            pl.BlockSpec((half, units), lambda i: (i, 0)),
        ],
        (mine, other, w_in, act_grad),
        "mlp",
        spare=10,
        grid=(steps,),
        flops=4 * rows * width_d * units,
        nbytes=9e6,
        trans=2 * rows * units,
    )


def mlp_down_body(act_ref, w_ref, keep_ref, send_ref, *, steps):
    i = pl.program_id(0)
    total = dot(act_ref[...], w_ref[...]).astype(bf16)

    @pl.when(i < steps // 2)
    def _():
        keep_ref[...] = total

    @pl.when(i >= steps // 2)
    def _():
        send_ref[...] = total


def mlp_down(activated, w_out, ties):
    rows, units = activated.shape
    width_d = w_out.shape[1]
    steps = 2
    blk = rows // steps
    half = sds((blk, width_d), bf16)
    return call(
        functools.partial(mlp_down_body, steps=steps),
        [
            (half, pl.BlockSpec((blk, width_d), lambda i: (jnp.minimum(i, steps // 2 - 1), 0))),
            (half, pl.BlockSpec((blk, width_d), lambda i: (jnp.maximum(i - steps // 2, 0), 0))),
        ],
        [
            pl.BlockSpec((blk, units), lambda i: (i, 0)),
            pl.BlockSpec((units, width_d), lambda i: (0, 0)),
        ],
        (activated, w_out),
        "mlp_down",
        grid=(steps,),
        flops=2 * rows * units * width_d,
        nbytes=4e6,
        ties=ties,
    )


def act_back_body(pos_ref, og_ref, w_ref, rel_ref, ag_ref):
    rel_ref[...] = og_ref[...]
    ag_ref[...] = dot_t(og_ref[...], w_ref[...])


def act_back(pos, out_grad, w_out):
    rows, width_d = out_grad.shape
    units = w_out.shape[0]
    steps = rows // GROUP
    blk = pl.BlockSpec((GROUP, width_d), lambda i, c: (i, 0))
    return call(
        act_back_body,
        [
            (sds((rows, width_d), bf16), blk),
            (sds((rows, units), f32), pl.BlockSpec((GROUP, units), lambda i, c: (i, 0))),
        ],
        [
            pl.BlockSpec((GROUP, width_d), lambda i, c: ((i + c[0] * (steps // 2)) % steps, 0)),
            pl.BlockSpec((units, width_d), lambda i, c: (0, 0)),
        ],
        (pos, out_grad, w_out),
        "act_back",
        grid=(steps,),
        prefetch=1,
        flops=2 * rows * width_d * units,
        nbytes=6e6,
    )


def through_norm(n, v, gain_vec):
    unit, inverse = centre(v)
    t = n * gain_vec
    back = inverse * (
        t - jnp.mean(t, axis=-1, keepdims=True) - unit * jnp.mean(t * unit, axis=-1, keepdims=True)
    )
    return back, unit


def norm_back_body(s_ref, r_ref, v_ref, gain_ref, base_ref, after_ref, branch_ref, gg_ref):
    gain_vec = gain_ref[...]

    def step(r, held):
        n = s_ref[r, :].astype(f32) + r_ref[r, :].astype(f32)
        back, unit = through_norm(n, v_ref[r, :], gain_vec)
        after = base_ref[r, :].astype(f32) + back
        after_ref[r, :] = after
        branch_ref[r, :] = after.astype(bf16)
        return held + folded(n * unit)

    total = by_chunks(s_ref.shape[0], step, jnp.zeros((8, s_ref.shape[1]), f32))
    gg_ref[...] = jnp.sum(total, axis=0, keepdims=True)


def norm_back(s, r, v, gain, base, ties):
    half, width_d = s.shape
    return call(
        norm_back_body,
        [
            (sds((half, width_d), f32), VMEM),
            (sds((half, width_d), bf16), VMEM),
            (sds((1, width_d), f32), VMEM),
        ],
        [VMEM] * 5,
        (s, r, v, gain, base),
        "norm_back",
        ties=ties,
        flops=20 * half * width_d,
        nbytes=5e6,
    )


def final_body(
    pos_ref, s_ref, r_ref, lat_ref, src_ref, gain_one_ref, gain_src_ref, base_ref, half_ref, lat_out, src_out, *, first,
):
    def run(v_ref, gain_ref, base, out_ref):
        gain_vec = gain_ref[...]

        def step(r, held):
            n = s_ref[r, :].astype(f32) + r_ref[r, :].astype(f32)
            back = through_norm(n, v_ref[r, :].astype(f32), gain_vec)[0]
            if base is not None:
                back = base[r, :] + back
            half_ref[r, :] = back.astype(bf16)
            out_ref[r, :] = back.astype(bf16)
            return held

        by_chunks(s_ref.shape[0], step)

    i = pl.program_id(0)
    pl.when(i < first)(lambda: run(lat_ref, gain_one_ref, base_ref, lat_out))
    pl.when(i >= first)(lambda: run(src_ref, gain_src_ref, None, src_out))


def final_norm(pos, s, r, latents, sources, gain_one, gain_src, base, ties):
    width_d = s.shape[1]
    blk = 128
    one, src = latents.shape[0] // 2 // blk, sources.shape[0] // 2 // blk
    at_one = lambda i: jnp.minimum(i, one - 1)
    at_src = lambda i: jnp.maximum(i - one, 0)
    spec = lambda f: pl.BlockSpec((blk, width_d), lambda i, c: (f(i, c), 0))
    gain_spec = pl.BlockSpec((1, width_d), lambda i, c: (0, 0))
    own_one, own_src = spec(lambda i, c: c[0] * one + at_one(i)), spec(lambda i, c: c[0] * src + at_src(i))
    each = spec(lambda i, c: i)
    return call(
        functools.partial(final_body, first=one),
        [(sds(s.shape, bf16), each), (sds(latents.shape, bf16), own_one), (sds(sources.shape, bf16), own_src)],
        [each, each, own_one, own_src, gain_spec, gain_spec, spec(lambda i, c: at_one(i))],
        (pos, s, r, latents, sources, gain_one, gain_src, base),
        "final_norm",
        grid=(one + src,),
        prefetch=1,
        flops=20 * s.size,
        nbytes=8 * s.size,
        ties=ties,
    )


def place_both_body(pos_ref, other_ref, lat_in, src_in, lat_out, src_out):
    i = pl.program_id(0)

    @pl.when(i == 0)
    def _():
        lat_out[...] = other_ref[...]

    @pl.when(i > 0)
    def _():
        src_out[...] = other_ref[...]


def place_both(pos, other, lat_whole, src_whole):
    blk, width_d = lat_whole.shape[0] // 2, other.shape[1]
    steps = other.shape[0] // blk
    spec = lambda f: pl.BlockSpec((blk, width_d), lambda i, c: (f(i, c), 0))
    return call(
        place_both_body,
        [
            (sds(lat_whole.shape, bf16), spec(lambda i, c: 1 - c[0])),
            (sds(src_whole.shape, bf16), spec(lambda i, c: (1 - c[0]) * (steps - 1) + jnp.maximum(i - 1, 0))),
        ],
        [spec(lambda i, c: i), ANY, ANY],
        (pos, other, lat_whole, src_whole),
        "place_both",
        grid=(steps,),
        prefetch=1,
        nbytes=4 * other.size,
        aliases={2: 0, 3: 1},
    )


def place_body(pos_ref, other_ref, whole_ref, out_ref):
    out_ref[...] = other_ref[...]


def place_other(pos, whole, other):
    half, width_d = other.shape
    rows = 256
    steps = half // rows
    return call(
        place_body,
        [(sds(whole.shape, bf16), pl.BlockSpec((rows, width_d), lambda i, c: ((1 - c[0]) * steps + i, 0)))],
        [pl.BlockSpec((rows, width_d), lambda i, c: (i, 0)), ANY],
        (pos, other, whole),
        "place_other",
        grid=(steps,),
        prefetch=1,
        nbytes=4 * half * width_d,
        aliases={2: 0},
    )[0]


def result_body(pos_ref, s_ref, r_ref, after_ref, half_ref, whole_ref, squares_ref):
    def step(r, held):
        result = after_ref[r, :] + (s_ref[r, :].astype(f32) + r_ref[r, :].astype(f32))
        half_ref[r, :] = result.astype(bf16)
        whole_ref[r, :] = result.astype(bf16)
        return held + folded(result * result)

    total = by_chunks(s_ref.shape[0], step, jnp.zeros((8, s_ref.shape[1]), f32))
    squares_ref[pl.ds(pl.program_id(0), 1), :] = jnp.sum(total, axis=0, keepdims=True)


def result_half(pos, s, r, after):
    half, width_d = s.shape
    steps = half // GROUP
    blk = pl.BlockSpec((GROUP, width_d), lambda i, c: (i, 0))
    own = pl.BlockSpec((GROUP, width_d), lambda i, c: (c[0] * steps + i, 0))
    return call(
        result_body,
        [
            (sds((half, width_d), bf16), blk),
            (sds((2 * half, width_d), bf16), own),
            (sds((steps, width_d), f32), pl.BlockSpec((steps, width_d), lambda i, c: (0, 0))),
        ],
        [blk] * 3,
        (pos, s, r, after),
        "result",
        grid=(steps,),
        prefetch=1,
        flops=6 * half * width_d,
        nbytes=5e6,
    )


def gains_body(
    pos_ref, clip_ref, frames_ref, keep, send, lat_ref, src_ref,
    self_ref, mlp_ref, squares_ref, out_ref, *, one_steps, src_steps, blocks, sets, copies, clips,
):
    i = pl.program_id(0)

    @pl.when(i == 0)
    def _():
        width_d = out_ref.shape[1]
        share = jnp.zeros((1, 1), f32)
        for b in range(blocks // 2):
            total = jnp.sum(squares_ref[b : b + 1, :], axis=1, keepdims=True)
            frames = frames_ref[clip_of(clip_ref, pos_ref, b, blocks, sets, True)].astype(f32)
            norm = jnp.sqrt(total / (GROUP * width_d) + 1e-06)
            share = share + norm / (jnp.broadcast_to(frames, (1, 1)) * (GROUPS_FRAME * clips))
        out_ref[0:2, :] = jnp.zeros((2, width_d), f32)
        out_ref[2:3, :] = self_ref[...] * copies
        out_ref[3:4, :] = mlp_ref[...] * copies
        out_ref[4:8, :] = jnp.broadcast_to(share * copies, (4, width_d))

    def add(row, v_ref, keep_ref, send_ref, kept):
        def step(r, held):
            n = jnp.where(kept, keep_ref[r, :].astype(f32), send_ref[r, :].astype(f32))
            return held + folded(n * centre(v_ref[r, :].astype(f32))[0])

        total = by_chunks(v_ref.shape[0], step, jnp.zeros((8, v_ref.shape[1]), f32))
        out_ref[row : row + 1, :] = out_ref[row : row + 1, :] + jnp.sum(total, axis=0, keepdims=True)

    pl.when(i < one_steps)(lambda: add(1, lat_ref, keep, send, i < one_steps // 2))
    pl.when(i >= one_steps)(lambda: add(0, src_ref, keep, send, i - one_steps < src_steps // 2))


def gains(pos, clips, frames, keep, send, latents, sources, self_gain, mlp_gain, squares, copies, ties):
    rows, width_d = latents.shape
    count = sources.shape[0]
    blk = 256
    one_steps, src_steps = rows // blk, count // blk
    one_half, src_half = one_steps // 2, src_steps // 2
    blocks = rows // GROUP
    sets = clips.shape[0] // GROUPS_FRAME // blocks
    clamp = lambda v, top: jnp.minimum(jnp.maximum(v, 0), top)
    spec = lambda f: pl.BlockSpec((blk, width_d), lambda i, *c: (f(i, c[0]), 0))
    fixed = lambda n: pl.BlockSpec((n, width_d), lambda i, *c: (0, 0))
    turn = lambda i, c, steps: (clamp(i, steps - 1) + c[0] * (steps // 2)) % steps
    kept = lambda i, c: jnp.where(
        i < one_steps, clamp(i, one_half - 1), one_half + clamp(i - one_steps, src_half - 1)
    )
    sent = lambda i, c: jnp.where(
        i < one_steps, clamp(i - one_half, one_half - 1), one_half + clamp(i - one_steps - src_half, src_half - 1)
    )
    return call(
        functools.partial(
            gains_body, one_steps=one_steps, src_steps=src_steps, blocks=blocks, sets=sets, copies=copies,
            clips=frames.shape[0],
        ),
        [(sds((8, width_d), f32), fixed(8))],
        [
            spec(kept),
            spec(sent),
            spec(lambda i, c: turn(i, c, one_steps)),
            spec(lambda i, c: turn(i - one_steps, c, src_steps)),
            fixed(1), fixed(1), fixed(blocks // 2),
        ],
        (pos, clips, frames, keep, send, latents, sources, self_gain, mlp_gain, squares),
        "gains",
        grid=(one_steps + src_steps,),
        prefetch=3,
        flops=20 * (rows + count) * width_d,
        nbytes=4 * (rows + count) * width_d,
        ties=ties,
    )[0]


def feature_grads_body(pos_ref, *refs, items, sends, blk):
    given = sum(a + b for a, b in items)
    keep_ref, send_refs = refs[given], refs[given + 1 :]
    at, column = 0, 0
    for lefts, rights in items:
        total, row = None, 0
        for k in range(lefts):
            left = refs[at + k]
            rows = left.shape[0]
            if rights == 1:
                right = refs[at + lefts][row : row + rows, :]
            else:
                right = refs[at + lefts + k][...]
            term = dot_ta(left[...], right)
            total = term if total is None else total + term
            row += rows
        at += lefts + rights
        first, column = column, column + total.shape[1]
        total = total.astype(bf16)
        for j in range(blk // 128):
            part = total[j * 128 : (j + 1) * 128]
            if sends == 0:
                keep_ref[j, :, first:column] = part
                continue
            mine = (pos_ref[1] + j) % 2 == 0

            @pl.when(mine)
            def _():
                keep_ref[j // 2, :, first:column] = part

            @pl.when(jnp.logical_not(mine))
            def _():
                width = send_refs[0].shape[2]
                for h, ref in enumerate(send_refs):
                    low, high = max(first, h * width), min(column, (h + 1) * width)
                    if low < high:
                        ref[j // 2, :, low - h * width : high - h * width] = part[:, low - first : high - first]


def feature_grads(pos, items, sends, ties=()):
    arrays, specs, counts, columns, flops = [], [], [], 0, 0
    features = items[0][0][0].shape[1]
    blk = 512
    for lefts, rights in items:
        counts.append((len(lefts), len(rights)))
        for v in lefts:
            arrays.append(v)
            specs.append(pl.BlockSpec((v.shape[0], blk), lambda i, c: (0, i)))
            flops += 2 * v.shape[0] * v.shape[1] * rights[0].shape[1]
        for v in rights:
            arrays.append(v)
            specs.append(pl.BlockSpec(v.shape, lambda i, c: (0, 0)))
        columns += rights[0].shape[1]
    steps = features // blk
    sets = features // 256 if sends else features // 128
    out = lambda n: (sds((sets, 128, n), bf16), pl.BlockSpec((sets // steps, 128, n), lambda i, c: (i, 0, 0)))
    return call(
        functools.partial(feature_grads_body, items=tuple(counts), sends=sends, blk=blk),
        [out(columns)] + [out(columns // sends)] * sends if sends else [out(columns)],
        specs,
        (pos, *arrays),
        "feature_grads",
        grid=(steps,),
        prefetch=1,
        flops=flops,
        nbytes=2 * features * columns + sum(2 * v.size for v in arrays),
        ties=ties,
    )


def stage_one_body(pos_ref, keep_ref, *refs):
    z = pos_ref[1] // 2
    gots, (own_ref, send_ref) = refs[:-2], refs[-2:]
    width = gots[0].shape[2]
    for h, got_ref in enumerate(gots):
        cols = slice(h * width, (h + 1) * width)
        for k in range(2):
            at = z ^ (2 * k)
            own_ref[k, :, cols] = keep_ref[at, :, cols].astype(f32) + got_ref[at].astype(f32)
            at = z ^ 1 ^ (2 * k)
            send_ref[k, :, cols] = (keep_ref[at, :, cols].astype(f32) + got_ref[at].astype(f32)).astype(bf16)


def stage_one(pos, keep, gots, ties=()):
    shape = (2, *keep.shape[1:])
    return call(
        stage_one_body,
        [(sds(shape, f32), VMEM), (sds(shape, bf16), VMEM)],
        [SMEM] + [VMEM] * (1 + len(gots)),
        (pos, keep, *gots),
        "stage_one",
        nbytes=4 * keep.size,
        ties=ties,
    )


def stage_two_body(keep_ref, got_ref, own_ref, send_ref):
    own_ref[...] = keep_ref[0] + got_ref[0].astype(f32)
    send_ref[...] = (keep_ref[1] + got_ref[1].astype(f32)).astype(bf16)


def stage_two(keep, got, ties=()):
    shape = keep.shape[1:]
    return call(
        stage_two_body,
        [(sds(shape, f32), VMEM), (sds(shape, bf16), VMEM)],
        [VMEM] * 2,
        (keep, got),
        "stage_two",
        nbytes=4 * keep.size,
        ties=ties,
    )


def stage_end_body(own_ref, got_ref, *outs, turned):
    total = own_ref[...] + got_ref[...].astype(f32)
    width = total.shape[1] // len(outs)
    for k, ref in enumerate(outs):
        part = total[:, k * width : (k + 1) * width]
        ref[...] = part.T if k in turned else part


def stage_end(own, got, parts, turned, ties=()):
    blk = own.shape
    width = blk[1] // parts
    return call(
        functools.partial(stage_end_body, turned=turned),
        [(sds((width, blk[0]) if k in turned else (blk[0], width), f32), VMEM) for k in range(parts)],
        [VMEM] * 2,
        (own, got),
        "stage_end",
        nbytes=10 * blk[0] * blk[1],
        ties=ties,
    )


def flip_x(v):
    return lax.ppermute(v, "seq", xor_pairs(1, 8))


def near_z(v):
    return lax.ppermute(v, "seq", xor_pairs(2, 8))


def far_z(v):
    return lax.ppermute(v, "seq", xor_pairs(4, 8))


def scatter_whole(pos, items, parts, turned, ties):
    whole = feature_grads(pos, items, 0, ties)[0]
    whole = whole.reshape(-1, whole.shape[2])
    total = lax.psum_scatter(whole, "seq", scatter_dimension=0, tiled=True).astype(f32)
    width = total.shape[1] // parts
    pieces = [total[:, k * width : (k + 1) * width] for k in range(parts)]
    return [piece.T if k in turned else piece for k, piece in enumerate(pieces)]


def tied(values, other):
    out = lax.optimization_barrier((other, *values))
    return list(out[1:]), out[0]


def cross_back_body(
    pos_ref, mine_ref, other_ref, wo_ref, q_ref, kvp_ref, idx_ref, wq_ref, wk_ref, wv_ref,
    dq_ref, dk_ref, dv_ref, keep_ref, send_ref, dkvp_s, grad_s, *, blocks,
):
    width = wq_ref.shape[1]
    heads = width // HEAD
    count = kvp_ref.shape[0]
    scale = HEAD ** (-0.5)
    rows = blocks * GROUP
    for part, ref in enumerate((mine_ref, other_ref)):
        grad_s[part * rows // 2 : (part + 1) * rows // 2, :] = dot_t(ref[...], wo_ref[...]).astype(bf16)
    for b in range(blocks):
        for h in range(heads):
            cols = slice(h * HEAD, (h + 1) * HEAD)
            vcols = slice(width + h * HEAD, width + (h + 1) * HEAD)
            q = q_ref[b * GROUP : (b + 1) * GROUP, cols]
            k = kvp_ref[b * SRC : (b + 1) * SRC, cols]
            v = kvp_ref[b * SRC : (b + 1) * SRC, vcols]
            do = grad_s[b * GROUP : (b + 1) * GROUP, cols]
            s = dot_t(q, k) * (scale * LOG2E)
            p = jnp.exp2(s - jnp.max(s, axis=-1, keepdims=True))
            p = p / jnp.sum(p, axis=-1, keepdims=True)
            dp = dot_t(do, v)
            delta = jnp.sum(p * dp, axis=-1, keepdims=True)
            ds = (p * (dp - delta) * scale).astype(bf16)
            dq_ref[b * GROUP : (b + 1) * GROUP, cols] = dot(ds, k).astype(bf16)
            dkvp_s[b * SRC : (b + 1) * SRC, cols] = dot_ta(ds, q).astype(bf16)
            dkvp_s[b * SRC : (b + 1) * SRC, vcols] = dot_ta(p.astype(bf16), do).astype(bf16)
    one = dot_t(dq_ref[...], wq_ref[...]).astype(bf16)
    keep_ref[0 : rows // 2, :] = one[0 : rows // 2]
    send_ref[0 : rows // 2, :] = one[rows // 2 :]
    half = count // 2
    row = jnp.concatenate([index_row(idx_ref, pos_ref, b, blocks, count) for b in range(blocks)], axis=1)
    for part, ref in enumerate((keep_ref, send_ref)):
        r0 = pl.multiple_of((pos_ref[0] if part == 0 else 1 - pos_ref[0]) * half, half)
        wanted = lax.broadcasted_iota(jnp.int32, (half, count), 0).astype(f32) + r0.astype(f32)
        picks = jnp.where(row == wanted, 1.0, 0.0).astype(bf16)
        dkv = dot(picks, dkvp_s[...]).astype(bf16)
        dk_ref[pl.ds(r0, half), :] = dkv[:, 0:width]
        dv_ref[pl.ds(r0, half), :] = dkv[:, width:]
        total = dot_t(dkv[:, 0:width], wk_ref[...]) + dot_t(dkv[:, width:], wv_ref[...])
        ref[rows // 2 :, :] = total.astype(bf16)


def cross_back(pos, mine, other, wo, q, kvp, idx, wq, wk, wv, ties):
    rows, width = q.shape
    width_d = wq.shape[0]
    count = kvp.shape[0]
    blocks = rows // GROUP
    return call(
        functools.partial(cross_back_body, blocks=blocks),
        [
            (sds((rows, width), bf16), VMEM),
            (sds((count, width), bf16), VMEM),
            (sds((count, width), bf16), VMEM),
            (sds(((rows + count) // 2, width_d), bf16), VMEM),
            (sds(((rows + count) // 2, width_d), bf16), VMEM),
        ],
        [SMEM] + [VMEM] * 9,
        (pos, mine, other, wo, q, kvp, idx, wq, wk, wv),
        "cross_back",
        ties=ties,
        scratch=[pltpu.VMEM((count, 2 * width), bf16), pltpu.VMEM((rows, width), bf16)],
        spare=14,
        flops=4e9,
        nbytes=12e6,
    )


def xor_pairs(bit, size):
    return [(i, i ^ bit) for i in range(size)]


def ring_pairs(d):
    return [(s, ((s // 2 + d) % 4) * 2 + s % 2) for s in range(8)]


def tensor_swap(x, bit):
    return lax.ppermute(x, "tensor", xor_pairs(bit, lax.axis_size("tensor")))


def seq_gather(x, between=None, guest=None):
    size = lax.axis_size("seq")
    if size == 8:
        move = lambda v, pairs: lax.ppermute(v, "seq", pairs)
        flip = xor_pairs(1, 8)
        beside = move(x, flip)
        up = move(x, ring_pairs(1))
        down = move(x, ring_pairs(-1))
        if guest is not None:
            (beside, up, guest), between = tied([beside, up, guest], between)
            guest = flip_x(guest)
        far = move(up, ring_pairs(1))
        down_beside = move(beside, ring_pairs(-1))
        if guest is not None:
            up_beside = move(beside, ring_pairs(1))
            (far_sent, up_beside), down_beside = tied([far, up_beside], down_beside)
        else:
            up_beside = move(up, flip)
            far_sent = far
        far_beside = move(far_sent, flip)
        pieces = [x, beside, up, down, far, up_beside, down_beside, far_beside]
    else:
        pieces = gather_whole(x)
    return pieces if guest is None else (pieces, between, guest)


def gather_whole(x):
    return [lax.all_gather(x, "seq", axis=0, tiled=True)]


def gather_entries(size, rows, sets):
    if size == 8:
        return tuple((k, 0, 0, k) for k in range(8))
    return whole_entries(size, rows, sets)


def whole_entries(size, rows, sets):
    return tuple((0, s * rows, s % sets, s // sets) for s in range(size))


def half_sum(keep, send):
    size = lax.axis_size("tensor")
    got = tensor_swap(send, 1)
    own = (keep.astype(f32) + got.astype(f32)).astype(bf16)
    bit = 2
    while True:
        other = tensor_swap(own, bit)
        if bit * 2 >= size:
            return own, other
        own = (own.astype(f32) + other.astype(f32)).astype(bf16)
        bit *= 2


def tensor_pieces(keep, send):
    size = lax.axis_size("tensor")
    return [keep if k == 0 else tensor_swap(send if k % 2 else keep, k) for k in range(size)]


def weight_far(weight):
    pieces = {0: weight}
    bit = lax.axis_size("tensor") // 2
    while bit >= 2:
        pieces.update({k + bit: tensor_swap(v, bit) for k, v in list(pieces.items())})
        bit //= 2
    return pieces


def weight_pieces(pieces):
    pieces = dict(pieces)
    pieces.update({k + 1: tensor_swap(v, 1) for k, v in list(pieces.items())})
    return [pieces[k] for k in range(len(pieces))]


def tie_all(pieces, other):
    keys = sorted(pieces)
    tied = lax.optimization_barrier((other, *[pieces[k] for k in keys]))
    return dict(zip(keys, tied[1:])), tied[0]


def sum_over(v, axis, only):
    size = lax.axis_size(axis)
    bit = only or 1
    while bit < size:
        v = v + lax.ppermute(v, axis, xor_pairs(bit, size))
        bit = size if only else bit * 2
    return v


def local(
    latents, sources, source_index, block_clip, clip_frames, norm_src, norm_cross, norm_self, norm_mlp,
    cross_q, cross_k, cross_v, cross_o, self_q, self_k, self_v, self_o, mlp_in, mlp_out, out_grad,
):
    rows, width_d = latents.shape
    blocks = rows // GROUP
    width = cross_q.shape[1]
    units = mlp_in.shape[1]
    tensor_size, seq_size = lax.axis_size("tensor"), lax.axis_size("seq")
    core = lax.axis_index("tensor") % 2
    pos = jnp.stack((core, lax.axis_index("seq"), lax.axis_index("tensor"))).astype(jnp.int32)
    sets = block_clip.shape[0] // GROUPS_FRAME // blocks
    gain = lambda g: g.reshape(1, width_d)
    kv_entries = gather_entries(seq_size, rows, sets)
    out_entries = gather_entries(seq_size, rows + 2 * EXTRA, sets)

    cross_o_far = weight_far(cross_o)
    normed_one, normed_src, cross_query, cross_kv, mixed_keep, mixed_send = cross_forward(
        pos, source_index, latents, sources, gain(norm_cross), gain(norm_src), cross_q, cross_k, cross_v
    )
    cross_o_far, mixed_keep = tie_all(cross_o_far, mixed_keep)
    after_cross, two_mine = project(
        pos, tensor_pieces(mixed_keep, mixed_send), weight_pieces(cross_o_far), latents, gain(norm_self), True
    )
    two_other = tensor_swap(two_mine, 1)
    query, key_value = qkv(two_mine, two_other, self_q, self_k, self_v)
    kv_pieces = seq_gather(key_value)
    self_o_tied, two_mine = tie_all({0: self_o}, two_mine)
    self_o_all = weight_pieces(weight_far(self_o_tied[0]))
    out_rel, act_grad = act_back(pos, out_grad, mlp_out)
    split = seq_size == 8
    query_pieces = seq_gather(query)
    self_keep, self_send, lse_rows, lse_columns = attend(
        pos, block_clip, query, kv_pieces, kv_entries, (act_grad, *self_o_all[1:])
    )
    after_self, three_mine = project(
        pos, tensor_pieces(self_keep, self_send), self_o_all, after_cross, gain(norm_mlp), False,
        query_pieces[1:4],
    )
    three_other = tensor_swap(three_mine, 1)
    activated, hidden_grad, three_keep, three_send = mlp(three_mine, three_other, mlp_in, act_grad)

    three_sum, three_got = half_sum(three_keep, three_send)
    in_items = (((three_mine, three_other), (hidden_grad,)),)
    out_items = (((out_rel,), (activated,)),)
    early = ()
    if split:
        in_keep, in_send = feature_grads(pos, in_items, 1, (three_sum,))
        out_keep, out_send_a, out_send_b = feature_grads(pos, out_items, 2, (in_keep,))
        early = (out_keep, *query_pieces[4:])
    down_keep, down_send = mlp_down(activated, mlp_out, (three_sum, *early[0:1]))
    early = (*early, down_keep)
    after_self_grad, self_branch, mlp_gain = norm_back(
        three_sum, three_got, after_self, gain(norm_mlp), out_rel, early
    )
    self_branch_other = tensor_swap(self_branch, 1)

    out_more, delta_columns = out_back(self_branch, self_branch_other, self_o, self_keep, self_send, lse_rows)
    self_query_grad = query_back(
        pos, block_clip, query, out_more, lse_columns, delta_columns, kv_pieces, kv_entries
    )
    if split:
        out_pieces, self_query_grad, in_got = seq_gather(out_more, self_query_grad, in_send)
    else:
        out_pieces = seq_gather(out_more)
    result_sum, result_got = half_sum(down_keep, down_send)
    output_half, output_whole, squares = result_half(pos, result_sum, result_got, after_self)
    output = place_other(pos, output_whole, tensor_swap(output_half, 1))
    early = ()
    if split:
        in_keep, in_send = stage_one(pos, in_keep, [in_got])
        (out_send_a, in_send), out_pieces[-1] = tied([out_send_a, in_send], out_pieces[-1])
        out_got_a = flip_x(out_send_a)
        early = (squares,)
    self_grads, two_keep, two_send = key_back(
        pos, block_clip, key_value, self_query_grad, self_q, self_k, self_v,
        query_pieces, kv_entries, out_pieces, out_entries, early,
    )
    if split:
        (two_send, out_send_b), out_got_a = tied([two_send, out_send_b], out_got_a)
        out_got_b = flip_x(out_send_b)
        in_got = near_z(in_send)
    two_sum, two_got = half_sum(two_keep, two_send)
    self_items = (
        ((two_mine, two_other), (self_grads,)),
        ((self_branch, self_branch_other), (self_keep, self_send)),
    )
    early = ()
    if split:
        self_wkeep, self_send_a, self_send_b = feature_grads(pos, self_items, 2, (two_sum,))
        in_own, in_send = stage_two(in_keep, in_got, (self_wkeep,))
        out_keep, out_send = stage_one(pos, out_keep, [out_got_a, out_got_b], (in_send,))
        early = (self_wkeep, in_own, out_keep, output)
    after_cross_grad, cross_branch, self_gain = norm_back(
        two_sum, two_got, after_cross, gain(norm_self), after_self_grad, early
    )
    cross_branch_other = tensor_swap(cross_branch, 1)

    if split:
        (self_send_a, in_send), cross_branch_other = tied([self_send_a, in_send], cross_branch_other)
        self_got_a = flip_x(self_send_a)
        in_got = far_z(in_send)
    cross_query_grad, cross_key_grad, cross_value_grad, both_keep, both_send = cross_back(
        pos, cross_branch, cross_branch_other, cross_o, cross_query, cross_kv, source_index,
        cross_q, cross_k, cross_v, (),
    )
    cross_items = (
        ((normed_one,), (cross_query_grad,)),
        ((normed_src,), (cross_key_grad,)),
        ((normed_src,), (cross_value_grad,)),
        ((cross_branch, cross_branch_other), (mixed_keep, mixed_send)),
    )
    gains_of = lambda ties: gains(
        pos, block_clip, clip_frames, both_keep, both_send, latents, sources,
        self_gain, mlp_gain, squares, 2.0 / tensor_size, ties,
    )
    final_of = lambda ties: final_norm(
        pos, both_sum, both_got, latents, sources, gain(norm_cross), gain(norm_src), after_cross_grad, ties
    )
    if split:
        both_send, self_send_b, out_send, self_got_a, in_got = lax.optimization_barrier(
            (both_send, self_send_b, out_send, self_got_a, in_got)
        )
        self_got_b = flip_x(self_send_b)
        out_got = near_z(out_send)
        both_sum, both_got = half_sum(both_keep, both_send)
        cross_wkeep, cross_wsend = feature_grads(pos, cross_items, 1, (both_sum,))
        out_own, out_send = stage_two(out_keep, out_got, (cross_wkeep,))
        self_wkeep, self_wsend = stage_one(pos, self_wkeep, [self_got_a, self_got_b], (out_own,))

        cross_wsend, out_send, self_wsend = lax.optimization_barrier((cross_wsend, out_send, self_wsend))
        cross_wgot = flip_x(cross_wsend)
        out_got = far_z(out_send)
        self_wgot = near_z(self_wsend)
        mlp_outs = stage_end(in_own, in_got, 1, (), (self_wsend,))
        small = gains_of((cross_wsend, mlp_outs[0]))
        small = sum_over(sum_over(small, "tensor", 1), "seq", 1)
        self_own, self_wsend = stage_two(self_wkeep, self_wgot, (out_got, small))
        self_wgot = far_z(self_wsend)
        cross_wkeep, cross_wsend = stage_one(pos, cross_wkeep, [cross_wgot], (self_wsend,))

        cross_wsend, small = lax.optimization_barrier((cross_wsend, small))
        cross_wgot = near_z(cross_wsend)
        both_half, lat_whole, src_whole = final_of(())
        mlp_outs = [*mlp_outs, stage_end(out_own, out_got, 1, (0,), (both_half,))[0]]
        small, both_half = lax.optimization_barrier((small, both_half))
        near, far, both = [lax.ppermute(small, "seq", xor_pairs(bit, 8)) for bit in (2, 4, 6)]
        small = (small + near) + (far + both)
        cross_own, cross_wsend = stage_two(cross_wkeep, cross_wgot, (self_wgot, small))

        cross_wsend, small, both_half = lax.optimization_barrier((cross_wsend, small, both_half))
        cross_wgot = far_z(cross_wsend)
        bit = 2
        while bit < tensor_size:
            small = sum_over(small, "tensor", bit)
            bit *= 2
        self_outs = stage_end(self_own, self_wgot, 4, (3,))
        latents_grad, sources_grad = place_both(pos, tensor_swap(both_half, 1), lat_whole, src_whole)
        cross_outs = stage_end(cross_own, cross_wgot, 4, (3,), (latents_grad, self_outs[0], mlp_outs[1]))
    else:
        both_sum, both_got = half_sum(both_keep, both_send)
        small = gains_of((both_sum,))
        small = sum_over(small, "tensor", 0)
        small = sum_over(small, "seq", 0)
        both_half, lat_whole, src_whole = final_of(())
        latents_grad, sources_grad = place_both(pos, tensor_swap(both_half, 1), lat_whole, src_whole)
        cross_outs = scatter_whole(pos, cross_items, 4, (3,), ())
        self_outs = scatter_whole(pos, self_items, 4, (3,), ())
        mlp_outs = scatter_whole(pos, in_items, 1, (), ()) + scatter_whole(pos, out_items, 1, (0,), ())
    return (
        output, latents_grad, sources_grad, small[0], small[1], small[2], small[3],
        *cross_outs, *self_outs, *mlp_outs, small[4, 0],
    )


def solution(mesh):
    in_specs = (
        P("seq", None), P("seq", None), P("seq", None), P(), P(), P(), P(), P(), P(),
        P(None, "tensor"), P(None, "tensor"), P(None, "tensor"), P("tensor", None),
        P(None, "tensor"), P(None, "tensor"), P(None, "tensor"), P("tensor", None),
        P(None, "tensor"), P("tensor", None), P("seq", None),
    )
    out_specs = (
        P("seq", None), P("seq", None), P("seq", None), P(), P(), P(), P(),
        P("seq", "tensor"), P("seq", "tensor"), P("seq", "tensor"), P("tensor", "seq"),
        P("seq", "tensor"), P("seq", "tensor"), P("seq", "tensor"), P("tensor", "seq"),
        P("seq", "tensor"), P("tensor", "seq"), P(),
    )
    return jax.shard_map(local, mesh=mesh, in_specs=in_specs, out_specs=out_specs, check_vma=False)
```
